32 devices in a mesh: tm: 4 (over z), space: 8 (over y, x, core).
Axes of the slice: x: 2, y: 2, z: 4, core: 2. Of those that a mesh axis runs over, the one named last changes fastest.
Arguments:
- wind: float32 [2, 4, 64, 512], P(None, 'tm', 'space'), may hold values from -0.3 to 0.3
- decay: float32 [4, 3, 64, 512], P('tm', None, 'space'), may hold values from 0.5 to 0.98
- inverse_error_variance: float32 [4, 3, 64, 512], P('tm', None, 'space'), may hold values from 0.5 to 2
- obs_index: int32 [4, 32768], P('tm', 'space'), may hold values from 0 to 12287
- obs_weight: float32 [4, 32768], P('tm', 'space'), may hold values from 0.5 to 4
- innovations: float32 [4, 32768], P('tm', 'space'), may hold values from -6 to 6
Outputs:
- increment: float32 [4, 3, 64, 512], P('tm', None, 'space')
- residual: float32 [4, 3, 64, 512], P('tm', None, 'space')
The draws below stay inside these ranges and needn't reach their ends.
Inputs may be any that keep to these rules, and one draw needn't show every extreme that they name: `obs_index`: each observation names a flattened (field, row, column) cell of the tile of the same subwindow and tile that holds the observation; several observations may name one cell.
All inputs are finite; a program needn't handle non-finite values.
Results may differ from the reference program's by a relative error of at most 0.0001.
Values sent between devices are 32-bit elements; how exact they have to be, the bound alone decides.
A program may use at most 64 MiB of HBM per device.

```python
import math
import jax
import jax.numpy as jnp

CX = 8
NY = 512
OBS_DEV = 4096
STEPS = 4
ITERS = 2
SUBW = 4
NX = 64
OBS = 32768
N_SPACE = 8


def place_ends(array, own_key, least, high):
    place = [jax.random.randint(jax.random.fold_in(own_key, axis), (), 0, length) for axis, length in enumerate(array.shape)]
    longest = array.shape.index(max(array.shape))
    neighbour = place[:longest] + [(place[longest] + 1) % array.shape[longest]] + place[longest + 1:]
    return array.at[tuple(place)].set(least).at[tuple(neighbour)].set(high)


def block_levels(stream_key, shape, cuts, smallest, high):
    level = 1.0
    for position, shards_of in cuts:
        steps = jax.random.uniform(jax.random.fold_in(jax.random.fold_in(stream_key, 6), position), (shards_of,), jnp.float32, smallest / len(cuts), high / len(cuts))
        level = level * jnp.repeat(jnp.exp(steps), shape[position] // shards_of).reshape((-1,) + (1,) * (len(shape) - 1 - position))
    return level


def centred(key, extent, deviation, bound, cuts=(), kind=jnp.bfloat16):
    level = block_levels(key, extent, cuts, -0.22, 0.18) if cuts else 1.0
    values = jax.random.normal(key, extent, jnp.float32) * deviation * level
    return jnp.minimum(jnp.maximum(values, -bound), bound).astype(kind)


def setup_inputs(seed: int = 0) -> dict:
    keys = jax.random.split(jax.random.key(seed), 7)
    return {
        "wind": jnp.clip(jax.random.uniform(keys[0], (2, SUBW, NX, NY), jnp.float32, -0.3, 0.3) * block_levels(keys[0], (2, SUBW, NX, NY), ((1, 4), (2, 8)), -0.4, 0.0), -0.3, 0.3),
        "decay": jnp.clip(0.5 + 0.48000002 * jax.random.uniform(keys[1], (SUBW, 3, NX, NY), jnp.float32) ** block_levels(keys[1], (SUBW, 3, NX, NY), ((0, 4), (2, 8)), -0.2, 0.2), 0.5, 0.98),
        "inverse_error_variance": jnp.clip(jnp.exp(math.log(2.0) - 1.3862944 * jax.random.uniform(keys[2], (SUBW, 3, NX, NY), jnp.float32) ** block_levels(keys[2], (SUBW, 3, NX, NY), ((0, 4), (2, 8)), -0.2, 0.2)), 0.5, 2.0),
        "obs_index": place_ends(jax.random.randint(keys[3], (SUBW, OBS), 0, 3 * CX * NY), jax.random.fold_in(keys[3], 1), 0, (3 * CX * NY) - 1).astype(jnp.int32),
        "obs_weight": jnp.clip(jnp.exp(math.log(4.0) - 2.0794415 * jax.random.uniform(keys[4], (SUBW, OBS), jnp.float32) ** block_levels(keys[4], (SUBW, OBS), ((0, 4), (1, 8)), -0.2, 0.2)), 0.5, 4.0),
        "innovations": centred(keys[5], (SUBW, OBS), 1.0, 6.0, ((0, 4), (1, 8)), jnp.float32),
    }


diffusion = 0.15


def along_rows(u):
    zero_row = jnp.zeros_like(u[:, :, :1])
    upper = jnp.concatenate([u[:, :, 1:], zero_row], axis=2)
    lower = jnp.concatenate([zero_row, u[:, :, :-1]], axis=2)
    return upper, lower


def along_cols(u):
    zero_col = jnp.zeros_like(u[..., :1])
    right = jnp.concatenate([u[..., 1:], zero_col], axis=3)
    left = jnp.concatenate([zero_col, u[..., :-1]], axis=3)
    return right, left


def perturbation_propagator(u, eastward_velocity, northward_velocity):
    upper, lower = along_rows(u)
    right, left = along_cols(u)
    laplace = upper + lower + right + left - 4.0 * u
    return u + diffusion * laplace - 0.5 * eastward_velocity * (upper - lower) - 0.5 * northward_velocity * (right - left)


def adjoint_step(v, eastward_velocity, northward_velocity):
    upper, lower = along_rows(v)
    right, left = along_cols(v)
    laplace = upper + lower + right + left - 4.0 * v
    upper_w, lower_w = along_rows(eastward_velocity * v)
    right_z, left_solution = along_cols(northward_velocity * v)
    return v + diffusion * laplace + 0.5 * (upper_w - lower_w) + 0.5 * (right_z - left_solution)


def tiles(field):
    return field.reshape(SUBW, 3, N_SPACE, CX, NY).transpose(0, 2, 1, 3, 4).reshape(SUBW, N_SPACE, 3 * CX * NY)


def untile(tiled):
    return tiled.reshape(SUBW, N_SPACE, 3, CX, NY).transpose(0, 2, 1, 3, 4).reshape(SUBW, 3, NX, NY)


def scatter_obs(values, index):
    def one(vals, idx):
        return jax.ops.segment_sum(vals, idx, num_segments=3 * CX * NY)
    return untile(jax.vmap(jax.vmap(one))(values, index))


def precondition(r, decay):
    v_rows = [None] * SUBW
    v_rows[SUBW - 1] = r[SUBW - 1]
    for k in range(SUBW - 2, -1, -1):
        v_rows[k] = r[k] + decay[k] * v_rows[k + 1]
    u_rows = [v_rows[0]]
    for k in range(1, SUBW):
        u_rows.append(v_rows[k] + decay[k - 1] * u_rows[k - 1])
    return jnp.stack(u_rows)


def reference(wind, decay, inverse_error_variance, obs_index, obs_weight, innovations):
    eastward_velocity = wind[0][:, None]
    northward_velocity = wind[1][:, None]
    index = obs_index.reshape(SUBW, N_SPACE, OBS_DEV)
    weight = obs_weight.reshape(SUBW, N_SPACE, OBS_DEV)
    departures = innovations.reshape(SUBW, N_SPACE, OBS_DEV)

    def hessian(conjugate_update_vector):
        predicted_state_grid = conjugate_update_vector
        for step in range(STEPS):
            predicted_state_grid = perturbation_propagator(predicted_state_grid, eastward_velocity, northward_velocity)
        displaced_grid_values = jnp.concatenate([jnp.zeros_like(predicted_state_grid[:1]), predicted_state_grid[:-1]], axis=0)
        mismatch = inverse_error_variance * (conjugate_update_vector - displaced_grid_values)
        back = jnp.concatenate([mismatch[1:], jnp.zeros_like(mismatch[:1])], axis=0)
        for step in range(STEPS):
            back = adjoint_step(back, eastward_velocity, northward_velocity)
        picked = jnp.take_along_axis(tiles(conjugate_update_vector), index, axis=2)
        return mismatch - back + scatter_obs(weight * picked, index)

    increment = jnp.zeros((SUBW, 3, NX, NY), jnp.float32)
    residual = scatter_obs(weight * departures, index)
    precond = precondition(residual, decay)
    direction = precond
    rz_now = jnp.sum(residual * precond)
    for it in range(ITERS):
        image = hessian(direction)
        alpha = rz_now / jnp.sum(direction * image)
        increment = increment + alpha * direction
        residual = residual - alpha * image
        if it + 1 < ITERS:
            precond = precondition(residual, decay)
            upcoming_residual_dot = jnp.sum(residual * precond)
            direction = precond + (upcoming_residual_dot / rz_now) * direction
            rz_now = upcoming_residual_dot
    return increment, residual
```

```python
import functools

import jax
import jax.numpy as jnp
from jax import lax
from jax.experimental import pallas as pl
from jax.experimental.pallas import tpu as pltpu
from jax.sharding import PartitionSpec as P

STEPS = 4
DIFFUSION = 0.15
MESH = pl.DeviceIdType.MESH
CHUNK = 1024
DIRECT = 64
DEC, RES, WIND, IEV, DIAG = range(5)
Z, Q, Y, W = range(4)


def split3(x):
    high = x.astype(jnp.bfloat16)
    rest = x - high.astype(jnp.float32)
    mid = rest.astype(jnp.bfloat16)
    low = (rest - mid.astype(jnp.float32)).astype(jnp.bfloat16)
    return high, mid, low


def folded(x):
    total = x[:, :128]
    for at in range(128, x.shape[1], 128):
        total = total + x[:, at : at + 128]
    return total


def packed(*terms):
    lane = lax.broadcasted_iota(jnp.int32, (1, 128), 1)
    out = jnp.zeros((1, 128), jnp.float32)
    for at, term in enumerate(terms):
        out = jnp.where(lane == at, jnp.sum(term, axis=(0, 1), keepdims=True), out)
    return out


def kernel(
    n_tm, n_sp, wind_in, decay_in, iev_in, obs_in, weight_in, innov_in, out,
    wind, decay, iev, obs, weight, innov, load_sem,
    r_own, g_own, dec_f, r_f, g_f, iev_f, wind_f, coef, z_f, y_f, jump_f, q_f, w_f, ret,
    sum_any, sum_tm, sum_sp, tm_send, tm_recv, st_send, st_recv, ret_send, ret_recv,
    any_send, any_recv, sp_send, sp_recv,
):
    k = lax.axis_index("tm")
    s = lax.axis_index("space")
    fields, rows, width = decay_in.shape[1:]
    n_own = fields * n_sp
    n_all = n_tm * n_sp
    owner = k < fields
    has_next, has_high, has_low = k < n_tm - 1, s < n_sp - 1, s > 0
    me = k * n_sp + s
    direct = n_all <= DIRECT
    mid = pl.ds(rows, rows)
    pending = []

    def at_tm(o):
        return lax.rem(k + o + n_tm, n_tm)

    def at_sp(o):
        return lax.rem(s + o + n_sp, n_sp)

    def place(at):
        return (at // n_sp, lax.rem(at, n_sp))

    def all_of(*conds):
        return functools.reduce(jnp.logical_and, conds)

    loads = [
        pltpu.make_async_copy(src, dst, load_sem.at[at])
        for at, (src, dst) in enumerate((
            (obs_in, obs), (innov_in, innov), (weight_in, weight),
            (decay_in, decay), (wind_in, wind), (iev_in, iev),
        ))
    ]
    for load in loads:
        load.start()
    barrier = pltpu.get_barrier_semaphore()

    def hello(device):
        pl.semaphore_signal(barrier, inc=1, device_id=device, device_id_type=MESH)

    if direct:
        @pl.when(owner)
        def _():
            for o in range(1, n_all):
                hello(place(lax.rem(me + o, n_all)))
    else:
        for o in range(1, n_tm):
            hello((at_tm(o), s))
        for o in range(1, n_sp):
            hello((k, at_sp(o)))

    def remote(src, dst, send, recv, device):
        return pltpu.make_async_remote_copy(
            src_ref=src, dst_ref=dst, send_sem=send, recv_sem=recv,
            device_id=device, device_id_type=MESH,
        )

    def start(copy, *conds):
        cond = all_of(*conds) if conds else None
        pending.append((copy, cond))
        if cond is None:
            copy.start()
        else:
            pl.when(cond)(copy.start)

    tiles_of = (
        (dec_f, lambda at: dec_f.at[at]),
        (r_f, lambda at: r_f.at[at]),
        (wind_f, lambda at: wind_f.at[at, :, mid]),
        (iev_f, lambda at: iev_f.at[at, mid]),
        (g_f, lambda at: g_f.at[at]),
    )
    sources = (
        lambda j: decay.at[0, j], lambda j: r_own.at[j], lambda j: wind.at[:, 0],
        lambda j: iev.at[0, j], lambda j: g_own.at[j],
    )
    last_has = (False, True, False, True, True)

    def give(kind):
        for j in range(fields):
            conds = (k != j,) if last_has[kind] else (k != j, has_next)
            start(remote(
                sources[kind](j), tiles_of[kind][1](k), tm_send.at[kind, j], tm_recv.at[kind, k], (j, s),
            ), *conds)

    def take(kind, at):
        dst = tiles_of[kind][1](at)
        pl.when(k != at)(remote(dst, dst, tm_send.at[kind, 0], tm_recv.at[kind, at], (at, s)).wait_recv)

    def sides(kind, at, pick):
        return (
            remote(pick(mid), pick(pl.ds(0, rows)), st_send.at[kind, at, 0], st_recv.at[kind, at, 0], (k, at_sp(1))),
            remote(pick(mid), pick(pl.ds(2 * rows, rows)), st_send.at[kind, at, 1], st_recv.at[kind, at, 1], (k, at_sp(-1))),
        )

    def to_sides(kind, at, pick):
        up, down = sides(kind, at, pick)
        start(up, has_high)
        start(down, has_low)

    def from_sides(kind, at, pick):
        up, down = sides(kind, at, pick)
        pl.when(has_low)(up.wait_recv)
        pl.when(has_high)(down.wait_recv)

    def give_back(kind, source):
        for o in range(1, n_tm):
            start(remote(
                source(at_tm(o)), ret.at[kind, k], ret_send.at[kind, o], ret_recv.at[kind, k], (at_tm(o), s),
            ))
        keep = source(k)
        ret[kind, k] = keep[...]

    blocks = width // 128
    tiles = fields * blocks * rows
    n_obs = obs.shape[1]
    lefts, rights = [], []
    for load in loads[:2]:
        load.wait()
    for at in range(0, n_obs, CHUNK):
        cell = obs[:, pl.ds(at, CHUNK)]
        field = cell // (rows * width)
        row = lax.rem(cell // width, rows)
        block = lax.rem(cell // 128, blocks)
        tile = (field * blocks + block) * rows + row
        lane = jnp.bitwise_and(cell, 127)
        left = (lax.broadcasted_iota(jnp.int32, (tiles, CHUNK), 0) == tile).astype(jnp.float32)
        lefts.append(left.astype(jnp.bfloat16).reshape(tiles // 16, 16, CHUNK))
        right = (lax.broadcasted_iota(jnp.int32, (128, CHUNK), 0) == lane).astype(jnp.float32)
        rights.append(right.astype(jnp.bfloat16))

    def scattered(values_of, target):
        acc = jnp.zeros((3 * tiles, 128), jnp.float32)
        for at in range(0, n_obs, CHUNK):
            left, right = lefts[at // CHUNK], rights[at // CHUNK]
            parts = [
                (left * piece[None]).reshape(tiles, CHUNK)
                for piece in split3(jnp.broadcast_to(values_of(pl.ds(at, CHUNK)), (16, CHUNK)))
            ]
            acc = acc + lax.dot_general(
                jnp.concatenate(parts, axis=0), right, (((1,), (1,)), ((), ())),
                preferred_element_type=jnp.float32,
            )
        x = acc[:tiles] + acc[tiles : 2 * tiles] + acc[2 * tiles :]
        for f in range(fields):
            target[f] = jnp.concatenate([x[(f * blocks + b) * rows :][:rows] for b in range(blocks)], axis=1)

    loads[2].wait()
    scattered(lambda part: weight[:, part] * innov[:, part], r_own)
    for load in loads[3:]:
        load.wait()
    if direct:
        pl.when(owner)(lambda: pl.semaphore_wait(barrier, n_own - 1))
        pl.when(jnp.logical_not(owner))(lambda: pl.semaphore_wait(barrier, n_own))
    else:
        pl.semaphore_wait(barrier, n_tm + n_sp - 2)
    for kind in (DEC, RES, WIND, IEV):
        give(kind)
    scattered(lambda part: weight[:, part], g_own)
    give(DIAG)

    high = 3 * rows - 1
    line = lax.broadcasted_iota(jnp.int32, (3 * rows, width), 0) + (s - 1) * rows
    column = lax.broadcasted_iota(jnp.int32, (3 * rows, width), 1)
    inside = jnp.logical_and(line >= 0, line < n_sp * rows)
    to_right = jnp.logical_and(inside, column < width - 1)
    to_left = jnp.logical_and(inside, column > 0)

    def model(u, by):
        for _ in range(STEPS):
            u = (
                (1.0 - 4.0 * DIFFUSION) * u
                + coef[by, 0] * pltpu.roll(u, high, 0) + coef[by, 1] * pltpu.roll(u, 1, 0)
                + coef[by, 2] * pltpu.roll(u, width - 1, 1) + coef[by, 3] * pltpu.roll(u, 1, 1)
            )
        return u

    def adjoint(v, by):
        for _ in range(STEPS):
            v = (
                (1.0 - 4.0 * DIFFUSION) * v
                + pltpu.roll(coef[by, 0] * v, 1, 0) + pltpu.roll(coef[by, 1] * v, high, 0)
                + pltpu.roll(coef[by, 2] * v, 1, 1) + pltpu.roll(coef[by, 3] * v, width - 1, 1)
            )
        return v

    def precondition(source, target):
        v = [source[at] for at in range(n_tm)]
        for at in range(n_tm - 2, -1, -1):
            v[at] = v[at] + dec_f[at] * v[at + 1]
        for at in range(1, n_tm):
            v[at] = v[at] + dec_f[at - 1] * v[at - 1]
        for at in range(n_tm):
            target[at, mid] = v[at]

    def forward(source):
        jumps, outer = [source[0, mid]], []
        for at in range(n_tm - 1):
            jump = source[at + 1] - model(source[at], at)
            jumps.append(jump[rows : 2 * rows])
            outer.append(iev_f[at + 1] * jump)
        return jumps, outer

    def closed(source, jumps, outer, target):
        for at in range(n_tm):
            image = iev_f[at, mid] * jumps[at] + g_f[at] * source[at, mid]
            if at < n_tm - 1:
                image = image - adjoint(outer[at], at)[rows : 2 * rows]
            target[at] = image

    def send_sums(which, row):
        if direct:
            count = n_own if which == 0 else n_all
            slot = sum_any.at[which, me, pl.ds(0, 1)]
            slot[...] = row
            for o in range(1, count):
                start(remote(slot, slot, any_send.at[which, o], any_recv.at[which, me], place(lax.rem(me + o, count))))
        else:
            count = fields if which == 0 else n_tm
            slot = sum_tm.at[which, k, pl.ds(0, 1)]
            slot[...] = row
            for o in range(1, count):
                start(remote(
                    slot, slot, any_send.at[which, o], any_recv.at[which, k], (lax.rem(k + o, count), s),
                ))

    def wait_sums(which):
        if direct:
            for src in range(n_own):
                slot = sum_any.at[which, src, pl.ds(0, 1)]
                pl.when(me != src)(remote(
                    slot, slot, any_send.at[which, 0], any_recv.at[which, src], (src // n_sp, src % n_sp)).wait_recv)
            sums = jnp.sum(sum_any[which, :, 0:1], axis=0)
        else:
            for src in range(fields):
                slot = sum_tm.at[which, src, pl.ds(0, 1)]
                pl.when(k != src)(remote(
                    slot, slot, any_send.at[which, 0], any_recv.at[which, src], (src, s)).wait_recv)
            slot = sum_sp.at[which, s, pl.ds(0, 1)]
            slot[...] = jnp.sum(sum_tm[which, :, 0:1], axis=0)
            for o in range(1, n_sp):
                start(remote(slot, slot, sp_send.at[which, o], sp_recv.at[which, o], (k, at_sp(o))))
            for o in range(1, n_sp):
                slot = sum_sp.at[which, at_sp(-o), pl.ds(0, 1)]
                remote(slot, slot, sp_send.at[which, o], sp_recv.at[which, o], (k, at_sp(-o))).wait_recv()
            sums = jnp.sum(sum_sp[which, :, 0:1], axis=0)
        return [sums[:, at : at + 1] for at in range(5)]

    def winds_of(at):
        return lambda part: wind_f.at[at, :, part]

    def ievs_of(at):
        return lambda part: iev_f.at[at, part]

    def settle(mark):
        for copy, cond in pending[mark:]:
            if cond is None:
                copy.wait_send()
            else:
                pl.when(cond)(copy.wait_send)
        del pending[mark:]

    @pl.when(owner)
    def work():
        mark = len(pending)
        for edge, cond in ((0, jnp.logical_not(has_low)), (2 * rows, jnp.logical_not(has_high))):
            @pl.when(cond)
            def _():
                for buffer in (z_f, y_f, iev_f):
                    buffer[:, pl.ds(edge, rows)] = jnp.zeros((n_tm, rows, width), jnp.float32)
                wind_f[:, :, pl.ds(edge, rows)] = jnp.zeros((n_tm, 2, rows, width), jnp.float32)
        r_f[k] = r_own[k]
        g_f[k] = g_own[k]
        dec_f[k] = decay[0, k]
        iev_f[k, mid] = iev[0, k]
        wind_f[k, :, mid] = wind[:, 0]
        for at in range(n_tm - 1):
            take(WIND, at)
            to_sides(WIND, at, winds_of(at))
        for at in range(n_tm):
            take(IEV, at)
            if at > 0:
                to_sides(IEV, at, ievs_of(at))
        for at in range(n_tm - 1):
            take(DEC, at)
        for at in range(n_tm):
            take(RES, at)
        precondition(r_f, z_f)
        to_sides(0, 0, lambda part: z_f.at[:, part])
        give_back(Z, lambda at: z_f.at[at, mid])
        rz_part = 0.0
        for at in range(n_tm):
            rz_part = rz_part + folded(r_f[at] * z_f[at, mid])
        for at in range(n_tm - 1):
            from_sides(WIND, at, winds_of(at))
            x_flow, y_flow = wind_f[at, 0], wind_f[at, 1]
            coef[at, 0] = jnp.where(inside, DIFFUSION - 0.5 * x_flow, 0.0)
            coef[at, 1] = jnp.where(inside, DIFFUSION + 0.5 * x_flow, 0.0)
            coef[at, 2] = jnp.where(to_right, DIFFUSION - 0.5 * y_flow, 0.0)
            coef[at, 3] = jnp.where(to_left, DIFFUSION + 0.5 * y_flow, 0.0)
        for at in range(1, n_tm):
            from_sides(IEV, at, ievs_of(at))
        for at in range(n_tm):
            take(DIAG, at)
        from_sides(0, 0, lambda part: z_f.at[:, part])
        jumps, outer = forward(z_f)
        dq_part = 0.0
        for at in range(n_tm):
            z = z_f[at, mid]
            jump_f[at] = jumps[at]
            dq_part = dq_part + folded(iev_f[at, mid] * jumps[at] * jumps[at] + g_f[at] * z * z)
        send_sums(0, packed(rz_part, dq_part))
        closed(z_f, jumps, outer, q_f)
        precondition(q_f, y_f)
        to_sides(1, 0, lambda part: y_f.at[:, part])
        give_back(Q, lambda at: q_f.at[at])
        give_back(Y, lambda at: y_f.at[at, mid])
        from_sides(1, 0, lambda part: y_f.at[:, part])
        jumps, outer = forward(y_f)
        rz, dq = wait_sums(0)[:2]
        alpha = rz / dq
        parts = [0.0, 0.0, 0.0]
        for at in range(n_tm):
            z, jump = z_f[at, mid], jump_f[at]
            r2 = r_f[at] - alpha * q_f[at]
            z2 = z - alpha * y_f[at, mid]
            jump2 = jump - alpha * jumps[at]
            scaled, seen = iev_f[at, mid] * jump2, g_f[at] * z2
            parts[0] = parts[0] + folded(r2 * z2)
            parts[1] = parts[1] + folded(scaled * jump2 + seen * z2)
            parts[2] = parts[2] + folded(2.0 * (scaled * jump + seen * z))
        send_sums(1, packed(rz_part, dq_part, *parts))
        closed(y_f, jumps, outer, w_f)
        give_back(W, lambda at: w_f.at[at])
        settle(mark)

    for kind in (Z, Q, Y):
        for j in range(fields):
            pl.when(k != j)(remote(
                ret.at[kind, j], ret.at[kind, j], ret_send.at[kind, 0], ret_recv.at[kind, j], (j, s)).wait_recv)
    rz, dq, rz2, dd, cross = wait_sums(1)
    alpha, beta = rz / dq, rz2 / rz
    alpha2 = rz2 / (dd + beta * cross + beta * beta * dq)
    first = alpha + alpha2 * (1.0 + beta)
    second = alpha2 * alpha
    for j in range(fields):
        pl.when(k != j)(remote(
            ret.at[W, j], ret.at[W, j], ret_send.at[W, 0], ret_recv.at[W, j], (j, s)).wait_recv)
    for f in range(fields):
        out[0, 0, f] = first * ret[Z, f] - second * ret[Y, f]
        out[1, 0, f] = r_own[f] - first * ret[Q, f] + second * ret[W, f]
    settle(0)


def on_device(wind, decay, iev, obs, weight, innov):
    n_tm, n_sp = lax.axis_size("tm"), lax.axis_size("space")
    fields, rows, width = decay.shape[1:]
    n_own = fields * n_sp
    n_any = n_own if n_tm * n_sp <= DIRECT else 1
    f32 = jnp.float32
    tile = (rows, width)
    tall = (3 * rows, width)
    vmem = pl.BlockSpec(memory_space=pltpu.VMEM)
    both = pl.pallas_call(
        functools.partial(kernel, n_tm, n_sp),
        out_shape=jax.ShapeDtypeStruct((2,) + decay.shape, f32),
        in_specs=[pl.BlockSpec(memory_space=pltpu.HBM)] * 6,
        out_specs=vmem,
        scratch_shapes=[
            pltpu.VMEM(wind.shape, f32),
            pltpu.VMEM(decay.shape, f32),
            pltpu.VMEM(iev.shape, f32),
            pltpu.VMEM(obs.shape, jnp.int32),
            pltpu.VMEM(weight.shape, f32),
            pltpu.VMEM(innov.shape, f32),
            pltpu.SemaphoreType.DMA((6,)),
            pltpu.VMEM((fields,) + tile, f32),
            pltpu.VMEM((fields,) + tile, f32),
            pltpu.VMEM((n_tm,) + tile, f32),
            pltpu.VMEM((n_tm,) + tile, f32),
            pltpu.VMEM((n_tm,) + tile, f32),
            pltpu.VMEM((n_tm,) + tall, f32),
            pltpu.VMEM((n_tm, 2) + tall, f32),
            pltpu.VMEM((n_tm - 1, 4) + tall, f32),
            pltpu.VMEM((n_tm,) + tall, f32),
            pltpu.VMEM((n_tm,) + tall, f32),
            pltpu.VMEM((n_tm,) + tile, f32),
            pltpu.VMEM((n_tm,) + tile, f32),
            pltpu.VMEM((n_tm,) + tile, f32),
            pltpu.VMEM((4, fields) + tile, f32),
            pltpu.VMEM((2, n_any, 8, 128), f32),
            pltpu.VMEM((2, fields, 8, 128), f32),
            pltpu.VMEM((2, n_sp, 8, 128), f32),
            pltpu.SemaphoreType.DMA((5, fields)),
            pltpu.SemaphoreType.DMA((5, n_tm)),
            pltpu.SemaphoreType.DMA((4, n_tm, 2)),
            pltpu.SemaphoreType.DMA((4, n_tm, 2)),
            pltpu.SemaphoreType.DMA((4, n_tm)),
            pltpu.SemaphoreType.DMA((4, fields)),
            pltpu.SemaphoreType.DMA((2, max(n_tm, n_any + n_any))),
            pltpu.SemaphoreType.DMA((2, max(n_tm, n_any))),
            pltpu.SemaphoreType.DMA((2, n_sp)),
            pltpu.SemaphoreType.DMA((2, n_sp)),
        ],
        compiler_params=pltpu.CompilerParams(
            collective_id=0, has_side_effects=True, vmem_limit_bytes=62 * 1024 * 1024
        ),
    )(wind, decay, iev, obs, weight, innov)
    return both[0], both[1]


def solution(mesh):
    placed = (
        P(None, "tm", "space", None),
        P("tm", None, "space", None),
        P("tm", None, "space", None),
        P("tm", "space"),
        P("tm", "space"),
        P("tm", "space"),
    )
    return jax.shard_map(
        on_device,
        mesh=mesh,
        in_specs=placed,
        out_specs=(P("tm", None, "space", None), P("tm", None, "space", None)),
        check_vma=False,
    )
```

```python
import functools

import jax
import jax.numpy as jnp
from jax import lax
from jax.experimental import pallas as pl
from jax.experimental.pallas import tpu as pltpu
from jax.sharding import PartitionSpec as P

STEPS = 4
DIFFUSION = 0.15
MESH = pl.DeviceIdType.MESH
CHUNK = 1024
DIRECT = 64
DEC, RES, WIND, IEV, DIAG = range(5)
Z, Q, Y, W = range(4)


def split(x):
    high = x.astype(jnp.bfloat16)
    return high, (x - high.astype(jnp.float32)).astype(jnp.bfloat16)


def folded(x):
    total = x[:, :128]
    for at in range(128, x.shape[1], 128):
        total = total + x[:, at : at + 128]
    return total


def packed(*terms):
    lane = lax.broadcasted_iota(jnp.int32, (1, 128), 1)
    out = jnp.zeros((1, 128), jnp.float32)
    for at, term in enumerate(terms):
        out = jnp.where(lane == at, jnp.sum(term, axis=(0, 1), keepdims=True), out)
    return out


def kernel(
    n_tm, n_sp, wind_in, decay_in, iev_in, obs_in, weight_in, innov_in, out,
    wind, decay, iev, obs, weight, innov, load_sem,
    r_own, g_own, dec_f, r_f, g_f, iev_f, wind_f, coef, z_f, y_f, jump_f, q_f, w_f, ret,
    sum_any, sum_tm, sum_sp, tm_send, tm_recv, st_send, st_recv, ret_send, ret_recv,
    any_send, any_recv, sp_send, sp_recv, met,
):
    k = lax.axis_index("tm")
    s = lax.axis_index("space")
    fields, rows, width = decay_in.shape[1:]
    n_own = fields * n_sp
    n_all = n_tm * n_sp
    owner = k < fields
    has_next, has_high, has_low = k < n_tm - 1, s < n_sp - 1, s > 0
    me = k * n_sp + s
    direct = n_all <= DIRECT
    mid = pl.ds(rows, rows)
    pending = []

    def at_tm(o):
        return lax.rem(k + o + n_tm, n_tm)

    def at_sp(o):
        return lax.rem(s + o + n_sp, n_sp)

    def place(at):
        return (at // n_sp, lax.rem(at, n_sp))

    def all_of(*conds):
        return functools.reduce(jnp.logical_and, conds)

    loads = [
        pltpu.make_async_copy(src, dst, load_sem.at[at])
        for at, (src, dst) in enumerate((
            (obs_in, obs), (innov_in, innov), (weight_in, weight),
            (decay_in, decay), (wind_in, wind), (iev_in, iev),
        ))
    ]
    for load in loads:
        load.start()
    barrier = pltpu.get_barrier_semaphore()

    def hello(semaphore, device):
        pl.semaphore_signal(semaphore, inc=1, device_id=device, device_id_type=MESH)

    @pl.when(owner)
    def _():
        for o in range(1, n_tm):
            hello(barrier, (at_tm(o), s))
        for cond, side in ((has_low, at_sp(-1)), (has_high, at_sp(1))):
            @pl.when(cond)
            def _():
                for o in range(n_tm):
                    hello(barrier, (at_tm(o), side))

    def remote(src, dst, send, recv, device):
        return pltpu.make_async_remote_copy(
            src_ref=src, dst_ref=dst, send_sem=send, recv_sem=recv,
            device_id=device, device_id_type=MESH,
        )

    def start(copy, *conds):
        cond = all_of(*conds) if conds else None
        pending.append((copy, cond))
        if cond is None:
            copy.start()
        else:
            pl.when(cond)(copy.start)

    tiles_of = (
        (dec_f, lambda at: dec_f.at[at]),
        (r_f, lambda at: r_f.at[at]),
        (wind_f, lambda at: wind_f.at[at, :, mid]),
        (iev_f, lambda at: iev_f.at[at, mid]),
        (g_f, lambda at: g_f.at[at]),
    )
    sources = (
        lambda j: decay.at[0, j], lambda j: r_own.at[j], lambda j: wind.at[:, 0],
        lambda j: iev.at[0, j], lambda j: g_own.at[j],
    )
    last_has = (False, True, False, True, True)

    def give(kind):
        for j in range(fields):
            conds = (k != j,) if last_has[kind] else (k != j, has_next)
            start(remote(
                sources[kind](j), tiles_of[kind][1](k), tm_send.at[kind, j], tm_recv.at[kind, k], (j, s),
            ), *conds)

    def take(kind, at):
        dst = tiles_of[kind][1](at)
        pl.when(k != at)(remote(dst, dst, tm_send.at[kind, 0], tm_recv.at[kind, at], (at, s)).wait_recv)

    def sides(kind, at, pick):
        return (
            remote(pick(mid), pick(pl.ds(0, rows)), st_send.at[kind, at, 0], st_recv.at[kind, at, 0], (k, at_sp(1))),
            remote(pick(mid), pick(pl.ds(2 * rows, rows)), st_send.at[kind, at, 1], st_recv.at[kind, at, 1], (k, at_sp(-1))),
        )

    def to_sides(kind, at, pick):
        up, down = sides(kind, at, pick)
        start(up, has_high)
        start(down, has_low)

    def from_sides(kind, at, pick):
        up, down = sides(kind, at, pick)
        pl.when(has_low)(up.wait_recv)
        pl.when(has_high)(down.wait_recv)

    def give_back(kind, source):
        for o in range(1, n_tm):
            start(remote(
                source(at_tm(o)), ret.at[kind, k], ret_send.at[kind, o], ret_recv.at[kind, k], (at_tm(o), s),
            ))
        keep = source(k)
        ret[kind, k] = keep[...]

    for load in loads[3:]:
        load.wait()
    slabs = 1 + has_low.astype(jnp.int32) + has_high.astype(jnp.int32)
    pl.semaphore_wait(barrier, fields * slabs - owner.astype(jnp.int32))

    reach = [1]
    while 2 * reach[-1] < n_sp - 1:
        reach.append(2 * reach[-1])

    def greet(at):
        if at < len(reach):
            far = reach[at]
            pl.when(s >= far)(lambda: hello(met.at[at, 0], (k, s - far)))
            pl.when(s < n_sp - far)(lambda: hello(met.at[at, 1], (k, s + far)))

    def greeted(at):
        if at < len(reach):
            far = reach[at]
            pl.when(s >= far)(lambda: pl.semaphore_wait(met.at[at, 1], 1))
            pl.when(s < n_sp - far)(lambda: pl.semaphore_wait(met.at[at, 0], 1))

    pl.when(owner)(lambda: greet(0))
    for kind in (DEC, WIND, IEV):
        give(kind)

    blocks = width // 128
    tiles = fields * blocks * rows
    n_obs = obs.shape[1]
    lefts, rights = [], []
    for load in loads[:2]:
        load.wait()
    for at in range(0, n_obs, CHUNK):
        cell = obs[:, pl.ds(at, CHUNK)]
        field = cell // (rows * width)
        row = lax.rem(cell // width, rows)
        block = lax.rem(cell // 128, blocks)
        tile = (field * blocks + block) * rows + row
        lane = jnp.bitwise_and(cell, 127)
        left = (lax.broadcasted_iota(jnp.int32, (tiles, CHUNK), 0) == tile).astype(jnp.float32)
        lefts.append(left.astype(jnp.bfloat16).reshape(tiles // 16, 16, CHUNK))
        right = (lax.broadcasted_iota(jnp.int32, (128, CHUNK), 0) == lane).astype(jnp.float32)
        rights.append(right.astype(jnp.bfloat16))

    def scattered(values_of, target):
        acc = jnp.zeros((2 * tiles, 128), jnp.float32)
        for at in range(0, n_obs, CHUNK):
            left, right = lefts[at // CHUNK], rights[at // CHUNK]
            parts = [
                (left * piece[None]).reshape(tiles, CHUNK)
                for piece in split(jnp.broadcast_to(values_of(pl.ds(at, CHUNK)), (16, CHUNK)))
            ]
            acc = acc + lax.dot_general(
                jnp.concatenate(parts, axis=0), right, (((1,), (1,)), ((), ())),
                preferred_element_type=jnp.float32,
            )
        x = acc[:tiles] + acc[tiles:]
        for f in range(fields):
            target[f] = jnp.concatenate([x[(f * blocks + b) * rows :][:rows] for b in range(blocks)], axis=1)

    loads[2].wait()
    scattered(lambda part: weight[:, part] * innov[:, part], r_own)
    give(RES)
    scattered(lambda part: weight[:, part], g_own)
    give(DIAG)

    high = 3 * rows - 1
    line = lax.broadcasted_iota(jnp.int32, (3 * rows, width), 0) + (s - 1) * rows
    column = lax.broadcasted_iota(jnp.int32, (3 * rows, width), 1)
    inside = jnp.logical_and(line >= 0, line < n_sp * rows)
    to_right = jnp.logical_and(inside, column < width - 1)
    to_left = jnp.logical_and(inside, column > 0)

    def model(u, by):
        for _ in range(STEPS):
            u = (
                (1.0 - 4.0 * DIFFUSION) * u
                + coef[by, 0] * pltpu.roll(u, high, 0) + coef[by, 1] * pltpu.roll(u, 1, 0)
                + coef[by, 2] * pltpu.roll(u, width - 1, 1) + coef[by, 3] * pltpu.roll(u, 1, 1)
            )
        return u

    def adjoint(v, by):
        for _ in range(STEPS):
            v = (
                (1.0 - 4.0 * DIFFUSION) * v
                + pltpu.roll(coef[by, 0] * v, 1, 0) + pltpu.roll(coef[by, 1] * v, high, 0)
                + pltpu.roll(coef[by, 2] * v, 1, 1) + pltpu.roll(coef[by, 3] * v, width - 1, 1)
            )
        return v

    def precondition(source, target):
        v = [source[at] for at in range(n_tm)]
        for at in range(n_tm - 2, -1, -1):
            v[at] = v[at] + dec_f[at] * v[at + 1]
        for at in range(1, n_tm):
            v[at] = v[at] + dec_f[at - 1] * v[at - 1]
        for at in range(n_tm):
            target[at, mid] = v[at]

    def forward(source):
        jumps, outer = [source[0, mid]], []
        for at in range(n_tm - 1):
            jump = source[at + 1] - model(source[at], at)
            jumps.append(jump[rows : 2 * rows])
            outer.append(iev_f[at + 1] * jump)
        return jumps, outer

    def closed(source, jumps, outer, target):
        for at in range(n_tm):
            image = iev_f[at, mid] * jumps[at] + g_f[at] * source[at, mid]
            if at < n_tm - 1:
                image = image - adjoint(outer[at], at)[rows : 2 * rows]
            target[at] = image

    def send_sums(which, row):
        if direct:
            count = n_own if which == 0 else n_all
            slot = sum_any.at[which, me, pl.ds(0, 1)]
            slot[...] = row
            for o in range(1, count):
                start(remote(slot, slot, any_send.at[which, o], any_recv.at[which, me], place(lax.rem(me + o, count))))
        else:
            count = fields if which == 0 else n_tm
            slot = sum_tm.at[which, k, pl.ds(0, 1)]
            slot[...] = row
            for o in range(1, count):
                start(remote(
                    slot, slot, any_send.at[which, o], any_recv.at[which, k], (lax.rem(k + o, count), s),
                ))

    def wait_sums(which):
        if direct:
            for src in range(n_own):
                slot = sum_any.at[which, src, pl.ds(0, 1)]
                pl.when(me != src)(remote(
                    slot, slot, any_send.at[which, 0], any_recv.at[which, src], (src // n_sp, src % n_sp)).wait_recv)
            sums = jnp.sum(sum_any[which, :, 0:1], axis=0)
        else:
            for src in range(fields):
                slot = sum_tm.at[which, src, pl.ds(0, 1)]
                pl.when(k != src)(remote(
                    slot, slot, any_send.at[which, 0], any_recv.at[which, src], (src, s)).wait_recv)
            slot = sum_sp.at[which, s, pl.ds(0, 1)]
            slot[...] = jnp.sum(sum_tm[which, :, 0:1], axis=0)
            for o in range(1, n_sp):
                start(remote(slot, slot, sp_send.at[which, o], sp_recv.at[which, o], (k, at_sp(o))))
            for o in range(1, n_sp):
                slot = sum_sp.at[which, at_sp(-o), pl.ds(0, 1)]
                remote(slot, slot, sp_send.at[which, o], sp_recv.at[which, o], (k, at_sp(-o))).wait_recv()
            sums = jnp.sum(sum_sp[which, :, 0:1], axis=0)
        return [sums[:, at : at + 1] for at in range(5)]

    def winds_of(at):
        return lambda part: wind_f.at[at, :, part]

    def ievs_of(at):
        return lambda part: iev_f.at[at, part]

    def settle(mark):
        for copy, cond in pending[mark:]:
            if cond is None:
                copy.wait_send()
            else:
                pl.when(cond)(copy.wait_send)
        del pending[mark:]

    @pl.when(owner)
    def work():
        mark = len(pending)
        for edge, cond in ((0, jnp.logical_not(has_low)), (2 * rows, jnp.logical_not(has_high))):
            @pl.when(cond)
            def _():
                for buffer in (z_f, y_f, iev_f):
                    buffer[:, pl.ds(edge, rows)] = jnp.zeros((n_tm, rows, width), jnp.float32)
                wind_f[:, :, pl.ds(edge, rows)] = jnp.zeros((n_tm, 2, rows, width), jnp.float32)
        r_f[k] = r_own[k]
        g_f[k] = g_own[k]
        dec_f[k] = decay[0, k]
        iev_f[k, mid] = iev[0, k]
        wind_f[k, :, mid] = wind[:, 0]
        greeted(0)
        greet(1)
        for at in range(n_tm - 1):
            take(WIND, at)
            to_sides(WIND, at, winds_of(at))
        for at in range(n_tm):
            take(IEV, at)
            if at > 0:
                to_sides(IEV, at, ievs_of(at))
        greeted(1)
        greet(2)
        for at in range(n_tm - 1):
            take(DEC, at)
        for at in range(n_tm):
            take(RES, at)
        precondition(r_f, z_f)
        to_sides(0, 0, lambda part: z_f.at[:, part])
        give_back(Z, lambda at: z_f.at[at, mid])
        rz_part = 0.0
        for at in range(n_tm):
            rz_part = rz_part + folded(r_f[at] * z_f[at, mid])
        for at in range(n_tm - 1):
            from_sides(WIND, at, winds_of(at))
            x_flow, y_flow = wind_f[at, 0], wind_f[at, 1]
            coef[at, 0] = jnp.where(inside, DIFFUSION - 0.5 * x_flow, 0.0)
            coef[at, 1] = jnp.where(inside, DIFFUSION + 0.5 * x_flow, 0.0)
            coef[at, 2] = jnp.where(to_right, DIFFUSION - 0.5 * y_flow, 0.0)
            coef[at, 3] = jnp.where(to_left, DIFFUSION + 0.5 * y_flow, 0.0)
        for at in range(1, n_tm):
            from_sides(IEV, at, ievs_of(at))
        for at in range(n_tm):
            take(DIAG, at)
        from_sides(0, 0, lambda part: z_f.at[:, part])
        jumps, outer = forward(z_f)
        dq_part = 0.0
        for at in range(n_tm):
            z = z_f[at, mid]
            jump_f[at] = jumps[at]
            dq_part = dq_part + folded(iev_f[at, mid] * jumps[at] * jumps[at] + g_f[at] * z * z)
        for at in range(2, len(reach)):
            greeted(at)
            greet(at + 1)
        send_sums(0, packed(rz_part, dq_part))
        closed(z_f, jumps, outer, q_f)
        precondition(q_f, y_f)
        to_sides(1, 0, lambda part: y_f.at[:, part])
        give_back(Q, lambda at: q_f.at[at])
        give_back(Y, lambda at: y_f.at[at, mid])
        from_sides(1, 0, lambda part: y_f.at[:, part])
        jumps, outer = forward(y_f)
        rz, dq = wait_sums(0)[:2]
        alpha = rz / dq
        parts = [0.0, 0.0, 0.0]
        for at in range(n_tm):
            z, jump = z_f[at, mid], jump_f[at]
            r2 = r_f[at] - alpha * q_f[at]
            z2 = z - alpha * y_f[at, mid]
            jump2 = jump - alpha * jumps[at]
            scaled, seen = iev_f[at, mid] * jump2, g_f[at] * z2
            parts[0] = parts[0] + folded(r2 * z2)
            parts[1] = parts[1] + folded(scaled * jump2 + seen * z2)
            parts[2] = parts[2] + folded(2.0 * (scaled * jump + seen * z))
        send_sums(1, packed(rz_part, dq_part, *parts))
        closed(y_f, jumps, outer, w_f)
        give_back(W, lambda at: w_f.at[at])
        settle(mark)

    for kind in (Z, Q, Y):
        for j in range(fields):
            pl.when(k != j)(remote(
                ret.at[kind, j], ret.at[kind, j], ret_send.at[kind, 0], ret_recv.at[kind, j], (j, s)).wait_recv)
    rz, dq, rz2, dd, cross = wait_sums(1)
    alpha, beta = rz / dq, rz2 / rz
    alpha2 = rz2 / (dd + beta * cross + beta * beta * dq)
    first = alpha + alpha2 * (1.0 + beta)
    second = alpha2 * alpha
    for j in range(fields):
        pl.when(k != j)(remote(
            ret.at[W, j], ret.at[W, j], ret_send.at[W, 0], ret_recv.at[W, j], (j, s)).wait_recv)
    for f in range(fields):
        out[0, 0, f] = first * ret[Z, f] - second * ret[Y, f]
        out[1, 0, f] = r_own[f] - first * ret[Q, f] + second * ret[W, f]
    settle(0)


def on_device(wind, decay, iev, obs, weight, innov):
    n_tm, n_sp = lax.axis_size("tm"), lax.axis_size("space")
    fields, rows, width = decay.shape[1:]
    n_own = fields * n_sp
    n_any = n_own if n_tm * n_sp <= DIRECT else 1
    f32 = jnp.float32
    tile = (rows, width)
    tall = (3 * rows, width)
    vmem = pl.BlockSpec(memory_space=pltpu.VMEM)
    both = pl.pallas_call(
        functools.partial(kernel, n_tm, n_sp),
        out_shape=pltpu.VMEM((2,) + decay.shape, f32),
        in_specs=[pl.BlockSpec(memory_space=pltpu.HBM)] * 6,
        out_specs=vmem,
        scratch_shapes=[
            pltpu.VMEM(wind.shape, f32),
            pltpu.VMEM(decay.shape, f32),
            pltpu.VMEM(iev.shape, f32),
            pltpu.VMEM(obs.shape, jnp.int32),
            pltpu.VMEM(weight.shape, f32),
            pltpu.VMEM(innov.shape, f32),
            pltpu.SemaphoreType.DMA((6,)),
            pltpu.VMEM((fields,) + tile, f32),
            pltpu.VMEM((fields,) + tile, f32),
            pltpu.VMEM((n_tm,) + tile, f32),
            pltpu.VMEM((n_tm,) + tile, f32),
            pltpu.VMEM((n_tm,) + tile, f32),
            pltpu.VMEM((n_tm,) + tall, f32),
            pltpu.VMEM((n_tm, 2) + tall, f32),
            pltpu.VMEM((n_tm - 1, 4) + tall, f32),
            pltpu.VMEM((n_tm,) + tall, f32),
            pltpu.VMEM((n_tm,) + tall, f32),
            pltpu.VMEM((n_tm,) + tile, f32),
            pltpu.VMEM((n_tm,) + tile, f32),
            pltpu.VMEM((n_tm,) + tile, f32),
            pltpu.VMEM((4, fields) + tile, f32),
            pltpu.VMEM((2, n_any, 8, 128), f32),
            pltpu.VMEM((2, fields, 8, 128), f32),
            pltpu.VMEM((2, n_sp, 8, 128), f32),
            pltpu.SemaphoreType.DMA((5, fields)),
            pltpu.SemaphoreType.DMA((5, n_tm)),
            pltpu.SemaphoreType.DMA((4, n_tm, 2)),
            pltpu.SemaphoreType.DMA((4, n_tm, 2)),
            pltpu.SemaphoreType.DMA((4, n_tm)),
            pltpu.SemaphoreType.DMA((4, fields)),
            pltpu.SemaphoreType.DMA((2, max(n_tm, n_any + n_any))),
            pltpu.SemaphoreType.DMA((2, max(n_tm, n_any))),
            pltpu.SemaphoreType.DMA((2, n_sp)),
            pltpu.SemaphoreType.DMA((2, n_sp)),
            pltpu.SemaphoreType.REGULAR((n_sp, 2)),
        ],
        compiler_params=pltpu.CompilerParams(
            collective_id=0, has_side_effects=True, vmem_limit_bytes=62 * 1024 * 1024
        ),
    )(wind, decay, iev, obs, weight, innov)
    return both[0], both[1]


def solution(mesh):
    placed = (
        P(None, "tm", "space", None),
        P("tm", None, "space", None),
        P("tm", None, "space", None),
        P("tm", "space"),
        P("tm", "space"),
        P("tm", "space"),
    )
    return jax.shard_map(
        on_device,
        mesh=mesh,
        in_specs=placed,
        out_specs=(P("tm", None, "space", None), P("tm", None, "space", None)),
        check_vma=False,
    )
```

```python
import functools

import jax
import jax.numpy as jnp
from jax import lax
from jax.experimental import pallas as pl
from jax.experimental.pallas import tpu as pltpu
from jax.sharding import PartitionSpec as P

STEPS = 4
DIFFUSION = 0.15
MESH = pl.DeviceIdType.MESH
CHUNK = 1024
DIRECT = 64
DEC, WIND, IEV, RES, DIAG = range(5)
NEXT = 3
Z, Q, Y, W = range(4)


def split(x):
    high = x.astype(jnp.bfloat16)
    return high, (x - high.astype(jnp.float32)).astype(jnp.bfloat16)


POWER = (0, 1, 2, 0, 1, 2, 0, 1)


def folded(x):
    total = x[:, :128]
    for at in range(128, x.shape[1], 128):
        total = total + x[:, at : at + 128]
    return total


def packed(*terms):
    lane = lax.broadcasted_iota(jnp.int32, (1, 128), 1)
    out = jnp.zeros((1, 128), jnp.float32)
    for at, term in enumerate(terms):
        total = term if term.shape == (1, 1) else jnp.sum(term, axis=(0, 1), keepdims=True)
        out = jnp.where(lane == at, total, out)
    return out


def kernel(
    n_tm, n_sp, wind_in, decay_in, iev_in, obs_in, weight_in, innov_in, out,
    obs, weight, innov, load_sem, keep_sem,
    r_own, g_own, dec_f, r_f, g_f, iev_f, wind_f, coef, z_f, y_f, jump_f, q_f, w_f, ret,
    sums, sum_tm, tm_send, tm_recv, by_send, by_recv, st_send, st_recv, ret_send, ret_recv,
    any_send, any_recv, sp_send, sp_recv, met,
):
    k = lax.axis_index("tm")
    s = lax.axis_index("space")
    fields, rows, width = decay_in.shape[1:]
    n_own = fields * n_sp
    n_all = n_tm * n_sp
    owner = k < fields
    has_next, has_high, has_low = k < n_tm - 1, s < n_sp - 1, s > 0
    me = k * n_sp + s
    direct = n_all <= DIRECT
    mid = pl.ds(rows, rows)
    pending = []

    def at_tm(o):
        return lax.rem(k + o + n_tm, n_tm)

    def at_sp(o):
        return lax.rem(s + o + n_sp, n_sp)

    def place(at):
        return (at // n_sp, lax.rem(at, n_sp))

    def all_of(*conds):
        return functools.reduce(jnp.logical_and, conds)

    loads = [
        pltpu.make_async_copy(src, dst, load_sem.at[at])
        for at, (src, dst) in enumerate((
            (obs_in, obs), (innov_in, innov), (weight_in, weight),
        ))
    ]
    for load in loads:
        load.start()
    barrier = pltpu.get_barrier_semaphore()

    def hello(semaphore, device):
        pl.semaphore_signal(semaphore, inc=1, device_id=device, device_id_type=MESH)

    @pl.when(owner)
    def _():
        for o in range(1, n_tm):
            hello(barrier, (at_tm(o), s))
        for cond, side in ((has_low, at_sp(-1)), (has_high, at_sp(1))):
            @pl.when(cond)
            def _():
                for o in range(n_tm):
                    hello(barrier, (at_tm(o), side))

    def remote(src, dst, send, recv, device):
        return pltpu.make_async_remote_copy(
            src_ref=src, dst_ref=dst, send_sem=send, recv_sem=recv,
            device_id=device, device_id_type=MESH,
        )

    def start(copy, *conds):
        cond = all_of(*conds) if conds else None
        pending.append((copy, cond))
        if cond is None:
            copy.start()
        else:
            pl.when(cond)(copy.start)

    tiles_of = (
        lambda at, part: dec_f.at[at, part],
        lambda at, part: wind_f.at[at, :, part],
        lambda at, part: iev_f.at[at, part],
        lambda at, part: r_f.at[at, part],
        lambda at, part: g_f.at[at],
    )
    sources = (
        lambda j: decay_in.at[0, j], lambda j: wind_in.at[:, 0], lambda j: iev_in.at[0, j],
        lambda j: r_own.at[j], lambda j: g_own.at[j],
    )
    last_has = (False, False, True, True, True)

    def give(kind):
        for j in range(fields):
            conds = (k != j,) if last_has[kind] else (k != j, has_next)
            start(remote(
                sources[kind](j), tiles_of[kind](k, mid), tm_send.at[kind, j], tm_recv.at[kind, k], (j, s),
            ), *conds)

    beside = ((has_high, pl.ds(0, rows), at_sp(1)), (has_low, pl.ds(2 * rows, rows), at_sp(-1)))

    def give_beside():
        for side, (cond, part, slab) in enumerate(beside):
            for j in range(fields):
                start(remote(
                    r_own.at[j], r_f.at[k, part], by_send.at[side, j], by_recv.at[side, k], (j, slab)), cond)

    def take_beside(at):
        for side, (cond, slab) in enumerate(((has_low, at_sp(-1)), (has_high, at_sp(1)))):
            dst = r_f.at[at, beside[side][1]]
            pl.when(cond)(remote(dst, dst, by_send.at[side, 0], by_recv.at[side, at], (at, slab)).wait_recv)

    def take(kind, at):
        dst = tiles_of[kind](at, mid)
        pl.when(k != at)(remote(dst, dst, tm_send.at[kind, 0], tm_recv.at[kind, at], (at, s)).wait_recv)

    def sides(kind, at, pick):
        return (
            remote(pick(mid), pick(pl.ds(0, rows)), st_send.at[kind, at, 0], st_recv.at[kind, at, 0], (k, at_sp(1))),
            remote(pick(mid), pick(pl.ds(2 * rows, rows)), st_send.at[kind, at, 1], st_recv.at[kind, at, 1], (k, at_sp(-1))),
        )

    def to_sides(kind, at, pick):
        up, down = sides(kind, at, pick)
        start(up, has_high)
        start(down, has_low)

    def from_sides(kind, at, pick):
        up, down = sides(kind, at, pick)
        pl.when(has_low)(up.wait_recv)
        pl.when(has_high)(down.wait_recv)

    def give_back(kind, source):
        for o in range(1, n_tm):
            start(remote(
                source(at_tm(o)), ret.at[kind, k], ret_send.at[kind, o], ret_recv.at[kind, k], (at_tm(o), s),
            ))
        keep = source(k)
        ret[kind, k] = keep[...]

    keeps = [
        pltpu.make_async_copy(sources[kind](k), tiles_of[kind](k, mid), keep_sem.at[kind])
        for kind in (DEC, WIND, IEV)
    ]

    @pl.when(owner)
    def _():
        for copy in keeps:
            copy.start()

    slabs = 1 + has_low.astype(jnp.int32) + has_high.astype(jnp.int32)
    pl.semaphore_wait(barrier, fields * slabs - owner.astype(jnp.int32))

    reach = [1]
    while 2 * reach[-1] < n_sp - 1:
        reach.append(2 * reach[-1])

    def greet(at):
        if at < len(reach):
            far = reach[at]
            pl.when(s >= far)(lambda: hello(met.at[at, 0], (k, s - far)))
            pl.when(s < n_sp - far)(lambda: hello(met.at[at, 1], (k, s + far)))

    def greeted(at):
        if at < len(reach):
            far = reach[at]
            pl.when(s >= far)(lambda: pl.semaphore_wait(met.at[at, 1], 1))
            pl.when(s < n_sp - far)(lambda: pl.semaphore_wait(met.at[at, 0], 1))

    pl.when(owner)(lambda: greet(0))
    for kind in (DEC, WIND, IEV):
        give(kind)

    blocks = width // 128
    tiles = fields * blocks * rows
    n_obs = obs.shape[1]
    lefts, rights = [], []
    for load in loads[:2]:
        load.wait()
    for at in range(0, n_obs, CHUNK):
        cell = obs[:, pl.ds(at, CHUNK)]
        field = cell // (rows * width)
        row = lax.rem(cell // width, rows)
        block = lax.rem(cell // 128, blocks)
        tile = (field * blocks + block) * rows + row
        lane = jnp.bitwise_and(cell, 127)
        left = (lax.broadcasted_iota(jnp.int32, (tiles, CHUNK), 0) == tile).astype(jnp.float32)
        lefts.append(left.astype(jnp.bfloat16).reshape(tiles // 16, 16, CHUNK))
        right = (lax.broadcasted_iota(jnp.int32, (128, CHUNK), 0) == lane).astype(jnp.float32)
        rights.append(right.astype(jnp.bfloat16))

    def scattered(values_of, target):
        acc = jnp.zeros((2 * tiles, 128), jnp.float32)
        for at in range(0, n_obs, CHUNK):
            left, right = lefts[at // CHUNK], rights[at // CHUNK]
            parts = [
                (left * piece[None]).reshape(tiles, CHUNK)
                for piece in split(jnp.broadcast_to(values_of(pl.ds(at, CHUNK)), (16, CHUNK)))
            ]
            acc = acc + lax.dot_general(
                jnp.concatenate(parts, axis=0), right, (((1,), (1,)), ((), ())),
                preferred_element_type=jnp.float32,
            )
        x = acc[:tiles] + acc[tiles:]
        for f in range(fields):
            target[f] = jnp.concatenate([x[(f * blocks + b) * rows :][:rows] for b in range(blocks)], axis=1)

    loads[2].wait()
    scattered(lambda part: weight[:, part] * innov[:, part], r_own)
    give_beside()
    give(RES)
    scattered(lambda part: weight[:, part], g_own)
    give(DIAG)

    high = 3 * rows - 1
    line = lax.broadcasted_iota(jnp.int32, (3 * rows, width), 0) + (s - 1) * rows
    column = lax.broadcasted_iota(jnp.int32, (3 * rows, width), 1)
    inside = jnp.logical_and(line >= 0, line < n_sp * rows)
    to_right = jnp.logical_and(inside, column < width - 1)
    to_left = jnp.logical_and(inside, column > 0)

    def model(u, by):
        for _ in range(STEPS):
            u = (
                (1.0 - 4.0 * DIFFUSION) * u
                + coef[by, 0] * pltpu.roll(u, high, 0) + coef[by, 1] * pltpu.roll(u, 1, 0)
                + coef[by, 2] * pltpu.roll(u, width - 1, 1) + coef[by, 3] * pltpu.roll(u, 1, 1)
            )
        return u

    def adjoint(v, by):
        for _ in range(STEPS):
            v = (
                (1.0 - 4.0 * DIFFUSION) * v
                + pltpu.roll(coef[by, 0] * v, 1, 0) + pltpu.roll(coef[by, 1] * v, high, 0)
                + pltpu.roll(coef[by, 2] * v, 1, 1) + pltpu.roll(coef[by, 3] * v, width - 1, 1)
            )
        return v

    def precondition(source, target, part):
        v = [source[at] for at in range(n_tm)]
        for at in range(n_tm - 2, -1, -1):
            v[at] = v[at] + dec_f[at, part] * v[at + 1]
        for at in range(1, n_tm):
            v[at] = v[at] + dec_f[at - 1, part] * v[at - 1]
        for at in range(n_tm):
            target[at, part] = v[at]

    def forward(source):
        jumps, outer = [source[0, mid]], []
        for at in range(n_tm - 1):
            jump = source[at + 1] - model(source[at], at)
            jumps.append(jump[rows : 2 * rows])
            outer.append(iev_f[at + 1] * jump)
        return jumps, outer

    def closed(source, jumps, outer, target):
        for at in range(n_tm):
            image = iev_f[at, mid] * jumps[at] + g_f[at] * source[at, mid]
            if at < n_tm - 1:
                image = image - adjoint(outer[at], at)[rows : 2 * rows]
            target[at] = image

    def send_sums(row):
        if direct:
            slot = sums.at[pl.ds(me, 1)]
            slot[...] = row
            for o in range(1, n_all):
                start(remote(slot, slot, any_send.at[o], any_recv.at[me], place(lax.rem(me + o, n_all))))
        else:
            slot = sum_tm.at[k, pl.ds(0, 1)]
            slot[...] = row
            for o in range(1, n_tm):
                start(remote(slot, slot, any_send.at[o], any_recv.at[k], (at_tm(o), s)))

    def wait_sums():
        if direct:
            for src in range(n_own):
                slot = sums.at[pl.ds(src, 1)]
                pl.when(me != src)(remote(
                    slot, slot, any_send.at[0], any_recv.at[src], (src // n_sp, src % n_sp)).wait_recv)
        else:
            for src in range(fields):
                slot = sum_tm.at[src, pl.ds(0, 1)]
                pl.when(k != src)(remote(
                    slot, slot, any_send.at[0], any_recv.at[src], (src, s)).wait_recv)
            slot = sums.at[pl.ds(s * 8, 8)]
            slot[...] = jnp.concatenate(
                [sum_tm[at, 0:1] for at in range(fields)] + [jnp.zeros((8 - fields, 128), jnp.float32)], axis=0)
            for o in range(1, n_sp):
                start(remote(slot, slot, sp_send.at[o], sp_recv.at[o], (k, at_sp(o))))
            for o in range(1, n_sp):
                slot = sums.at[pl.ds(at_sp(-o) * 8, 8)]
                remote(slot, slot, sp_send.at[o], sp_recv.at[o], (k, at_sp(-o))).wait_recv()
        return sums[...]

    reach_of = (range(n_tm - 1), range(n_tm - 1), range(1, n_tm))

    def settle(mark):
        for copy, cond in pending[mark:]:
            if cond is None:
                copy.wait_send()
            else:
                pl.when(cond)(copy.wait_send)
        del pending[mark:]

    @pl.when(owner)
    def work():
        mark = len(pending)
        for edge, cond in ((0, jnp.logical_not(has_low)), (2 * rows, jnp.logical_not(has_high))):
            @pl.when(cond)
            def _():
                for buffer in (r_f, y_f, iev_f, dec_f):
                    buffer[:, pl.ds(edge, rows)] = jnp.zeros((n_tm, rows, width), jnp.float32)
                wind_f[:, :, pl.ds(edge, rows)] = jnp.zeros((n_tm, 2, rows, width), jnp.float32)
        r_f[k, mid] = r_own[k]
        g_f[k] = g_own[k]
        for copy in keeps:
            copy.wait()
        greeted(0)
        for kind in (DEC, WIND, IEV):
            for at in reach_of[kind]:
                take(kind, at)
                to_sides(kind, at, functools.partial(tiles_of[kind], at))
        take(IEV, 0)
        for at in range(n_tm - 1):
            from_sides(DEC, at, functools.partial(tiles_of[DEC], at))
        for at in range(n_tm):
            take(RES, at)
            take_beside(at)
        greet(1)
        precondition(r_f, z_f, slice(None))
        give_back(Z, lambda at: z_f.at[at, mid])
        rz_part = 0.0
        for at in range(n_tm):
            rz_part = rz_part + folded(r_f[at, mid] * z_f[at, mid])
        for at in range(n_tm - 1):
            from_sides(WIND, at, functools.partial(tiles_of[WIND], at))
            x_flow, y_flow = wind_f[at, 0], wind_f[at, 1]
            coef[at, 0] = jnp.where(inside, DIFFUSION - 0.5 * x_flow, 0.0)
            coef[at, 1] = jnp.where(inside, DIFFUSION + 0.5 * x_flow, 0.0)
            coef[at, 2] = jnp.where(to_right, DIFFUSION - 0.5 * y_flow, 0.0)
            coef[at, 3] = jnp.where(to_left, DIFFUSION + 0.5 * y_flow, 0.0)
        for at in range(1, n_tm):
            from_sides(IEV, at, functools.partial(tiles_of[IEV], at))
        for at in range(n_tm):
            take(DIAG, at)
        jumps, outer = forward(z_f)
        dq_part = 0.0
        for at in range(n_tm):
            z = z_f[at, mid]
            jump_f[at] = jumps[at]
            dq_part = dq_part + folded(iev_f[at, mid] * jumps[at] * jumps[at] + g_f[at] * z * z)
        rz_part, dq_part = (jnp.sum(part, axis=(0, 1), keepdims=True) for part in (rz_part, dq_part))
        guess = jnp.where(dq_part > 0.0, rz_part / jnp.where(dq_part > 0.0, dq_part, 1.0), 0.0)
        closed(z_f, jumps, outer, q_f)
        precondition(q_f, y_f, mid)
        to_sides(NEXT, 0, lambda part: y_f.at[:, part])
        give_back(Q, lambda at: q_f.at[at])
        give_back(Y, lambda at: y_f.at[at, mid])
        greeted(1)
        greet(2)
        from_sides(NEXT, 0, lambda part: y_f.at[:, part])
        jumps, outer = forward(y_f)
        terms = [0.0] * len(POWER)
        for at in range(n_tm):
            z, y, q, jump_z, jump_y = z_f[at, mid], y_f[at, mid], q_f[at], jump_f[at], jumps[at]
            r2, z2, jump2 = r_f[at, mid] - guess * q, z - guess * y, jump_z - guess * jump_y
            here = iev_f[at, mid], g_f[at]
            scaled2, seen2 = here[0] * jump2, here[1] * z2
            scaled_y, seen_y = here[0] * jump_y, here[1] * y
            for i, term in enumerate((
                r2 * z2, -(r2 * y + z2 * q), q * y,
                scaled2 * jump2 + seen2 * z2, -2.0 * (scaled2 * jump_y + seen2 * y), scaled_y * jump_y + seen_y * y,
                2.0 * (scaled2 * jump_z + seen2 * z), -2.0 * (scaled_y * jump_z + seen_y * z),
            )):
                terms[i] = terms[i] + folded(term)
        for at in range(2, len(reach)):
            greeted(at)
            greet(at + 1)
        send_sums(packed(rz_part, dq_part, guess, *terms))
        closed(y_f, jumps, outer, w_f)
        give_back(W, lambda at: w_f.at[at])
        settle(mark)

    for kind in (Z, Q, Y):
        for j in range(fields):
            pl.when(k != j)(remote(
                ret.at[kind, j], ret.at[kind, j], ret_send.at[kind, 0], ret_recv.at[kind, j], (j, s)).wait_recv)
    table = wait_sums()
    rz, dq = (jnp.sum(table[:, at : at + 1], axis=0, keepdims=True) for at in range(2))
    alpha = rz / dq
    shift = alpha - table[:, 2:3]
    lane = lax.broadcasted_iota(jnp.int32, table.shape, 1)
    scale = jnp.ones(table.shape, jnp.float32)
    for at, power in enumerate(POWER):
        if power:
            scale = jnp.where(lane == at + 3, shift if power == 1 else shift * shift, scale)
    table = jnp.sum(table * scale, axis=0, keepdims=True)
    lane = lax.broadcasted_iota(jnp.int32, (1, 128), 1)

    def group(least, most):
        inside = jnp.logical_and(lane >= 3 + least, lane < 3 + most)
        return jnp.sum(jnp.where(inside, table, 0.0), axis=1, keepdims=True)

    rz2, dd, cross = group(0, 3), group(3, 6), group(6, 8)
    beta = rz2 / rz
    alpha2 = rz2 / (dd + beta * cross + beta * beta * dq)
    first = alpha + alpha2 * (1.0 + beta)
    second = alpha2 * alpha
    for j in range(fields):
        pl.when(k != j)(remote(
            ret.at[W, j], ret.at[W, j], ret_send.at[W, 0], ret_recv.at[W, j], (j, s)).wait_recv)
    for f in range(fields):
        out[0, 0, f] = first * ret[Z, f] - second * ret[Y, f]
        out[1, 0, f] = r_own[f] - first * ret[Q, f] + second * ret[W, f]
    settle(0)


def on_device(wind, decay, iev, obs, weight, innov):
    n_tm, n_sp = lax.axis_size("tm"), lax.axis_size("space")
    fields, rows, width = decay.shape[1:]
    n_own = fields * n_sp
    direct = n_tm * n_sp <= DIRECT
    f32 = jnp.float32
    tile = (rows, width)
    tall = (3 * rows, width)
    vmem = pl.BlockSpec(memory_space=pltpu.VMEM)
    both = pl.pallas_call(
        functools.partial(kernel, n_tm, n_sp),
        out_shape=pltpu.VMEM((2,) + decay.shape, f32),
        in_specs=[pl.BlockSpec(memory_space=pltpu.HBM)] * 6,
        out_specs=vmem,
        scratch_shapes=[
            pltpu.VMEM(obs.shape, jnp.int32),
            pltpu.VMEM(weight.shape, f32),
            pltpu.VMEM(innov.shape, f32),
            pltpu.SemaphoreType.DMA((3,)),
            pltpu.SemaphoreType.DMA((3,)),
            pltpu.VMEM((fields,) + tile, f32),
            pltpu.VMEM((fields,) + tile, f32),
            pltpu.VMEM((n_tm,) + tall, f32),
            pltpu.VMEM((n_tm,) + tall, f32),
            pltpu.VMEM((n_tm,) + tile, f32),
            pltpu.VMEM((n_tm,) + tall, f32),
            pltpu.VMEM((n_tm, 2) + tall, f32),
            pltpu.VMEM((n_tm - 1, 4) + tall, f32),
            pltpu.VMEM((n_tm,) + tall, f32),
            pltpu.VMEM((n_tm,) + tall, f32),
            pltpu.VMEM((n_tm,) + tile, f32),
            pltpu.VMEM((n_tm,) + tile, f32),
            pltpu.VMEM((n_tm,) + tile, f32),
            pltpu.VMEM((4, fields) + tile, f32),
            pltpu.VMEM((n_own if direct else 8 * n_sp, 128), f32),
            pltpu.VMEM((n_tm, 8, 128), f32),
            pltpu.SemaphoreType.DMA((5, fields)),
            pltpu.SemaphoreType.DMA((5, n_tm)),
            pltpu.SemaphoreType.DMA((2, fields)),
            pltpu.SemaphoreType.DMA((2, n_tm)),
            pltpu.SemaphoreType.DMA((4, n_tm, 2)),
            pltpu.SemaphoreType.DMA((4, n_tm, 2)),
            pltpu.SemaphoreType.DMA((4, n_tm)),
            pltpu.SemaphoreType.DMA((4, fields)),
            pltpu.SemaphoreType.DMA((n_tm * n_sp if direct else n_tm,)),
            pltpu.SemaphoreType.DMA((n_own if direct else n_tm,)),
            pltpu.SemaphoreType.DMA((n_sp,)),
            pltpu.SemaphoreType.DMA((n_sp,)),
            pltpu.SemaphoreType.REGULAR((n_sp, 2)),
        ],
        compiler_params=pltpu.CompilerParams(
            collective_id=0, has_side_effects=True, vmem_limit_bytes=62 * 1024 * 1024
        ),
    )(wind, decay, iev, obs, weight, innov)
    return both[0], both[1]


def solution(mesh):
    placed = (
        P(None, "tm", "space", None),
        P("tm", None, "space", None),
        P("tm", None, "space", None),
        P("tm", "space"),
        P("tm", "space"),
        P("tm", "space"),
    )
    return jax.shard_map(
        on_device,
        mesh=mesh,
        in_specs=placed,
        out_specs=(P("tm", None, "space", None), P("tm", None, "space", None)),
        check_vma=False,
    )
```

```python
import functools

import jax
import jax.numpy as jnp
from jax import lax
from jax.experimental import pallas as pl
from jax.experimental.pallas import tpu as pltpu
from jax.sharding import PartitionSpec as P

STEPS = 4
DIFFUSION = 0.15
MESH = pl.DeviceIdType.MESH
CHUNK = 2048
DIRECT = 64
DEC, WIND, IEV, RES, DIAG = range(5)
NEXT = 3
S_TM, S_BY, S_MATE, S_UP, S_DOWN, S_RET, S_ANY = range(7)
R_DIAG, R_BY, R_MATE, R_RET, R_LAST, R_ANY, R_SIDE = range(7)
Z, Q, Y, W = range(4)


def split(x):
    high = x.astype(jnp.bfloat16)
    return high, (x - high.astype(jnp.float32)).astype(jnp.bfloat16)


POWER = (0, 1, 2, 0, 1, 2, 0, 1)


def folded(x):
    total = x[:, :128]
    for at in range(128, x.shape[1], 128):
        total = total + x[:, at : at + 128]
    return total


def packed(*terms):
    lane = lax.broadcasted_iota(jnp.int32, (1, 128), 1)
    out = jnp.zeros((1, 128), jnp.float32)
    for at, term in enumerate(terms):
        total = term if term.shape == (1, 1) else jnp.sum(term, axis=(0, 1), keepdims=True)
        out = jnp.where(lane == at, total, out)
    return out


def kernel(
    n_tm, n_sp, wind_in, decay_in, iev_in, obs_in, weight_in, innov_in, out,
    obs, weight, innov, load_sem,
    r_own, g_own, dec_f, r_f, g_f, iev_f, wind_f, coef, z_f, y_f, jump_f, q_f, w_f, ret,
    sums, sum_tm, size, sent, tm_recv, come, far_send, far_recv, met,
):
    k = lax.axis_index("tm")
    s = lax.axis_index("space")
    fields, rows, width = decay_in.shape[1:]
    n_own = fields * n_sp
    n_all = n_tm * n_sp
    owner = k < fields
    has_next, has_high, has_low = k < n_tm - 1, s < n_sp - 1, s > 0
    me = k * n_sp + s
    direct = n_all <= DIRECT
    mid = pl.ds(rows, rows)

    def at_tm(o):
        return lax.rem(k + o + n_tm, n_tm)

    def at_sp(o):
        return lax.rem(s + o + n_sp, n_sp)

    def place(at):
        return (at // n_sp, lax.rem(at, n_sp))

    def all_of(*conds):
        return functools.reduce(jnp.logical_and, conds)

    loads = [
        pltpu.make_async_copy(src, dst, load_sem.at[0])
        for src, dst in ((obs_in, obs), (innov_in, innov), (weight_in, weight))
    ]
    for load in loads:
        load.start()
    barrier = pltpu.get_barrier_semaphore()

    def hello(semaphore, device):
        pl.semaphore_signal(semaphore, inc=1, device_id=device, device_id_type=MESH)

    @pl.when(owner)
    def _():
        for o in range(1, n_tm):
            hello(barrier, (at_tm(o), s))
        for cond, side in ((has_low, at_sp(-1)), (has_high, at_sp(1))):
            @pl.when(cond)
            def _():
                for o in range(n_tm):
                    hello(barrier, (at_tm(o), side))

    def remote(src, dst, send, recv, device):
        return pltpu.make_async_remote_copy(
            src_ref=src, dst_ref=dst, send_sem=send, recv_sem=recv,
            device_id=device, device_id_type=MESH,
        )

    def start(copy, *conds):
        if conds:
            pl.when(all_of(*conds))(copy.start)
        else:
            copy.start()

    tile_lines = rows * width // 128

    def await_lines(semaphore, count):
        pltpu.make_async_copy(size.at[pl.ds(0, count)], size.at[pl.ds(0, count)], semaphore).wait()

    def await_tiles(semaphore, count, *conds):
        if conds:
            pl.when(all_of(*conds))(lambda: await_lines(semaphore, count * tile_lines))
        else:
            await_lines(semaphore, count * tile_lines)

    tiles_of = (
        lambda at, part: dec_f.at[at, part],
        lambda at, part: wind_f.at[at, :, part],
        lambda at, part: iev_f.at[at, part],
        lambda at, part: r_f.at[at, part],
        lambda at, part: g_f.at[at],
    )
    sources = (
        lambda j: decay_in.at[0, j], lambda j: wind_in.at[:, 0], lambda j: iev_in.at[0, j],
        lambda j: r_own.at[j], lambda j: g_own.at[j],
    )
    last_has = (False, False, True, True, True)

    def came(kind, at):
        return come.at[R_DIAG] if kind == DIAG else tm_recv.at[kind, at]

    def give(kind):
        for j in range(fields):
            conds = (k != j,) if last_has[kind] else (k != j, has_next)
            start(remote(
                sources[kind](j), tiles_of[kind](k, mid), sent.at[S_TM], came(kind, k), (j, s),
            ), *conds)

    even = lax.rem(s, 2) == 0
    low, upper = pl.ds(0, rows), pl.ds(2 * rows, rows)

    off_chip = jnp.logical_or(all_of(even, has_low), all_of(~even, has_high))

    def give_beside():
        for cond, part, slab in ((all_of(even, has_low), upper, at_sp(-1)), (all_of(~even, has_high), low, at_sp(1))):
            for j in range(fields):
                copy = remote(r_own.at[j], r_f.at[k, part], sent.at[S_BY], come.at[R_BY], (j, slab))
                start(copy, cond)

    def to_mate(at):
        for cond, part, slab in ((even, low, at_sp(1)), (~even, upper, at_sp(-1))):
            start(remote(r_f.at[at, mid], r_f.at[at, part], sent.at[S_MATE], come.at[R_MATE], (k, slab)), cond)

    def take(kind, at):
        dst = tiles_of[kind](at, mid)
        pl.when(k != at)(remote(dst, dst, sent.at[S_TM], came(kind, at), (at, s)).wait_recv)

    def to_sides(kind, pick):
        side = R_SIDE + 2 * kind
        start(remote(pick(mid), pick(low), sent.at[S_UP], come.at[side], (k, at_sp(1))), has_high)
        start(remote(pick(mid), pick(upper), sent.at[S_DOWN], come.at[side + 1], (k, at_sp(-1))), has_low)

    def from_sides(kind, count):
        await_tiles(come.at[R_SIDE + 2 * kind], count, has_low)
        await_tiles(come.at[R_SIDE + 2 * kind + 1], count, has_high)

    def give_back(kind, source):
        for o in range(1, n_tm):
            start(remote(
                source(at_tm(o)), ret.at[kind, k], sent.at[S_RET], come.at[R_LAST if kind == W else R_RET], (at_tm(o), s),
            ))
        keep = source(k)
        ret[kind, k] = keep[...]

    keeps = [
        pltpu.make_async_copy(sources[kind](k), tiles_of[kind](k, mid), load_sem.at[1])
        for kind in (DEC, WIND, IEV)
    ]

    @pl.when(owner)
    def _():
        for copy in keeps:
            copy.start()

    slabs = 1 + has_low.astype(jnp.int32) + has_high.astype(jnp.int32)
    pl.semaphore_wait(barrier, fields * slabs - owner.astype(jnp.int32))

    reach = [1]
    while 2 * reach[-1] < n_sp - 1:
        reach.append(2 * reach[-1])

    def greet(at):
        if at < len(reach):
            far = reach[at]
            pl.when(s >= far)(lambda: hello(met.at[at, 0], (k, s - far)))
            pl.when(s < n_sp - far)(lambda: hello(met.at[at, 1], (k, s + far)))

    def greeted(at):
        if at < len(reach):
            far = reach[at]
            pl.when(s >= far)(lambda: pl.semaphore_wait(met.at[at, 1], 1))
            pl.when(s < n_sp - far)(lambda: pl.semaphore_wait(met.at[at, 0], 1))

    pl.when(owner)(lambda: greet(0))
    for kind in (DEC, WIND, IEV):
        give(kind)

    blocks = width // 128
    tiles = fields * blocks * rows
    n_obs = obs.shape[1]
    lefts, rights = [], []
    await_lines(load_sem.at[0], 3 * n_obs // 128)
    for at in range(0, n_obs, CHUNK):
        cell = obs[:, pl.ds(at, CHUNK)]
        field = cell // (rows * width)
        row = lax.rem(cell // width, rows)
        block = lax.rem(cell // 128, blocks)
        tile = (field * blocks + block) * rows + row
        lane = jnp.bitwise_and(cell, 127)
        left = (lax.broadcasted_iota(jnp.int32, (tiles, CHUNK), 0) == tile).astype(jnp.float32)
        lefts.append(left.astype(jnp.bfloat16).reshape(tiles // 16, 16, CHUNK))
        right = (lax.broadcasted_iota(jnp.int32, (128, CHUNK), 0) == lane).astype(jnp.float32)
        rights.append(right.astype(jnp.bfloat16))

    def scattered(values_of, target):
        acc = jnp.zeros((2 * tiles, 128), jnp.float32)
        for at in range(0, n_obs, CHUNK):
            left, right = lefts[at // CHUNK], rights[at // CHUNK]
            parts = [
                (left * piece[None]).reshape(tiles, CHUNK)
                for piece in split(jnp.broadcast_to(values_of(pl.ds(at, CHUNK)), (16, CHUNK)))
            ]
            acc = acc + lax.dot_general(
                jnp.concatenate(parts, axis=0), right, (((1,), (1,)), ((), ())),
                preferred_element_type=jnp.float32,
            )
        x = acc[:tiles] + acc[tiles:]
        for f in range(fields):
            target[f] = jnp.concatenate([x[(f * blocks + b) * rows :][:rows] for b in range(blocks)], axis=1)

    scattered(lambda part: weight[:, part] * innov[:, part], r_own)
    give_beside()
    give(RES)
    scattered(lambda part: weight[:, part], g_own)
    give(DIAG)

    high = 3 * rows - 1
    line = lax.broadcasted_iota(jnp.int32, (3 * rows, width), 0) + (s - 1) * rows
    column = lax.broadcasted_iota(jnp.int32, (3 * rows, width), 1)
    inside = jnp.logical_and(line >= 0, line < n_sp * rows)
    to_right = jnp.logical_and(inside, column < width - 1)
    to_left = jnp.logical_and(inside, column > 0)

    def model(us):
        for _ in range(STEPS):
            us = [
                (1.0 - 4.0 * DIFFUSION) * u
                + coef[by, 0] * pltpu.roll(u, high, 0) + coef[by, 1] * pltpu.roll(u, 1, 0)
                + coef[by, 2] * pltpu.roll(u, width - 1, 1) + coef[by, 3] * pltpu.roll(u, 1, 1)
                for by, u in enumerate(us)
            ]
        return us

    def adjoint(vs):
        for _ in range(STEPS):
            vs = [
                (1.0 - 4.0 * DIFFUSION) * v
                + pltpu.roll(coef[by, 0] * v, 1, 0) + pltpu.roll(coef[by, 1] * v, high, 0)
                + pltpu.roll(coef[by, 2] * v, 1, 1) + pltpu.roll(coef[by, 3] * v, width - 1, 1)
                for by, v in enumerate(vs)
            ]
        return vs

    def precondition(source, target, part):
        v = [source[at] for at in range(n_tm)]
        for at in range(n_tm - 2, -1, -1):
            v[at] = v[at] + dec_f[at, part] * v[at + 1]
        for at in range(1, n_tm):
            v[at] = v[at] + dec_f[at - 1, part] * v[at - 1]
        for at in range(n_tm):
            target[at, part] = v[at]

    def forward(source):
        jumps, outer = [source[0, mid]], []
        for at, ahead in enumerate(model([source[at] for at in range(n_tm - 1)])):
            jump = source[at + 1] - ahead
            jumps.append(jump[rows : 2 * rows])
            outer.append(iev_f[at + 1] * jump)
        return jumps, outer

    def closed(source, jumps, outer, target):
        back = adjoint(outer)
        for at in range(n_tm):
            image = iev_f[at, mid] * jumps[at] + g_f[at] * source[at, mid]
            if at < n_tm - 1:
                image = image - back[at][rows : 2 * rows]
            target[at] = image

    def send_sums(row):
        if direct:
            slot = sums.at[pl.ds(me, 1)]
            slot[...] = row
            for to in range(n_all):
                start(remote(
                    slot, slot, sent.at[S_ANY], come.at[R_ANY], (to // n_sp, to % n_sp)), me != to)
        else:
            slot = sum_tm.at[k, pl.ds(0, 1)]
            slot[...] = row
            for o in range(1, n_tm):
                start(remote(slot, slot, far_send.at[0, o], far_recv.at[0, k], (at_tm(o), s)))

    def wait_sums():
        if direct:
            pl.when(owner)(lambda: await_lines(come.at[R_ANY], n_own - 1))
            pl.when(~owner)(lambda: await_lines(come.at[R_ANY], n_own))
        else:
            for src in range(fields):
                slot = sum_tm.at[src, pl.ds(0, 1)]
                pl.when(k != src)(remote(
                    slot, slot, far_send.at[0, 0], far_recv.at[0, src], (src, s)).wait_recv)
            slot = sums.at[pl.ds(s * 8, 8)]
            slot[...] = jnp.concatenate(
                [sum_tm[at, 0:1] for at in range(fields)] + [jnp.zeros((8 - fields, 128), jnp.float32)], axis=0)
            for o in range(1, n_sp):
                start(remote(slot, slot, far_send.at[1, o], far_recv.at[1, o], (k, at_sp(o))))
            for o in range(1, n_sp):
                slot = sums.at[pl.ds(at_sp(-o) * 8, 8)]
                remote(slot, slot, far_send.at[1, o], far_recv.at[1, o], (k, at_sp(-o))).wait_recv()
        return sums[...]

    reach_of = (range(n_tm - 1), range(n_tm - 1), range(1, n_tm))

    @pl.when(owner)
    def work():
        for edge, cond in ((0, jnp.logical_not(has_low)), (2 * rows, jnp.logical_not(has_high))):
            @pl.when(cond)
            def _():
                for buffer in (r_f, y_f, iev_f, dec_f):
                    buffer[:, pl.ds(edge, rows)] = jnp.zeros((n_tm, rows, width), jnp.float32)
                wind_f[:, :, pl.ds(edge, rows)] = jnp.zeros((n_tm, 2, rows, width), jnp.float32)
        r_f[k, mid] = r_own[k]
        g_f[k] = g_own[k]
        await_tiles(load_sem.at[1], 4)
        greeted(0)
        for kind in (DEC, WIND, IEV):
            for at in reach_of[kind]:
                take(kind, at)
                to_sides(kind, functools.partial(tiles_of[kind], at))
        take(IEV, 0)
        from_sides(DEC, n_tm - 1)
        for at in range(n_tm):
            take(RES, at)
            to_mate(at)
        await_tiles(come.at[R_MATE], n_tm)
        await_tiles(come.at[R_BY], n_tm, off_chip)
        greet(1)
        precondition(r_f, z_f, slice(None))
        give_back(Z, lambda at: z_f.at[at, mid])
        rz_part = 0.0
        for at in range(n_tm):
            rz_part = rz_part + folded(r_f[at, mid] * z_f[at, mid])
        from_sides(WIND, 2 * (n_tm - 1))
        for at in range(n_tm - 1):
            x_flow, y_flow = wind_f[at, 0], wind_f[at, 1]
            coef[at, 0] = jnp.where(inside, DIFFUSION - 0.5 * x_flow, 0.0)
            coef[at, 1] = jnp.where(inside, DIFFUSION + 0.5 * x_flow, 0.0)
            coef[at, 2] = jnp.where(to_right, DIFFUSION - 0.5 * y_flow, 0.0)
            coef[at, 3] = jnp.where(to_left, DIFFUSION + 0.5 * y_flow, 0.0)
        from_sides(IEV, n_tm - 1)
        await_tiles(come.at[R_DIAG], n_tm - 1)
        jumps, outer = forward(z_f)
        dq_part = 0.0
        for at in range(n_tm):
            z = z_f[at, mid]
            jump_f[at] = jumps[at]
            dq_part = dq_part + folded(iev_f[at, mid] * jumps[at] * jumps[at] + g_f[at] * z * z)
        rz_part, dq_part = (jnp.sum(part, axis=(0, 1), keepdims=True) for part in (rz_part, dq_part))
        guess = jnp.where(dq_part > 0.0, rz_part / jnp.where(dq_part > 0.0, dq_part, 1.0), 0.0)
        closed(z_f, jumps, outer, q_f)
        precondition(q_f, y_f, mid)
        to_sides(NEXT, lambda part: y_f.at[:, part])
        give_back(Q, lambda at: q_f.at[at])
        give_back(Y, lambda at: y_f.at[at, mid])
        greeted(1)
        greet(2)
        from_sides(NEXT, n_tm)
        jumps, outer = forward(y_f)
        terms = [0.0] * len(POWER)
        for at in range(n_tm):
            z, y, q, jump_z, jump_y = z_f[at, mid], y_f[at, mid], q_f[at], jump_f[at], jumps[at]
            r2, z2, jump2 = r_f[at, mid] - guess * q, z - guess * y, jump_z - guess * jump_y
            here = iev_f[at, mid], g_f[at]
            scaled2, seen2 = here[0] * jump2, here[1] * z2
            scaled_y, seen_y = here[0] * jump_y, here[1] * y
            for i, term in enumerate((
                r2 * z2, -(r2 * y + z2 * q), q * y,
                scaled2 * jump2 + seen2 * z2, -2.0 * (scaled2 * jump_y + seen2 * y), scaled_y * jump_y + seen_y * y,
                2.0 * (scaled2 * jump_z + seen2 * z), -2.0 * (scaled_y * jump_z + seen_y * z),
            )):
                terms[i] = terms[i] + folded(term)
        for at in range(2, len(reach)):
            greeted(at)
            greet(at + 1)
        send_sums(packed(rz_part, dq_part, guess, *terms))
        closed(y_f, jumps, outer, w_f)
        give_back(W, lambda at: w_f.at[at])
        await_tiles(sent.at[S_MATE], n_tm)
        await_tiles(sent.at[S_UP], 4 * (n_tm - 1) + n_tm, has_high)
        await_tiles(sent.at[S_DOWN], 4 * (n_tm - 1) + n_tm, has_low)
        await_tiles(sent.at[S_RET], 4 * (n_tm - 1))
        if direct:
            await_lines(sent.at[S_ANY], n_all - 1)
        else:
            slot = sum_tm.at[k, pl.ds(0, 1)]
            for o in range(1, n_tm):
                remote(slot, slot, far_send.at[0, o], far_recv.at[0, k], (at_tm(o), s)).wait_send()

    def back(semaphore, kinds):
        await_tiles(semaphore, kinds * (fields - 1), owner)
        await_tiles(semaphore, kinds * fields, ~owner)

    back(come.at[R_RET], 3)
    table = wait_sums()
    rz, dq = (jnp.sum(table[:, at : at + 1], axis=0, keepdims=True) for at in range(2))
    alpha = rz / dq
    shift = alpha - table[:, 2:3]
    lane = lax.broadcasted_iota(jnp.int32, table.shape, 1)
    scale = jnp.ones(table.shape, jnp.float32)
    for at, power in enumerate(POWER):
        if power:
            scale = jnp.where(lane == at + 3, shift if power == 1 else shift * shift, scale)
    table = jnp.sum(table * scale, axis=0, keepdims=True)
    lane = lax.broadcasted_iota(jnp.int32, (1, 128), 1)

    def group(least, most):
        inside = jnp.logical_and(lane >= 3 + least, lane < 3 + most)
        return jnp.sum(jnp.where(inside, table, 0.0), axis=1, keepdims=True)

    rz2, dd, cross = group(0, 3), group(3, 6), group(6, 8)
    beta = rz2 / rz
    alpha2 = rz2 / (dd + beta * cross + beta * beta * dq)
    first = alpha + alpha2 * (1.0 + beta)
    second = alpha2 * alpha
    back(come.at[R_LAST], 1)
    for f in range(fields):
        out[0, 0, f] = first * ret[Z, f] - second * ret[Y, f]
        out[1, 0, f] = r_own[f] - first * ret[Q, f] + second * ret[W, f]
    for has, kinds in ((has_next, 6), (~has_next, 3)):
        await_tiles(sent.at[S_TM], kinds * (fields - 1), has, owner)
        await_tiles(sent.at[S_TM], kinds * fields, has, ~owner)
    await_tiles(sent.at[S_BY], fields, off_chip)
    if not direct:
        slot = sums.at[pl.ds(s * 8, 8)]
        for o in range(1, n_sp):
            remote(slot, slot, far_send.at[1, o], far_recv.at[1, o], (k, at_sp(o))).wait_send()


def on_device(wind, decay, iev, obs, weight, innov):
    n_tm, n_sp = lax.axis_size("tm"), lax.axis_size("space")
    fields, rows, width = decay.shape[1:]
    n_own = fields * n_sp
    direct = n_tm * n_sp <= DIRECT
    f32 = jnp.float32
    tile = (rows, width)
    tall = (3 * rows, width)
    vmem = pl.BlockSpec(memory_space=pltpu.VMEM)
    both = pl.pallas_call(
        functools.partial(kernel, n_tm, n_sp),
        out_shape=pltpu.VMEM((2,) + decay.shape, f32),
        in_specs=[pl.BlockSpec(memory_space=pltpu.HBM)] * 6,
        out_specs=vmem,
        scratch_shapes=[
            pltpu.VMEM(obs.shape, jnp.int32),
            pltpu.VMEM(weight.shape, f32),
            pltpu.VMEM(innov.shape, f32),
            pltpu.SemaphoreType.DMA((2,)),
            pltpu.VMEM((fields,) + tile, f32),
            pltpu.VMEM((fields,) + tile, f32),
            pltpu.VMEM((n_tm,) + tall, f32),
            pltpu.VMEM((n_tm,) + tall, f32),
            pltpu.VMEM((n_tm,) + tile, f32),
            pltpu.VMEM((n_tm,) + tall, f32),
            pltpu.VMEM((n_tm, 2) + tall, f32),
            pltpu.VMEM((n_tm - 1, 4) + tall, f32),
            pltpu.VMEM((n_tm,) + tall, f32),
            pltpu.VMEM((n_tm,) + tall, f32),
            pltpu.VMEM((n_tm,) + tile, f32),
            pltpu.VMEM((n_tm,) + tile, f32),
            pltpu.VMEM((n_tm,) + tile, f32),
            pltpu.VMEM((4, fields) + tile, f32),
            pltpu.VMEM((n_own if direct else 8 * n_sp, 128), f32),
            pltpu.VMEM((n_tm, 8, 128), f32),
            pltpu.VMEM((rows * width // 128 * max(6 * fields, 5 * n_tm - 4), 128), f32),
            pltpu.SemaphoreType.DMA((7,)),
            pltpu.SemaphoreType.DMA((4, n_tm)),
            pltpu.SemaphoreType.DMA((6 + 2 * 4,)),
            pltpu.SemaphoreType.DMA((1, 1) if direct else (2, max(n_tm, n_sp))),
            pltpu.SemaphoreType.DMA((1, 1) if direct else (2, max(n_tm, n_sp))),
            pltpu.SemaphoreType.REGULAR((3 if n_sp <= 8 else n_sp, 2)),
        ],
        compiler_params=pltpu.CompilerParams(
            collective_id=0, has_side_effects=True, vmem_limit_bytes=62 * 1024 * 1024
        ),
    )(wind, decay, iev, obs, weight, innov)
    return both[0], both[1]


def solution(mesh):
    placed = (
        P(None, "tm", "space", None),
        P("tm", None, "space", None),
        P("tm", None, "space", None),
        P("tm", "space"),
        P("tm", "space"),
        P("tm", "space"),
    )
    return jax.shard_map(
        on_device,
        mesh=mesh,
        in_specs=placed,
        out_specs=(P("tm", None, "space", None), P("tm", None, "space", None)),
        check_vma=False,
    )
```

```python
import functools

import jax
import jax.numpy as jnp
from jax import lax
from jax.experimental import pallas as pl
from jax.experimental.pallas import tpu as pltpu
from jax.sharding import PartitionSpec as P

STEPS = 4
DIFFUSION = 0.15
MESH = pl.DeviceIdType.MESH
CHUNK = 2048
DIRECT = 64
DEC, WIND, IEV, RES, DIAG = range(5)
NEXT = 3
S_TM, S_BY, S_MATE, S_UP, S_DOWN, S_RET, S_ANY = range(7)
R_DIAG, R_BY, R_MATE, R_RET, R_LAST, R_ANY, R_SIDE = range(7)
Z, Q, Y, W = range(4)


def split(x):
    high = x.astype(jnp.bfloat16)
    return high, (x - high.astype(jnp.float32)).astype(jnp.bfloat16)


POWER = (0, 1, 2, 0, 1, 2, 0, 1)


def folded(x):
    total = x[:, :128]
    for at in range(128, x.shape[1], 128):
        total = total + x[:, at : at + 128]
    return total


def packed(*terms):
    lane = lax.broadcasted_iota(jnp.int32, (1, 128), 1)
    out = jnp.zeros((1, 128), jnp.float32)
    for at, term in enumerate(terms):
        total = term if term.shape == (1, 1) else jnp.sum(term, axis=(0, 1), keepdims=True)
        out = jnp.where(lane == at, total, out)
    return out


def kernel(
    n_tm, n_sp, wind_in, decay_in, iev_in, obs_in, weight_in, innov_in, out,
    obs, weight, innov, load_sem,
    r_own, g_own, dec_f, r_f, g_f, iev_f, wind_f, coef, z_f, y_f, jump_f, q_f, w_f, ret,
    sums, sum_tm, size, sent, tm_recv, come, far_send, far_recv, met,
):
    k = lax.axis_index("tm")
    s = lax.axis_index("space")
    fields, rows, width = decay_in.shape[1:]
    n_own = fields * n_sp
    n_all = n_tm * n_sp
    owner = k < fields
    has_next, has_high, has_low = k < n_tm - 1, s < n_sp - 1, s > 0
    me = k * n_sp + s
    direct = n_all <= DIRECT
    mid = pl.ds(rows, rows)

    def at_tm(o):
        return lax.rem(k + o + n_tm, n_tm)

    def at_sp(o):
        return lax.rem(s + o + n_sp, n_sp)

    def place(at):
        return (at // n_sp, lax.rem(at, n_sp))

    def all_of(*conds):
        return functools.reduce(jnp.logical_and, conds)

    loads = [
        pltpu.make_async_copy(src, dst, load_sem.at[0])
        for src, dst in ((obs_in, obs), (innov_in, innov), (weight_in, weight))
    ]
    for load in loads:
        load.start()
    barrier = pltpu.get_barrier_semaphore()

    def hello(semaphore, device):
        pl.semaphore_signal(semaphore, inc=1, device_id=device, device_id_type=MESH)

    @pl.when(owner)
    def _():
        for o in range(1, n_tm):
            hello(barrier, (at_tm(o), s))
        for cond, side in ((has_low, at_sp(-1)), (has_high, at_sp(1))):
            @pl.when(cond)
            def _():
                for o in range(n_tm):
                    hello(barrier, (at_tm(o), side))

    def remote(src, dst, send, recv, device):
        return pltpu.make_async_remote_copy(
            src_ref=src, dst_ref=dst, send_sem=send, recv_sem=recv,
            device_id=device, device_id_type=MESH,
        )

    def start(copy, *conds):
        if conds:
            pl.when(all_of(*conds))(copy.start)
        else:
            copy.start()

    tile_lines = rows * width // 128

    def await_lines(semaphore, count):
        pltpu.make_async_copy(size.at[pl.ds(0, count)], size.at[pl.ds(0, count)], semaphore).wait()

    def await_tiles(semaphore, count, *conds):
        if conds:
            pl.when(all_of(*conds))(lambda: await_lines(semaphore, count * tile_lines))
        else:
            await_lines(semaphore, count * tile_lines)

    tiles_of = (
        lambda at, part: dec_f.at[at, part],
        lambda at, part: wind_f.at[at, :, part],
        lambda at, part: iev_f.at[at, part],
        lambda at, part: r_f.at[at, part],
        lambda at, part: g_f.at[at],
    )
    sources = (
        lambda j: decay_in.at[0, j], lambda j: wind_in.at[:, 0], lambda j: iev_in.at[0, j],
        lambda j: r_own.at[j], lambda j: g_own.at[j],
    )
    last_has = (False, False, True, True, True)

    def came(kind, at):
        return come.at[R_DIAG] if kind == DIAG else tm_recv.at[kind, at]

    def give(kind, *when):
        for j in range(fields):
            conds = (k != j,) + when if last_has[kind] else (k != j, has_next) + when
            start(remote(
                sources[kind](j), tiles_of[kind](k, mid), sent.at[S_TM], came(kind, k), (j, s),
            ), *conds)

    even = lax.rem(s, 2) == 0
    low, upper = pl.ds(0, rows), pl.ds(2 * rows, rows)

    off_chip = jnp.logical_or(all_of(even, has_low), all_of(~even, has_high))

    def give_beside():
        for cond, part, slab in ((all_of(even, has_low), upper, at_sp(-1)), (all_of(~even, has_high), low, at_sp(1))):
            for j in range(fields):
                copy = remote(r_own.at[j], r_f.at[k, part], sent.at[S_BY], come.at[R_BY], (j, slab))
                start(copy, cond)

    def to_mate(at):
        for cond, part, slab in ((even, low, at_sp(1)), (~even, upper, at_sp(-1))):
            start(remote(r_f.at[at, mid], r_f.at[at, part], sent.at[S_MATE], come.at[R_MATE], (k, slab)), cond)

    def take(kind, at):
        dst = tiles_of[kind](at, mid)
        pl.when(k != at)(remote(dst, dst, sent.at[S_TM], came(kind, at), (at, s)).wait_recv)

    needed = {DEC: rows, WIND: rows, IEV: STEPS, NEXT: rows}

    def to_sides(kind, source, target, *conds):
        rim, side = needed[kind], R_SIDE + 2 * kind
        start(remote(
            source(rows - rim, rim), target(pl.ds(rows - rim, rim)), sent.at[S_UP], come.at[side], (k, at_sp(1)),
        ), has_high, *conds)
        start(remote(
            source(0, rim), target(pl.ds(2 * rows, rim)), sent.at[S_DOWN], come.at[side + 1], (k, at_sp(-1)),
        ), has_low, *conds)

    def from_sides(kind, count):
        lines = count * needed[kind] * width // 128
        for side, cond in enumerate((has_low, has_high)):
            pl.when(cond)(functools.partial(await_lines, come.at[R_SIDE + 2 * kind + side], lines))

    def held(kind, at):
        return lambda first, rim: tiles_of[kind](at, pl.ds(rows + first, rim))

    own = {
        DEC: lambda first, rim: decay_in.at[0, k, pl.ds(first, rim)],
        WIND: lambda first, rim: wind_in.at[:, 0, pl.ds(first, rim)],
        IEV: lambda first, rim: iev_in.at[0, k, pl.ds(first, rim)],
    }

    def give_back(kind, source):
        for o in range(1, n_tm):
            start(remote(
                source(at_tm(o)), ret.at[kind, k], sent.at[S_RET], come.at[R_LAST if kind == W else R_RET], (at_tm(o), s),
            ))
        keep = source(k)
        ret[kind, k] = keep[...]

    keeps = [
        pltpu.make_async_copy(sources[kind](k), tiles_of[kind](k, mid), load_sem.at[1])
        for kind in (DEC, WIND, IEV)
    ]

    @pl.when(owner)
    def _():
        for copy in keeps:
            copy.start()

    slabs = 1 + has_low.astype(jnp.int32) + has_high.astype(jnp.int32)
    pl.semaphore_wait(barrier, fields * slabs - owner.astype(jnp.int32))

    reach = [1]
    while 2 * reach[-1] < n_sp - 1:
        reach.append(2 * reach[-1])

    def greet(at):
        if at < len(reach):
            far = reach[at]
            pl.when(s >= far)(lambda: hello(met.at[at, 0], (k, s - far)))
            pl.when(s < n_sp - far)(lambda: hello(met.at[at, 1], (k, s + far)))

    def greeted(at):
        if at < len(reach):
            far = reach[at]
            pl.when(s >= far)(lambda: pl.semaphore_wait(met.at[at, 1], 1))
            pl.when(s < n_sp - far)(lambda: pl.semaphore_wait(met.at[at, 0], 1))

    pl.when(owner)(lambda: greet(0))
    for kind in (DEC, WIND):
        give(kind)
    give(IEV, k > 0)

    @pl.when(owner)
    def _():
        for kind in (DEC, WIND):
            to_sides(kind, own[kind], functools.partial(tiles_of[kind], k))
        to_sides(IEV, own[IEV], functools.partial(tiles_of[IEV], k), k > 0)


    blocks = width // 128
    tiles = fields * blocks * rows
    n_obs = obs.shape[1]
    lefts, rights = [], []
    await_lines(load_sem.at[0], 3 * n_obs // 128)
    for at in range(0, n_obs, CHUNK):
        cell = obs[:, pl.ds(at, CHUNK)]
        field = cell // (rows * width)
        row = lax.rem(cell // width, rows)
        block = lax.rem(cell // 128, blocks)
        tile = (field * blocks + block) * rows + row
        lane = jnp.bitwise_and(cell, 127)
        left = (lax.broadcasted_iota(jnp.int32, (tiles, CHUNK), 0) == tile).astype(jnp.float32)
        lefts.append(left.astype(jnp.bfloat16).reshape(tiles // 16, 16, CHUNK))
        right = (lax.broadcasted_iota(jnp.int32, (128, CHUNK), 0) == lane).astype(jnp.float32)
        rights.append(right.astype(jnp.bfloat16))

    def scattered(values_of, target):
        acc = jnp.zeros((2 * tiles, 128), jnp.float32)
        for at in range(0, n_obs, CHUNK):
            left, right = lefts[at // CHUNK], rights[at // CHUNK]
            parts = [
                (left * piece[None]).reshape(tiles, CHUNK)
                for piece in split(jnp.broadcast_to(values_of(pl.ds(at, CHUNK)), (16, CHUNK)))
            ]
            acc = acc + lax.dot_general(
                jnp.concatenate(parts, axis=0), right, (((1,), (1,)), ((), ())),
                preferred_element_type=jnp.float32,
            )
        x = acc[:tiles] + acc[tiles:]
        for f in range(fields):
            target[f] = jnp.concatenate([x[(f * blocks + b) * rows :][:rows] for b in range(blocks)], axis=1)

    scattered(lambda part: weight[:, part] * innov[:, part], r_own)
    give_beside()
    give(RES)
    give(IEV, k == 0)
    scattered(lambda part: weight[:, part], g_own)
    give(DIAG)

    high = 3 * rows - 1
    line = lax.broadcasted_iota(jnp.int32, (3 * rows, width), 0) + (s - 1) * rows
    column = lax.broadcasted_iota(jnp.int32, (3 * rows, width), 1)
    inside = jnp.logical_and(line >= 0, line < n_sp * rows)
    to_right = jnp.logical_and(inside, column < width - 1)
    to_left = jnp.logical_and(inside, column > 0)

    def model(us):
        for _ in range(STEPS):
            us = [
                (1.0 - 4.0 * DIFFUSION) * u
                + coef[by, 0] * pltpu.roll(u, high, 0) + coef[by, 1] * pltpu.roll(u, 1, 0)
                + coef[by, 2] * pltpu.roll(u, width - 1, 1) + coef[by, 3] * pltpu.roll(u, 1, 1)
                for by, u in enumerate(us)
            ]
        return us

    def adjoint(vs):
        for _ in range(STEPS):
            vs = [
                (1.0 - 4.0 * DIFFUSION) * v
                + pltpu.roll(coef[by, 0] * v, 1, 0) + pltpu.roll(coef[by, 1] * v, high, 0)
                + pltpu.roll(coef[by, 2] * v, 1, 1) + pltpu.roll(coef[by, 3] * v, width - 1, 1)
                for by, v in enumerate(vs)
            ]
        return vs

    def precondition(source, target, part):
        v = [source[at] for at in range(n_tm)]
        for at in range(n_tm - 2, -1, -1):
            v[at] = v[at] + dec_f[at, part] * v[at + 1]
        for at in range(1, n_tm):
            v[at] = v[at] + dec_f[at - 1, part] * v[at - 1]
        for at in range(n_tm):
            target[at, part] = v[at]

    def forward(source):
        jumps, outer = [source[0, mid]], []
        for at, ahead in enumerate(model([source[at] for at in range(n_tm - 1)])):
            jump = source[at + 1] - ahead
            jumps.append(jump[rows : 2 * rows])
            outer.append(iev_f[at + 1] * jump)
        return jumps, outer

    def closed(source, jumps, outer, target):
        back = adjoint(outer)
        for at in range(n_tm):
            image = iev_f[at, mid] * jumps[at] + g_f[at] * source[at, mid]
            if at < n_tm - 1:
                image = image - back[at][rows : 2 * rows]
            target[at] = image

    def send_sums(row):
        if direct:
            slot = sums.at[pl.ds(me, 1)]
            slot[...] = row
            for to in range(n_all):
                start(remote(
                    slot, slot, sent.at[S_ANY], come.at[R_ANY], (to // n_sp, to % n_sp)), me != to)
        else:
            slot = sum_tm.at[k, pl.ds(0, 1)]
            slot[...] = row
            for o in range(1, n_tm):
                start(remote(slot, slot, far_send.at[0, o], far_recv.at[0, k], (at_tm(o), s)))

    def wait_sums():
        if direct:
            pl.when(owner)(lambda: await_lines(come.at[R_ANY], n_own - 1))
            pl.when(~owner)(lambda: await_lines(come.at[R_ANY], n_own))
        else:
            for src in range(fields):
                slot = sum_tm.at[src, pl.ds(0, 1)]
                pl.when(k != src)(remote(
                    slot, slot, far_send.at[0, 0], far_recv.at[0, src], (src, s)).wait_recv)
            slot = sums.at[pl.ds(s * 8, 8)]
            slot[...] = jnp.concatenate(
                [sum_tm[at, 0:1] for at in range(fields)] + [jnp.zeros((8 - fields, 128), jnp.float32)], axis=0)
            for o in range(1, n_sp):
                start(remote(slot, slot, far_send.at[1, o], far_recv.at[1, o], (k, at_sp(o))))
            for o in range(1, n_sp):
                slot = sums.at[pl.ds(at_sp(-o) * 8, 8)]
                remote(slot, slot, far_send.at[1, o], far_recv.at[1, o], (k, at_sp(-o))).wait_recv()
        return sums[...]

    reach_of = {DEC: range(n_tm - 1), WIND: range(n_tm - 1), IEV: range(1, n_tm)}

    @pl.when(owner)
    def work():
        for edge, cond in ((0, jnp.logical_not(has_low)), (2 * rows, jnp.logical_not(has_high))):
            @pl.when(cond)
            def _():
                for buffer in (r_f, y_f, iev_f, dec_f):
                    buffer[:, pl.ds(edge, rows)] = jnp.zeros((n_tm, rows, width), jnp.float32)
                wind_f[:, :, pl.ds(edge, rows)] = jnp.zeros((n_tm, 2, rows, width), jnp.float32)
        for edge in (0, 3 * rows - (rows - STEPS)):
            iev_f[:, pl.ds(edge, rows - STEPS)] = jnp.zeros((n_tm, rows - STEPS, width), jnp.float32)
        r_f[k, mid] = r_own[k]
        g_f[k] = g_own[k]
        await_tiles(load_sem.at[1], 4)
        greeted(0)
        for at in (1, 0) + tuple(range(2, n_tm)):
            for kind in (DEC, WIND, IEV):
                if at in reach_of[kind]:
                    take(kind, at)
                    to_sides(kind, held(kind, at), functools.partial(tiles_of[kind], at), k != at)
        from_sides(DEC, n_tm - 1)
        for at in range(n_tm):
            take(RES, at)
            to_mate(at)
        await_tiles(come.at[R_MATE], n_tm)
        await_tiles(come.at[R_BY], n_tm, off_chip)
        greet(1)
        precondition(r_f, z_f, slice(None))
        give_back(Z, lambda at: z_f.at[at, mid])
        rz_part = 0.0
        for at in range(n_tm):
            rz_part = rz_part + folded(r_f[at, mid] * z_f[at, mid])
        from_sides(WIND, 2 * (n_tm - 1))
        for at in range(n_tm - 1):
            x_flow, y_flow = wind_f[at, 0], wind_f[at, 1]
            coef[at, 0] = jnp.where(inside, DIFFUSION - 0.5 * x_flow, 0.0)
            coef[at, 1] = jnp.where(inside, DIFFUSION + 0.5 * x_flow, 0.0)
            coef[at, 2] = jnp.where(to_right, DIFFUSION - 0.5 * y_flow, 0.0)
            coef[at, 3] = jnp.where(to_left, DIFFUSION + 0.5 * y_flow, 0.0)
        from_sides(IEV, n_tm - 1)
        take(IEV, 0)
        await_tiles(come.at[R_DIAG], n_tm - 1)
        jumps, outer = forward(z_f)
        dq_part = 0.0
        for at in range(n_tm):
            z = z_f[at, mid]
            jump_f[at] = jumps[at]
            dq_part = dq_part + folded(iev_f[at, mid] * jumps[at] * jumps[at] + g_f[at] * z * z)
        rz_part, dq_part = (jnp.sum(part, axis=(0, 1), keepdims=True) for part in (rz_part, dq_part))
        guess = jnp.where(dq_part > 0.0, rz_part / jnp.where(dq_part > 0.0, dq_part, 1.0), 0.0)
        closed(z_f, jumps, outer, q_f)
        precondition(q_f, y_f, mid)
        to_sides(NEXT, lambda first, rim: y_f.at[:, pl.ds(rows + first, rim)], lambda part: y_f.at[:, part])
        give_back(Q, lambda at: q_f.at[at])
        give_back(Y, lambda at: y_f.at[at, mid])
        greeted(1)
        greet(2)
        from_sides(NEXT, n_tm)
        jumps, outer = forward(y_f)
        terms = [0.0] * len(POWER)
        for at in range(n_tm):
            z, y, q, jump_z, jump_y = z_f[at, mid], y_f[at, mid], q_f[at], jump_f[at], jumps[at]
            r2, z2, jump2 = r_f[at, mid] - guess * q, z - guess * y, jump_z - guess * jump_y
            here = iev_f[at, mid], g_f[at]
            scaled2, seen2 = here[0] * jump2, here[1] * z2
            scaled_y, seen_y = here[0] * jump_y, here[1] * y
            for i, term in enumerate((
                r2 * z2, -(r2 * y + z2 * q), q * y,
                scaled2 * jump2 + seen2 * z2, -2.0 * (scaled2 * jump_y + seen2 * y), scaled_y * jump_y + seen_y * y,
                2.0 * (scaled2 * jump_z + seen2 * z), -2.0 * (scaled_y * jump_z + seen_y * z),
            )):
                terms[i] = terms[i] + folded(term)
        for at in range(2, len(reach)):
            greeted(at)
            greet(at + 1)
        send_sums(packed(rz_part, dq_part, guess, *terms))
        closed(y_f, jumps, outer, w_f)
        give_back(W, lambda at: w_f.at[at])
        side_lines = ((n_tm - 1) * (3 * rows + STEPS) + n_tm * rows) * width // 128
        await_tiles(sent.at[S_MATE], n_tm)
        pl.when(has_high)(functools.partial(await_lines, sent.at[S_UP], side_lines))
        pl.when(has_low)(functools.partial(await_lines, sent.at[S_DOWN], side_lines))
        await_tiles(sent.at[S_RET], 4 * (n_tm - 1))
        if direct:
            await_lines(sent.at[S_ANY], n_all - 1)
        else:
            slot = sum_tm.at[k, pl.ds(0, 1)]
            for o in range(1, n_tm):
                remote(slot, slot, far_send.at[0, o], far_recv.at[0, k], (at_tm(o), s)).wait_send()

    def back(semaphore, kinds):
        await_tiles(semaphore, kinds * (fields - 1), owner)
        await_tiles(semaphore, kinds * fields, ~owner)

    back(come.at[R_RET], 3)
    table = wait_sums()
    rz, dq = (jnp.sum(table[:, at : at + 1], axis=0, keepdims=True) for at in range(2))
    alpha = rz / dq
    shift = alpha - table[:, 2:3]
    lane = lax.broadcasted_iota(jnp.int32, table.shape, 1)
    scale = jnp.ones(table.shape, jnp.float32)
    for at, power in enumerate(POWER):
        if power:
            scale = jnp.where(lane == at + 3, shift if power == 1 else shift * shift, scale)
    table = jnp.sum(table * scale, axis=0, keepdims=True)
    lane = lax.broadcasted_iota(jnp.int32, (1, 128), 1)

    def group(least, most):
        inside = jnp.logical_and(lane >= 3 + least, lane < 3 + most)
        return jnp.sum(jnp.where(inside, table, 0.0), axis=1, keepdims=True)

    rz2, dd, cross = group(0, 3), group(3, 6), group(6, 8)
    beta = rz2 / rz
    alpha2 = rz2 / (dd + beta * cross + beta * beta * dq)
    first = alpha + alpha2 * (1.0 + beta)
    second = alpha2 * alpha
    back(come.at[R_LAST], 1)
    for f in range(fields):
        out[0, 0, f] = first * ret[Z, f] - second * ret[Y, f]
        out[1, 0, f] = r_own[f] - first * ret[Q, f] + second * ret[W, f]
    for has, kinds in ((has_next, 6), (~has_next, 3)):
        await_tiles(sent.at[S_TM], kinds * (fields - 1), has, owner)
        await_tiles(sent.at[S_TM], kinds * fields, has, ~owner)
    await_tiles(sent.at[S_BY], fields, off_chip)
    if not direct:
        slot = sums.at[pl.ds(s * 8, 8)]
        for o in range(1, n_sp):
            remote(slot, slot, far_send.at[1, o], far_recv.at[1, o], (k, at_sp(o))).wait_send()


def on_device(wind, decay, iev, obs, weight, innov):
    n_tm, n_sp = lax.axis_size("tm"), lax.axis_size("space")
    fields, rows, width = decay.shape[1:]
    n_own = fields * n_sp
    direct = n_tm * n_sp <= DIRECT
    f32 = jnp.float32
    tile = (rows, width)
    tall = (3 * rows, width)
    vmem = pl.BlockSpec(memory_space=pltpu.VMEM)
    both = pl.pallas_call(
        functools.partial(kernel, n_tm, n_sp),
        out_shape=pltpu.VMEM((2,) + decay.shape, f32),
        in_specs=[pl.BlockSpec(memory_space=pltpu.HBM)] * 6,
        out_specs=vmem,
        scratch_shapes=[
            pltpu.VMEM(obs.shape, jnp.int32),
            pltpu.VMEM(weight.shape, f32),
            pltpu.VMEM(innov.shape, f32),
            pltpu.SemaphoreType.DMA((2,)),
            pltpu.VMEM((fields,) + tile, f32),
            pltpu.VMEM((fields,) + tile, f32),
            pltpu.VMEM((n_tm,) + tall, f32),
            pltpu.VMEM((n_tm,) + tall, f32),
            pltpu.VMEM((n_tm,) + tile, f32),
            pltpu.VMEM((n_tm,) + tall, f32),
            pltpu.VMEM((n_tm, 2) + tall, f32),
            pltpu.VMEM((n_tm - 1, 4) + tall, f32),
            pltpu.VMEM((n_tm,) + tall, f32),
            pltpu.VMEM((n_tm,) + tall, f32),
            pltpu.VMEM((n_tm,) + tile, f32),
            pltpu.VMEM((n_tm,) + tile, f32),
            pltpu.VMEM((n_tm,) + tile, f32),
            pltpu.VMEM((4, fields) + tile, f32),
            pltpu.VMEM((n_own if direct else 8 * n_sp, 128), f32),
            pltpu.VMEM((n_tm, 8, 128), f32),
            pltpu.VMEM((rows * width // 128 * max(6 * fields, 5 * n_tm - 4), 128), f32),
            pltpu.SemaphoreType.DMA((7,)),
            pltpu.SemaphoreType.DMA((4, n_tm)),
            pltpu.SemaphoreType.DMA((6 + 2 * 4,)),
            pltpu.SemaphoreType.DMA((1, 1) if direct else (2, max(n_tm, n_sp))),
            pltpu.SemaphoreType.DMA((1, 1) if direct else (2, max(n_tm, n_sp))),
            pltpu.SemaphoreType.REGULAR((3 if n_sp <= 8 else n_sp, 2)),
        ],
        compiler_params=pltpu.CompilerParams(
            collective_id=0, has_side_effects=True, vmem_limit_bytes=62 * 1024 * 1024
        ),
    )(wind, decay, iev, obs, weight, innov)
    return both[0], both[1]


def solution(mesh):
    placed = (
        P(None, "tm", "space", None),
        P("tm", None, "space", None),
        P("tm", None, "space", None),
        P("tm", "space"),
        P("tm", "space"),
        P("tm", "space"),
    )
    return jax.shard_map(
        on_device,
        mesh=mesh,
        in_specs=placed,
        out_specs=(P("tm", None, "space", None), P("tm", None, "space", None)),
        check_vma=False,
    )
```

```python
import functools

import jax
import jax.numpy as jnp
from jax import lax
from jax.experimental import pallas as pl
from jax.experimental.pallas import tpu as pltpu
from jax.sharding import PartitionSpec as P

STEPS = 4
DIFFUSION = 0.15
MESH = pl.DeviceIdType.MESH
CHUNK = 2048
DIRECT = 64
DEC, WIND, IEV, RES, DIAG = range(5)
NEXT = 3
S_TM, S_BY, S_MATE, S_UP, S_DOWN, S_RET, S_ANY = range(7)
R_DIAG, R_BY, R_MATE, R_RET, R_LAST, R_ANY, R_RIM, R_SIDE = 0, 1, 2, 3, 4, 5, 6, 8
Z, Q, Y, W = range(4)


def split(x):
    high = x.astype(jnp.bfloat16)
    return high, (x - high.astype(jnp.float32)).astype(jnp.bfloat16)


POWER = (0, 1, 2, 0, 1, 2, 0, 1)


def folded(x):
    total = x[:, :128]
    for at in range(128, x.shape[1], 128):
        total = total + x[:, at : at + 128]
    return total


def packed(*terms):
    lane = lax.broadcasted_iota(jnp.int32, (1, 128), 1)
    out = jnp.zeros((1, 128), jnp.float32)
    for at, term in enumerate(terms):
        total = term if term.shape == (1, 1) else jnp.sum(term, axis=(0, 1), keepdims=True)
        out = jnp.where(lane == at, total, out)
    return out


def kernel(
    n_tm, n_sp, wind_in, decay_in, iev_in, obs_in, weight_in, innov_in, out,
    obs, weight, innov, load_sem,
    r_own, g_own, dec_f, r_f, g_f, iev_f, wind_f, coef, z_f, y_f, y_rim, coef_rim, jump_f, q_f, w_f, ret,
    sums, sum_tm, size, sent, tm_recv, come, far_send, far_recv, met,
):
    k = lax.axis_index("tm")
    s = lax.axis_index("space")
    fields, rows, width = decay_in.shape[1:]
    n_own = fields * n_sp
    n_all = n_tm * n_sp
    owner = k < fields
    has_next, has_high, has_low = k < n_tm - 1, s < n_sp - 1, s > 0
    me = k * n_sp + s
    direct = n_all <= DIRECT
    mid = pl.ds(rows, rows)

    def at_tm(o):
        return lax.rem(k + o + n_tm, n_tm)

    def at_sp(o):
        return lax.rem(s + o + n_sp, n_sp)

    def place(at):
        return (at // n_sp, lax.rem(at, n_sp))

    def all_of(*conds):
        return functools.reduce(jnp.logical_and, conds)

    loads = [
        pltpu.make_async_copy(src, dst, load_sem.at[0])
        for src, dst in ((obs_in, obs), (innov_in, innov), (weight_in, weight))
    ]
    for load in loads:
        load.start()
    barrier = pltpu.get_barrier_semaphore()

    def hello(semaphore, device):
        pl.semaphore_signal(semaphore, inc=1, device_id=device, device_id_type=MESH)

    @pl.when(owner)
    def _():
        for o in range(1, n_tm):
            hello(barrier, (at_tm(o), s))
        for cond, side in ((has_low, at_sp(-1)), (has_high, at_sp(1))):
            @pl.when(cond)
            def _():
                for o in range(n_tm):
                    hello(barrier, (at_tm(o), side))

    def remote(src, dst, send, recv, device):
        return pltpu.make_async_remote_copy(
            src_ref=src, dst_ref=dst, send_sem=send, recv_sem=recv,
            device_id=device, device_id_type=MESH,
        )

    def start(copy, *conds):
        if conds:
            pl.when(all_of(*conds))(copy.start)
        else:
            copy.start()

    tile_lines = rows * width // 128

    def await_lines(semaphore, count):
        pltpu.make_async_copy(size.at[pl.ds(0, count)], size.at[pl.ds(0, count)], semaphore).wait()

    def await_tiles(semaphore, count, *conds):
        if conds:
            pl.when(all_of(*conds))(lambda: await_lines(semaphore, count * tile_lines))
        else:
            await_lines(semaphore, count * tile_lines)

    tiles_of = (
        lambda at, part: dec_f.at[at, part],
        lambda at, part: wind_f.at[at, :, part],
        lambda at, part: iev_f.at[at, part],
        lambda at, part: r_f.at[at, part],
        lambda at, part: g_f.at[at],
    )
    sources = (
        lambda j: decay_in.at[0, j], lambda j: wind_in.at[:, 0], lambda j: iev_in.at[0, j],
        lambda j: r_own.at[j], lambda j: g_own.at[j],
    )
    last_has = (False, False, True, True, True)

    def came(kind, at):
        return come.at[R_DIAG] if kind == DIAG else tm_recv.at[kind, at]

    def give(kind, *when):
        for j in range(fields):
            conds = (k != j,) + when if last_has[kind] else (k != j, has_next) + when
            start(remote(
                sources[kind](j), tiles_of[kind](k, mid), sent.at[S_TM], came(kind, k), (j, s),
            ), *conds)

    even = lax.rem(s, 2) == 0
    low, upper = pl.ds(0, rows), pl.ds(2 * rows, rows)

    off_chip = jnp.logical_or(all_of(even, has_low), all_of(~even, has_high))

    def give_beside():
        for cond, part, slab in ((all_of(even, has_low), upper, at_sp(-1)), (all_of(~even, has_high), low, at_sp(1))):
            for j in range(fields):
                copy = remote(r_own.at[j], r_f.at[k, part], sent.at[S_BY], come.at[R_BY], (j, slab))
                start(copy, cond)

    def to_mate(at):
        for cond, part, slab in ((even, low, at_sp(1)), (~even, upper, at_sp(-1))):
            start(remote(r_f.at[at, mid], r_f.at[at, part], sent.at[S_MATE], come.at[R_MATE], (k, slab)), cond)

    def take(kind, at):
        dst = tiles_of[kind](at, mid)
        pl.when(k != at)(remote(dst, dst, sent.at[S_TM], came(kind, at), (at, s)).wait_recv)

    needed = {DEC: rows, WIND: rows, IEV: STEPS, NEXT: rows}

    def to_sides(kind, source, target, *conds):
        rim, side = needed[kind], R_SIDE + 2 * kind
        start(remote(
            source(rows - rim, rim), target(pl.ds(rows - rim, rim)), sent.at[S_UP], come.at[side], (k, at_sp(1)),
        ), has_high, *conds)
        start(remote(
            source(0, rim), target(pl.ds(2 * rows, rim)), sent.at[S_DOWN], come.at[side + 1], (k, at_sp(-1)),
        ), has_low, *conds)

    def from_sides(kind, count):
        lines = count * needed[kind] * width // 128
        for side, cond in enumerate((has_low, has_high)):
            pl.when(cond)(functools.partial(await_lines, come.at[R_SIDE + 2 * kind + side], lines))

    def held(kind, at):
        return lambda first, rim: tiles_of[kind](at, pl.ds(rows + first, rim))

    own = {
        DEC: lambda first, rim: decay_in.at[0, k, pl.ds(first, rim)],
        WIND: lambda first, rim: wind_in.at[:, 0, pl.ds(first, rim)],
        IEV: lambda first, rim: iev_in.at[0, k, pl.ds(first, rim)],
    }

    def give_back(kind, source):
        for o in range(1, n_tm):
            start(remote(
                source(at_tm(o)), ret.at[kind, k], sent.at[S_RET], come.at[R_LAST if kind == W else R_RET], (at_tm(o), s),
            ))
        keep = source(k)
        ret[kind, k] = keep[...]

    keeps = [
        pltpu.make_async_copy(sources[kind](k), tiles_of[kind](k, mid), load_sem.at[1])
        for kind in (DEC, WIND, IEV)
    ]

    @pl.when(owner)
    def _():
        for copy in keeps:
            copy.start()

    slabs = 1 + has_low.astype(jnp.int32) + has_high.astype(jnp.int32)
    pl.semaphore_wait(barrier, fields * slabs - owner.astype(jnp.int32))

    reach = [1]
    while 2 * reach[-1] < n_sp - 1:
        reach.append(2 * reach[-1])

    def greet(at):
        if at < len(reach):
            far = reach[at]
            pl.when(s >= far)(lambda: hello(met.at[at, 0], (k, s - far)))
            pl.when(s < n_sp - far)(lambda: hello(met.at[at, 1], (k, s + far)))

    def greeted(at):
        if at < len(reach):
            far = reach[at]
            pl.when(s >= far)(lambda: pl.semaphore_wait(met.at[at, 1], 1))
            pl.when(s < n_sp - far)(lambda: pl.semaphore_wait(met.at[at, 0], 1))

    pl.when(owner)(lambda: greet(0))
    for kind in (DEC, WIND):
        give(kind)
    give(IEV, k > 0)

    @pl.when(owner)
    def _():
        for kind in (DEC, WIND):
            to_sides(kind, own[kind], functools.partial(tiles_of[kind], k))
        to_sides(IEV, own[IEV], functools.partial(tiles_of[IEV], k), k > 0)


    blocks = width // 128
    tiles = fields * blocks * rows
    n_obs = obs.shape[1]
    lefts, rights = [], []
    await_lines(load_sem.at[0], 3 * n_obs // 128)
    for at in range(0, n_obs, CHUNK):
        cell = obs[:, pl.ds(at, CHUNK)]
        field = cell // (rows * width)
        row = lax.rem(cell // width, rows)
        block = lax.rem(cell // 128, blocks)
        tile = (field * blocks + block) * rows + row
        lane = jnp.bitwise_and(cell, 127)
        left = (lax.broadcasted_iota(jnp.int32, (tiles, CHUNK), 0) == tile).astype(jnp.float32)
        lefts.append(left.astype(jnp.bfloat16).reshape(tiles // 16, 16, CHUNK))
        right = (lax.broadcasted_iota(jnp.int32, (128, CHUNK), 0) == lane).astype(jnp.float32)
        rights.append(right.astype(jnp.bfloat16))

    def scattered(values_of, target):
        acc = jnp.zeros((2 * tiles, 128), jnp.float32)
        for at in range(0, n_obs, CHUNK):
            left, right = lefts[at // CHUNK], rights[at // CHUNK]
            parts = [
                (left * piece[None]).reshape(tiles, CHUNK)
                for piece in split(jnp.broadcast_to(values_of(pl.ds(at, CHUNK)), (16, CHUNK)))
            ]
            acc = acc + lax.dot_general(
                jnp.concatenate(parts, axis=0), right, (((1,), (1,)), ((), ())),
                preferred_element_type=jnp.float32,
            )
        x = acc[:tiles] + acc[tiles:]
        for f in range(fields):
            target[f] = jnp.concatenate([x[(f * blocks + b) * rows :][:rows] for b in range(blocks)], axis=1)

    scattered(lambda part: weight[:, part] * innov[:, part], r_own)
    give(RES)
    give_beside()
    give(IEV, k == 0)
    scattered(lambda part: weight[:, part], g_own)
    give(DIAG)

    line = lax.broadcasted_iota(jnp.int32, (3 * rows, width), 0) + (s - 1) * rows
    column = lax.broadcasted_iota(jnp.int32, (3 * rows, width), 1)
    inside = jnp.logical_and(line >= 0, line < n_sp * rows)
    to_right = jnp.logical_and(inside, column < width - 1)
    to_left = jnp.logical_and(inside, column > 0)

    def ring(own_rows, rim):
        return jnp.concatenate([own_rows, rim], axis=0)

    def rim_of(x):
        return jnp.concatenate([x[2 * rows : 2 * rows + STEPS], x[rows - STEPS : rows]], axis=0)

    def tall_by(by, c):
        return coef[by, c]

    def ring_by(by, c):
        return ring(coef[by, c, mid], coef_rim[by, c])

    def model(us, factor):
        last = us[0].shape[0] - 1
        for _ in range(STEPS):
            us = [
                (1.0 - 4.0 * DIFFUSION) * u
                + factor(by, 0) * pltpu.roll(u, last, 0) + factor(by, 1) * pltpu.roll(u, 1, 0)
                + factor(by, 2) * pltpu.roll(u, width - 1, 1) + factor(by, 3) * pltpu.roll(u, 1, 1)
                for by, u in enumerate(us)
            ]
        return us

    def adjoint(vs, factor):
        last = vs[0].shape[0] - 1
        for _ in range(STEPS):
            vs = [
                (1.0 - 4.0 * DIFFUSION) * v
                + pltpu.roll(factor(by, 0) * v, 1, 0) + pltpu.roll(factor(by, 1) * v, last, 0)
                + pltpu.roll(factor(by, 2) * v, 1, 1) + pltpu.roll(factor(by, 3) * v, width - 1, 1)
                for by, v in enumerate(vs)
            ]
        return vs

    def precondition(source, target, part):
        v = [source[at] for at in range(n_tm)]
        for at in range(n_tm - 2, -1, -1):
            v[at] = v[at] + dec_f[at, part] * v[at + 1]
        for at in range(1, n_tm):
            v[at] = v[at] + dec_f[at - 1, part] * v[at - 1]
        for at in range(n_tm):
            target[at, part] = v[at]

    def forward(source):
        jumps, outer = [source[0, mid]], []
        for at, ahead in enumerate(model([source[at] for at in range(n_tm - 1)], tall_by)):
            jump = source[at + 1] - ahead
            jumps.append(jump[rows : 2 * rows])
            weighted = iev_f[at + 1] * jump
            outer.append(ring(weighted[rows : 2 * rows], rim_of(weighted)))
        return jumps, outer

    def closed(source, jumps, outer, target):
        back = adjoint(outer, ring_by)
        for at in range(n_tm):
            image = iev_f[at, mid] * jumps[at] + g_f[at] * source[at, mid]
            if at < n_tm - 1:
                image = image - back[at][:rows]
            target[at] = image

    def send_sums(row):
        if direct:
            slot = sums.at[pl.ds(me, 1)]
            slot[...] = row
            for to in range(n_all):
                start(remote(
                    slot, slot, sent.at[S_ANY], come.at[R_ANY], (to // n_sp, to % n_sp)), me != to)
        else:
            slot = sum_tm.at[k, pl.ds(0, 1)]
            slot[...] = row
            for o in range(1, n_tm):
                start(remote(slot, slot, far_send.at[0, o], far_recv.at[0, k], (at_tm(o), s)))

    def wait_sums():
        if direct:
            pl.when(owner)(lambda: await_lines(come.at[R_ANY], n_own - 1))
            pl.when(~owner)(lambda: await_lines(come.at[R_ANY], n_own))
        else:
            for src in range(fields):
                slot = sum_tm.at[src, pl.ds(0, 1)]
                pl.when(k != src)(remote(
                    slot, slot, far_send.at[0, 0], far_recv.at[0, src], (src, s)).wait_recv)
            slot = sums.at[pl.ds(s * 8, 8)]
            slot[...] = jnp.concatenate(
                [sum_tm[at, 0:1] for at in range(fields)] + [jnp.zeros((8 - fields, 128), jnp.float32)], axis=0)
            for o in range(1, n_sp):
                start(remote(slot, slot, far_send.at[1, o], far_recv.at[1, o], (k, at_sp(o))))
            for o in range(1, n_sp):
                slot = sums.at[pl.ds(at_sp(-o) * 8, 8)]
                remote(slot, slot, far_send.at[1, o], far_recv.at[1, o], (k, at_sp(-o))).wait_recv()
        return sums[...]

    reach_of = {DEC: range(n_tm - 1), WIND: range(n_tm - 1), IEV: range(1, n_tm)}

    @pl.when(owner)
    def work():
        for edge, cond in ((0, jnp.logical_not(has_low)), (2 * rows, jnp.logical_not(has_high))):
            @pl.when(cond)
            def _():
                for buffer in (r_f, y_f, iev_f, dec_f):
                    buffer[:, pl.ds(edge, rows)] = jnp.zeros((n_tm, rows, width), jnp.float32)
                y_rim[:, pl.ds(STEPS if edge == 0 else 0, STEPS)] = jnp.zeros((n_tm - 1, STEPS, width), jnp.float32)
                wind_f[:, :, pl.ds(edge, rows)] = jnp.zeros((n_tm, 2, rows, width), jnp.float32)
        for edge in (0, 3 * rows - (rows - STEPS)):
            iev_f[:, pl.ds(edge, rows - STEPS)] = jnp.zeros((n_tm, rows - STEPS, width), jnp.float32)
        r_f[k, mid] = r_own[k]
        g_f[k] = g_own[k]
        await_tiles(load_sem.at[1], 4)
        greeted(0)
        for at in (1, 0) + tuple(range(2, n_tm)):
            for kind in (DEC, WIND, IEV):
                if at in reach_of[kind]:
                    take(kind, at)
                    to_sides(kind, held(kind, at), functools.partial(tiles_of[kind], at), k != at)
        from_sides(DEC, n_tm - 1)
        for at in range(n_tm):
            take(RES, at)
            to_mate(at)
        await_tiles(come.at[R_MATE], n_tm)
        await_tiles(come.at[R_BY], n_tm, off_chip)
        greet(1)
        precondition(r_f, z_f, slice(None))
        give_back(Z, lambda at: z_f.at[at, mid])
        rz_part = 0.0
        for at in range(n_tm):
            rz_part = rz_part + folded(r_f[at, mid] * z_f[at, mid])
        from_sides(WIND, 2 * (n_tm - 1))
        for at in range(n_tm - 1):
            x_flow, y_flow = wind_f[at, 0], wind_f[at, 1]
            coef[at, 0] = jnp.where(inside, DIFFUSION - 0.5 * x_flow, 0.0)
            coef[at, 1] = jnp.where(inside, DIFFUSION + 0.5 * x_flow, 0.0)
            coef[at, 2] = jnp.where(to_right, DIFFUSION - 0.5 * y_flow, 0.0)
            coef[at, 3] = jnp.where(to_left, DIFFUSION + 0.5 * y_flow, 0.0)
            for c in range(4):
                coef_rim[at, c] = rim_of(coef[at, c])
        from_sides(IEV, n_tm - 1)
        take(IEV, 0)
        await_tiles(come.at[R_DIAG], n_tm - 1)
        jumps, outer = forward(z_f)
        dq_part = 0.0
        for at in range(n_tm):
            z = z_f[at, mid]
            jump_f[at] = jumps[at]
            dq_part = dq_part + folded(iev_f[at, mid] * jumps[at] * jumps[at] + g_f[at] * z * z)
        rz_part, dq_part = (jnp.sum(part, axis=(0, 1), keepdims=True) for part in (rz_part, dq_part))
        guess = jnp.where(dq_part > 0.0, rz_part / jnp.where(dq_part > 0.0, dq_part, 1.0), 0.0)
        closed(z_f, jumps, outer, q_f)
        precondition(q_f, y_f, mid)
        whole_k = pl.ds(0, n_tm - 1)
        start(remote(
            y_f.at[whole_k, pl.ds(2 * rows - STEPS, STEPS)], y_rim.at[:, pl.ds(STEPS, STEPS)],
            sent.at[S_UP], come.at[R_RIM], (k, at_sp(1))), has_high)
        start(remote(
            y_f.at[whole_k, pl.ds(rows, STEPS)], y_rim.at[:, pl.ds(0, STEPS)],
            sent.at[S_DOWN], come.at[R_RIM + 1], (k, at_sp(-1))), has_low)
        to_sides(NEXT, lambda first, rim: y_f.at[:, pl.ds(rows + first, rim)], lambda part: y_f.at[:, part])
        give_back(Q, lambda at: q_f.at[at])
        give_back(Y, lambda at: y_f.at[at, mid])
        greeted(1)
        greet(2)
        terms = [0.0] * len(POWER)
        for at in range(n_tm):
            z, y, q = z_f[at, mid], y_f[at, mid], q_f[at]
            r2, z2 = r_f[at, mid] - guess * q, z - guess * y
            seen2, seen_y = g_f[at] * z2, g_f[at] * y
            for i, term in enumerate((
                r2 * z2, -(r2 * y + z2 * q), q * y,
                seen2 * z2, -2.0 * (seen2 * y), seen_y * y, 2.0 * (seen2 * z), -2.0 * (seen_y * z),
            )):
                terms[i] = terms[i] + folded(term)
        rim_lines = (n_tm - 1) * STEPS * width // 128
        for side, cond in enumerate((has_low, has_high)):
            pl.when(cond)(functools.partial(await_lines, come.at[R_RIM + side], rim_lines))
        ahead = model([ring(y_f[at, mid], y_rim[at]) for at in range(n_tm - 1)], ring_by)
        for at in range(n_tm):
            jump_z = jump_f[at]
            jump_y = y_f[at, mid] - ahead[at - 1][:rows] if at else y_f[at, mid]
            jump2 = jump_z - guess * jump_y
            scaled2, scaled_y = iev_f[at, mid] * jump2, iev_f[at, mid] * jump_y
            for i, term in enumerate((
                scaled2 * jump2, -2.0 * (scaled2 * jump_y), scaled_y * jump_y,
                2.0 * (scaled2 * jump_z), -2.0 * (scaled_y * jump_z),
            )):
                terms[3 + i] = terms[3 + i] + folded(term)
        for at in range(2, len(reach)):
            greeted(at)
            greet(at + 1)
        send_sums(packed(rz_part, dq_part, guess, *terms))
        from_sides(NEXT, n_tm)
        jumps, outer = forward(y_f)
        closed(y_f, jumps, outer, w_f)
        give_back(W, lambda at: w_f.at[at])
        side_lines = ((n_tm - 1) * (3 * rows + 2 * STEPS) + n_tm * rows) * width // 128
        await_tiles(sent.at[S_MATE], n_tm)
        pl.when(has_high)(functools.partial(await_lines, sent.at[S_UP], side_lines))
        pl.when(has_low)(functools.partial(await_lines, sent.at[S_DOWN], side_lines))
        await_tiles(sent.at[S_RET], 4 * (n_tm - 1))
        if direct:
            await_lines(sent.at[S_ANY], n_all - 1)
        else:
            slot = sum_tm.at[k, pl.ds(0, 1)]
            for o in range(1, n_tm):
                remote(slot, slot, far_send.at[0, o], far_recv.at[0, k], (at_tm(o), s)).wait_send()

    def back(semaphore, kinds):
        await_tiles(semaphore, kinds * (fields - 1), owner)
        await_tiles(semaphore, kinds * fields, ~owner)

    back(come.at[R_RET], 3)
    table = wait_sums()
    rz, dq = (jnp.sum(table[:, at : at + 1], axis=0, keepdims=True) for at in range(2))
    alpha = rz / dq
    shift = alpha - table[:, 2:3]
    lane = lax.broadcasted_iota(jnp.int32, table.shape, 1)
    scale = jnp.ones(table.shape, jnp.float32)
    for at, power in enumerate(POWER):
        if power:
            scale = jnp.where(lane == at + 3, shift if power == 1 else shift * shift, scale)
    table = jnp.sum(table * scale, axis=0, keepdims=True)
    lane = lax.broadcasted_iota(jnp.int32, (1, 128), 1)

    def group(least, most):
        inside = jnp.logical_and(lane >= 3 + least, lane < 3 + most)
        return jnp.sum(jnp.where(inside, table, 0.0), axis=1, keepdims=True)

    rz2, dd, cross = group(0, 3), group(3, 6), group(6, 8)
    beta = rz2 / rz
    alpha2 = rz2 / (dd + beta * cross + beta * beta * dq)
    first = alpha + alpha2 * (1.0 + beta)
    second = alpha2 * alpha
    back(come.at[R_LAST], 1)
    for f in range(fields):
        out[0, 0, f] = first * ret[Z, f] - second * ret[Y, f]
        out[1, 0, f] = r_own[f] - first * ret[Q, f] + second * ret[W, f]
    for has, kinds in ((has_next, 6), (~has_next, 3)):
        await_tiles(sent.at[S_TM], kinds * (fields - 1), has, owner)
        await_tiles(sent.at[S_TM], kinds * fields, has, ~owner)
    await_tiles(sent.at[S_BY], fields, off_chip)
    if not direct:
        slot = sums.at[pl.ds(s * 8, 8)]
        for o in range(1, n_sp):
            remote(slot, slot, far_send.at[1, o], far_recv.at[1, o], (k, at_sp(o))).wait_send()


def on_device(wind, decay, iev, obs, weight, innov):
    n_tm, n_sp = lax.axis_size("tm"), lax.axis_size("space")
    fields, rows, width = decay.shape[1:]
    n_own = fields * n_sp
    direct = n_tm * n_sp <= DIRECT
    f32 = jnp.float32
    tile = (rows, width)
    tall = (3 * rows, width)
    vmem = pl.BlockSpec(memory_space=pltpu.VMEM)
    both = pl.pallas_call(
        functools.partial(kernel, n_tm, n_sp),
        out_shape=pltpu.VMEM((2,) + decay.shape, f32),
        in_specs=[pl.BlockSpec(memory_space=pltpu.HBM)] * 6,
        out_specs=vmem,
        scratch_shapes=[
            pltpu.VMEM(obs.shape, jnp.int32),
            pltpu.VMEM(weight.shape, f32),
            pltpu.VMEM(innov.shape, f32),
            pltpu.SemaphoreType.DMA((2,)),
            pltpu.VMEM((fields,) + tile, f32),
            pltpu.VMEM((fields,) + tile, f32),
            pltpu.VMEM((n_tm,) + tall, f32),
            pltpu.VMEM((n_tm,) + tall, f32),
            pltpu.VMEM((n_tm,) + tile, f32),
            pltpu.VMEM((n_tm,) + tall, f32),
            pltpu.VMEM((n_tm, 2) + tall, f32),
            pltpu.VMEM((n_tm - 1, 4) + tall, f32),
            pltpu.VMEM((n_tm,) + tall, f32),
            pltpu.VMEM((n_tm,) + tall, f32),
            pltpu.VMEM((n_tm - 1,) + tile, f32),
            pltpu.VMEM((n_tm - 1, 4) + tile, f32),
            pltpu.VMEM((n_tm,) + tile, f32),
            pltpu.VMEM((n_tm,) + tile, f32),
            pltpu.VMEM((n_tm,) + tile, f32),
            pltpu.VMEM((4, fields) + tile, f32),
            pltpu.VMEM((n_own if direct else 8 * n_sp, 128), f32),
            pltpu.VMEM((n_tm, 8, 128), f32),
            pltpu.VMEM((rows * width // 128 * max(6 * fields, 5 * n_tm), 128), f32),
            pltpu.SemaphoreType.DMA((7,)),
            pltpu.SemaphoreType.DMA((4, n_tm)),
            pltpu.SemaphoreType.DMA((8 + 2 * 4,)),
            pltpu.SemaphoreType.DMA((1, 1) if direct else (2, max(n_tm, n_sp))),
            pltpu.SemaphoreType.DMA((1, 1) if direct else (2, max(n_tm, n_sp))),
            pltpu.SemaphoreType.REGULAR((3 if n_sp <= 8 else n_sp, 2)),
        ],
        compiler_params=pltpu.CompilerParams(
            collective_id=0, has_side_effects=True, vmem_limit_bytes=62 * 1024 * 1024
        ),
    )(wind, decay, iev, obs, weight, innov)
    return both[0], both[1]


def solution(mesh):
    placed = (
        P(None, "tm", "space", None),
        P("tm", None, "space", None),
        P("tm", None, "space", None),
        P("tm", "space"),
        P("tm", "space"),
        P("tm", "space"),
    )
    return jax.shard_map(
        on_device,
        mesh=mesh,
        in_specs=placed,
        out_specs=(P("tm", None, "space", None), P("tm", None, "space", None)),
        check_vma=False,
    )
```

```python
import functools

import jax
import jax.numpy as jnp
from jax import lax
from jax.experimental import pallas as pl
from jax.experimental.pallas import tpu as pltpu
from jax.sharding import PartitionSpec as P

STEPS = 4
DIFFUSION = 0.15
MESH = pl.DeviceIdType.MESH
CHUNK = 2048
DIRECT = 64
DEC, WIND, IEV, RES, DIAG = range(5)
NEXT = 3
S_TM, S_BY, S_MATE, S_UP, S_DOWN, S_RET, S_ANY = range(7)
R_DIAG, R_BY, R_MATE, R_RET, R_LAST, R_ANY, R_RIM, R_SIDE = 0, 1, 2, 3, 4, 5, 6, 8
Z, Q, Y, W = range(4)


def split(x):
    high = x.astype(jnp.bfloat16)
    return high, (x - high.astype(jnp.float32)).astype(jnp.bfloat16)


POWER = (0, 1, 2, 0, 1, 2, 0, 1)


def folded(x):
    total = x[:, :128]
    for at in range(128, x.shape[1], 128):
        total = total + x[:, at : at + 128]
    return total


def packed(*terms):
    lane = lax.broadcasted_iota(jnp.int32, (1, 128), 1)
    out = jnp.zeros((1, 128), jnp.float32)
    for at, term in enumerate(terms):
        total = term if term.shape == (1, 1) else jnp.sum(term, axis=(0, 1), keepdims=True)
        out = jnp.where(lane == at, total, out)
    return out


def kernel(
    n_tm, n_sp, wind_in, decay_in, iev_in, obs_in, weight_in, innov_in, out,
    obs, weight, innov, load_sem,
    r_own, g_own, dec_f, r_f, g_f, iev_f, wind_f, coef, z_f, y_f, y_rim, coef_rim, jump_f, q_f, w_f, ret,
    sums, sum_tm, size, sent, tm_recv, come, far_send, far_recv, met,
):
    k = lax.axis_index("tm")
    s = lax.axis_index("space")
    fields, rows, width = decay_in.shape[1:]
    n_own = fields * n_sp
    n_all = n_tm * n_sp
    owner = k < fields
    has_next, has_high, has_low = k < n_tm - 1, s < n_sp - 1, s > 0
    me = k * n_sp + s
    direct = n_all <= DIRECT
    mid = pl.ds(rows, rows)

    def at_tm(o):
        return lax.rem(k + o + n_tm, n_tm)

    def at_sp(o):
        return lax.rem(s + o + n_sp, n_sp)

    def place(at):
        return (at // n_sp, lax.rem(at, n_sp))

    def all_of(*conds):
        return functools.reduce(jnp.logical_and, conds)

    loads = [
        pltpu.make_async_copy(src, dst, load_sem.at[0])
        for src, dst in ((obs_in, obs), (innov_in, innov), (weight_in, weight))
    ]
    for load in loads:
        load.start()
    barrier = pltpu.get_barrier_semaphore()

    def hello(semaphore, device):
        pl.semaphore_signal(semaphore, inc=1, device_id=device, device_id_type=MESH)

    @pl.when(owner)
    def _():
        for o in range(1, n_tm):
            hello(barrier, (at_tm(o), s))
        for cond, side in ((has_low, at_sp(-1)), (has_high, at_sp(1))):
            @pl.when(cond)
            def _():
                for o in range(n_tm):
                    hello(barrier, (at_tm(o), side))

    def remote(src, dst, send, recv, device):
        return pltpu.make_async_remote_copy(
            src_ref=src, dst_ref=dst, send_sem=send, recv_sem=recv,
            device_id=device, device_id_type=MESH,
        )

    def start(copy, *conds):
        if conds:
            pl.when(all_of(*conds))(copy.start)
        else:
            copy.start()

    tile_lines = rows * width // 128

    def await_lines(semaphore, count):
        pltpu.make_async_copy(size.at[pl.ds(0, count)], size.at[pl.ds(0, count)], semaphore).wait()

    def await_tiles(semaphore, count, *conds):
        if conds:
            pl.when(all_of(*conds))(lambda: await_lines(semaphore, count * tile_lines))
        else:
            await_lines(semaphore, count * tile_lines)

    tiles_of = (
        lambda at, part: dec_f.at[at, part],
        lambda at, part: wind_f.at[at, :, part],
        lambda at, part: iev_f.at[at, part],
        lambda at, part: r_f.at[at, part],
        lambda at, part: g_f.at[at],
    )
    sources = (
        lambda j: decay_in.at[0, j], lambda j: wind_in.at[:, 0], lambda j: iev_in.at[0, j],
        lambda j: r_own.at[j], lambda j: g_own.at[j],
    )
    last_has = (False, False, True, True, True)

    def came(kind, at):
        return come.at[R_DIAG] if kind == DIAG else tm_recv.at[kind, at]

    def give(kind, *when):
        for j in range(fields):
            conds = (k != j,) + when if last_has[kind] else (k != j, has_next) + when
            start(remote(
                sources[kind](j), tiles_of[kind](k, mid), sent.at[S_TM], came(kind, k), (j, s),
            ), *conds)

    even = lax.rem(s, 2) == 0
    low, upper = pl.ds(0, rows), pl.ds(2 * rows, rows)

    off_chip = jnp.logical_or(all_of(even, has_low), all_of(~even, has_high))

    def give_beside():
        for cond, part, slab in ((all_of(even, has_low), upper, at_sp(-1)), (all_of(~even, has_high), low, at_sp(1))):
            for j in range(fields):
                copy = remote(r_own.at[j], r_f.at[k, part], sent.at[S_BY], come.at[R_BY], (j, slab))
                start(copy, cond)

    def to_mate(at):
        for cond, part, slab in ((even, low, at_sp(1)), (~even, upper, at_sp(-1))):
            start(remote(r_f.at[at, mid], r_f.at[at, part], sent.at[S_MATE], come.at[R_MATE], (k, slab)), cond)

    def take(kind, at):
        dst = tiles_of[kind](at, mid)
        pl.when(k != at)(remote(dst, dst, sent.at[S_TM], came(kind, at), (at, s)).wait_recv)

    needed = {DEC: rows, WIND: rows, IEV: STEPS, NEXT: rows}

    def to_sides(kind, source, target, *conds):
        rim, side = needed[kind], R_SIDE + 2 * kind
        start(remote(
            source(rows - rim, rim), target(pl.ds(rows - rim, rim)), sent.at[S_UP], come.at[side], (k, at_sp(1)),
        ), has_high, *conds)
        start(remote(
            source(0, rim), target(pl.ds(2 * rows, rim)), sent.at[S_DOWN], come.at[side + 1], (k, at_sp(-1)),
        ), has_low, *conds)

    def from_sides(kind, count):
        lines = count * needed[kind] * width // 128
        for side, cond in enumerate((has_low, has_high)):
            pl.when(cond)(functools.partial(await_lines, come.at[R_SIDE + 2 * kind + side], lines))

    def held(kind, at):
        return lambda first, rim: tiles_of[kind](at, pl.ds(rows + first, rim))

    own = {
        DEC: lambda first, rim: decay_in.at[0, k, pl.ds(first, rim)],
        WIND: lambda first, rim: wind_in.at[:, 0, pl.ds(first, rim)],
        IEV: lambda first, rim: iev_in.at[0, k, pl.ds(first, rim)],
    }

    def give_back(kind, source):
        for o in range(1, n_tm):
            start(remote(
                source(at_tm(o)), ret.at[kind, k], sent.at[S_RET], come.at[R_LAST if kind == W else R_RET], (at_tm(o), s),
            ))
        keep = source(k)
        ret[kind, k] = keep[...]

    keeps = [
        pltpu.make_async_copy(sources[kind](k), tiles_of[kind](k, mid), load_sem.at[1])
        for kind in (DEC, WIND, IEV)
    ]

    @pl.when(owner)
    def _():
        for copy in keeps:
            copy.start()

    slabs = 1 + has_low.astype(jnp.int32) + has_high.astype(jnp.int32)
    pl.semaphore_wait(barrier, fields * slabs - owner.astype(jnp.int32))

    reach = [1]
    while 2 * reach[-1] < n_sp - 1:
        reach.append(2 * reach[-1])

    def greet(at):
        if at < len(reach):
            far = reach[at]
            pl.when(s >= far)(lambda: hello(met.at[at, 0], (k, s - far)))
            pl.when(s < n_sp - far)(lambda: hello(met.at[at, 1], (k, s + far)))

    def greeted(at):
        if at < len(reach):
            far = reach[at]
            pl.when(s >= far)(lambda: pl.semaphore_wait(met.at[at, 1], 1))
            pl.when(s < n_sp - far)(lambda: pl.semaphore_wait(met.at[at, 0], 1))

    pl.when(owner)(lambda: greet(0))
    for kind in (DEC, WIND):
        give(kind)
    give(IEV, k > 0)

    @pl.when(owner)
    def _():
        for kind in (DEC, WIND):
            to_sides(kind, own[kind], functools.partial(tiles_of[kind], k))
        to_sides(IEV, own[IEV], functools.partial(tiles_of[IEV], k), k > 0)


    blocks = width // 128
    tiles = fields * blocks * rows
    n_obs = obs.shape[1]
    lefts, rights = [], []
    await_lines(load_sem.at[0], 3 * n_obs // 128)
    for at in range(0, n_obs, CHUNK):
        cell = obs[:, pl.ds(at, CHUNK)]
        field = cell // (rows * width)
        row = lax.rem(cell // width, rows)
        block = lax.rem(cell // 128, blocks)
        tile = (field * blocks + block) * rows + row
        lane = jnp.bitwise_and(cell, 127)
        left = (lax.broadcasted_iota(jnp.int32, (tiles, CHUNK), 0) == tile).astype(jnp.float32)
        lefts.append(left.astype(jnp.bfloat16).reshape(tiles // 16, 16, CHUNK))
        right = (lax.broadcasted_iota(jnp.int32, (128, CHUNK), 0) == lane).astype(jnp.float32)
        rights.append(right.astype(jnp.bfloat16))

    def scattered(values_of, target):
        acc = jnp.zeros((2 * tiles, 128), jnp.float32)
        for at in range(0, n_obs, CHUNK):
            left, right = lefts[at // CHUNK], rights[at // CHUNK]
            parts = [
                (left * piece[None]).reshape(tiles, CHUNK)
                for piece in split(jnp.broadcast_to(values_of(pl.ds(at, CHUNK)), (16, CHUNK)))
            ]
            acc = acc + lax.dot_general(
                jnp.concatenate(parts, axis=0), right, (((1,), (1,)), ((), ())),
                preferred_element_type=jnp.float32,
            )
        x = acc[:tiles] + acc[tiles:]
        for f in range(fields):
            target[f] = jnp.concatenate([x[(f * blocks + b) * rows :][:rows] for b in range(blocks)], axis=1)

    scattered(lambda part: weight[:, part] * innov[:, part], r_own)
    give(RES)
    give_beside()
    give(IEV, k == 0)
    scattered(lambda part: weight[:, part], g_own)
    give(DIAG)

    line = lax.broadcasted_iota(jnp.int32, (3 * rows, width), 0) + (s - 1) * rows
    column = lax.broadcasted_iota(jnp.int32, (3 * rows, width), 1)
    inside = jnp.logical_and(line >= 0, line < n_sp * rows)
    to_right = jnp.logical_and(inside, column < width - 1)
    to_left = jnp.logical_and(inside, column > 0)

    def ring(own_rows, rim):
        return jnp.concatenate([own_rows, rim], axis=0)

    def rim_of(x):
        return jnp.concatenate([x[2 * rows : 2 * rows + STEPS], x[rows - STEPS : rows]], axis=0)

    def tall_by(by, c):
        return coef[by, c]

    def ring_by(by, c):
        return ring(coef[by, c, mid], coef_rim[by, c])

    def model(us, factor):
        last = us[0].shape[0] - 1
        for _ in range(STEPS):
            us = [
                (1.0 - 4.0 * DIFFUSION) * u
                + factor(by, 0) * pltpu.roll(u, last, 0) + factor(by, 1) * pltpu.roll(u, 1, 0)
                + factor(by, 2) * pltpu.roll(u, width - 1, 1) + factor(by, 3) * pltpu.roll(u, 1, 1)
                for by, u in enumerate(us)
            ]
        return us

    def adjoint(vs, factor):
        last = vs[0].shape[0] - 1
        for _ in range(STEPS):
            vs = [
                (1.0 - 4.0 * DIFFUSION) * v
                + pltpu.roll(factor(by, 0) * v, 1, 0) + pltpu.roll(factor(by, 1) * v, last, 0)
                + pltpu.roll(factor(by, 2) * v, 1, 1) + pltpu.roll(factor(by, 3) * v, width - 1, 1)
                for by, v in enumerate(vs)
            ]
        return vs

    def precondition(source, target, part):
        v = [source[at] for at in range(n_tm)]
        for at in range(n_tm - 2, -1, -1):
            v[at] = v[at] + dec_f[at, part] * v[at + 1]
        for at in range(1, n_tm):
            v[at] = v[at] + dec_f[at - 1, part] * v[at - 1]
        for at in range(n_tm):
            target[at, part] = v[at]

    def forward(source, pause=None):
        jumps, outer = [source[0, mid]], []
        reached = model([source[at] for at in range(n_tm - 1)], tall_by)
        if pause is not None:
            pause()
        for at, ahead in enumerate(reached):
            jump = source[at + 1] - ahead
            jumps.append(jump[rows : 2 * rows])
            weighted = iev_f[at + 1] * jump
            outer.append(ring(weighted[rows : 2 * rows], rim_of(weighted)))
        return jumps, outer

    def closed(source, jumps, outer, target):
        back = adjoint(outer, ring_by)
        for at in range(n_tm):
            image = iev_f[at, mid] * jumps[at] + g_f[at] * source[at, mid]
            if at < n_tm - 1:
                image = image - back[at][:rows]
            target[at] = image

    def send_sums(row):
        if direct:
            slot = sums.at[pl.ds(me, 1)]
            slot[...] = row
            for to in range(n_all):
                start(remote(
                    slot, slot, sent.at[S_ANY], come.at[R_ANY], (to // n_sp, to % n_sp)), me != to)
        else:
            slot = sum_tm.at[k, pl.ds(0, 1)]
            slot[...] = row
            for o in range(1, n_tm):
                start(remote(slot, slot, far_send.at[0, o], far_recv.at[0, k], (at_tm(o), s)))

    def wait_sums():
        if direct:
            pl.when(owner)(lambda: await_lines(come.at[R_ANY], n_own - 1))
            pl.when(~owner)(lambda: await_lines(come.at[R_ANY], n_own))
        else:
            for src in range(fields):
                slot = sum_tm.at[src, pl.ds(0, 1)]
                pl.when(k != src)(remote(
                    slot, slot, far_send.at[0, 0], far_recv.at[0, src], (src, s)).wait_recv)
            slot = sums.at[pl.ds(s * 8, 8)]
            slot[...] = jnp.concatenate(
                [sum_tm[at, 0:1] for at in range(fields)] + [jnp.zeros((8 - fields, 128), jnp.float32)], axis=0)
            for o in range(1, n_sp):
                start(remote(slot, slot, far_send.at[1, o], far_recv.at[1, o], (k, at_sp(o))))
            for o in range(1, n_sp):
                slot = sums.at[pl.ds(at_sp(-o) * 8, 8)]
                remote(slot, slot, far_send.at[1, o], far_recv.at[1, o], (k, at_sp(-o))).wait_recv()
        return sums[...]

    reach_of = {DEC: range(n_tm - 1), WIND: range(n_tm - 1), IEV: range(1, n_tm)}

    @pl.when(owner)
    def work():
        for edge, cond in ((0, jnp.logical_not(has_low)), (2 * rows, jnp.logical_not(has_high))):
            @pl.when(cond)
            def _():
                for buffer in (r_f, y_f, iev_f, dec_f):
                    buffer[:, pl.ds(edge, rows)] = jnp.zeros((n_tm, rows, width), jnp.float32)
                y_rim[:, pl.ds(STEPS if edge == 0 else 0, STEPS)] = jnp.zeros((n_tm - 1, STEPS, width), jnp.float32)
                wind_f[:, :, pl.ds(edge, rows)] = jnp.zeros((n_tm, 2, rows, width), jnp.float32)
        for edge in (0, 3 * rows - (rows - STEPS)):
            iev_f[:, pl.ds(edge, rows - STEPS)] = jnp.zeros((n_tm, rows - STEPS, width), jnp.float32)
        r_f[k, mid] = r_own[k]
        g_f[k] = g_own[k]
        await_tiles(load_sem.at[1], 4)
        greeted(0)
        for at in (1, 0) + tuple(range(2, n_tm)):
            for kind in (DEC, WIND, IEV):
                if at in reach_of[kind]:
                    take(kind, at)
                    to_sides(kind, held(kind, at), functools.partial(tiles_of[kind], at), k != at)
        for at in range(n_tm):
            take(RES, at)
            to_mate(at)
        from_sides(WIND, 2 * (n_tm - 1))
        for at in range(n_tm - 1):
            x_flow, y_flow = wind_f[at, 0], wind_f[at, 1]
            coef[at, 0] = jnp.where(inside, DIFFUSION - 0.5 * x_flow, 0.0)
            coef[at, 1] = jnp.where(inside, DIFFUSION + 0.5 * x_flow, 0.0)
            coef[at, 2] = jnp.where(to_right, DIFFUSION - 0.5 * y_flow, 0.0)
            coef[at, 3] = jnp.where(to_left, DIFFUSION + 0.5 * y_flow, 0.0)
            for c in range(4):
                coef_rim[at, c] = rim_of(coef[at, c])
        from_sides(DEC, n_tm - 1)
        await_tiles(come.at[R_MATE], n_tm)
        await_tiles(come.at[R_BY], n_tm, off_chip)
        greet(1)
        precondition(r_f, z_f, slice(None))

        def weights():
            from_sides(IEV, n_tm - 1)
            take(IEV, 0)
            await_tiles(come.at[R_DIAG], n_tm - 1)

        jumps, outer = forward(z_f, weights)
        closed(z_f, jumps, outer, q_f)
        precondition(q_f, y_f, mid)
        whole_k = pl.ds(0, n_tm - 1)
        start(remote(
            y_f.at[whole_k, pl.ds(2 * rows - STEPS, STEPS)], y_rim.at[:, pl.ds(STEPS, STEPS)],
            sent.at[S_UP], come.at[R_RIM], (k, at_sp(1))), has_high)
        start(remote(
            y_f.at[whole_k, pl.ds(rows, STEPS)], y_rim.at[:, pl.ds(0, STEPS)],
            sent.at[S_DOWN], come.at[R_RIM + 1], (k, at_sp(-1))), has_low)
        to_sides(NEXT, lambda first, rim: y_f.at[:, pl.ds(rows + first, rim)], lambda part: y_f.at[:, part])
        rz_part = dq_part = 0.0
        for at in range(n_tm):
            z = z_f[at, mid]
            jump_f[at] = jumps[at]
            rz_part = rz_part + folded(r_f[at, mid] * z)
            dq_part = dq_part + folded(iev_f[at, mid] * jumps[at] * jumps[at] + g_f[at] * z * z)
        rz_part, dq_part = (jnp.sum(part, axis=(0, 1), keepdims=True) for part in (rz_part, dq_part))
        guess = jnp.where(dq_part > 0.0, rz_part / jnp.where(dq_part > 0.0, dq_part, 1.0), 0.0)
        give_back(Z, lambda at: z_f.at[at, mid])
        give_back(Q, lambda at: q_f.at[at])
        give_back(Y, lambda at: y_f.at[at, mid])
        greeted(1)
        greet(2)
        terms = [0.0] * len(POWER)
        for at in range(n_tm):
            z, y, q = z_f[at, mid], y_f[at, mid], q_f[at]
            r2, z2 = r_f[at, mid] - guess * q, z - guess * y
            seen2, seen_y = g_f[at] * z2, g_f[at] * y
            for i, term in enumerate((
                r2 * z2, -(r2 * y + z2 * q), q * y,
                seen2 * z2, -2.0 * (seen2 * y), seen_y * y, 2.0 * (seen2 * z), -2.0 * (seen_y * z),
            )):
                terms[i] = terms[i] + folded(term)
        terms[:3] = [jnp.sum(term, axis=(0, 1), keepdims=True) for term in terms[:3]]
        rim_lines = (n_tm - 1) * STEPS * width // 128
        for side, cond in enumerate((has_low, has_high)):
            pl.when(cond)(functools.partial(await_lines, come.at[R_RIM + side], rim_lines))
        ahead = model([ring(y_f[at, mid], y_rim[at]) for at in range(n_tm - 1)], ring_by)
        for at in range(n_tm):
            jump_z = jump_f[at]
            jump_y = y_f[at, mid] - ahead[at - 1][:rows] if at else y_f[at, mid]
            jump2 = jump_z - guess * jump_y
            scaled2, scaled_y = iev_f[at, mid] * jump2, iev_f[at, mid] * jump_y
            for i, term in enumerate((
                scaled2 * jump2, -2.0 * (scaled2 * jump_y), scaled_y * jump_y,
                2.0 * (scaled2 * jump_z), -2.0 * (scaled_y * jump_z),
            )):
                terms[3 + i] = terms[3 + i] + folded(term)
        for at in range(2, len(reach)):
            greeted(at)
            greet(at + 1)
        send_sums(packed(rz_part, dq_part, guess, *terms))
        from_sides(NEXT, n_tm)
        jumps, outer = forward(y_f)
        closed(y_f, jumps, outer, w_f)
        give_back(W, lambda at: w_f.at[at])
        side_lines = ((n_tm - 1) * (3 * rows + 2 * STEPS) + n_tm * rows) * width // 128
        await_tiles(sent.at[S_MATE], n_tm)
        pl.when(has_high)(functools.partial(await_lines, sent.at[S_UP], side_lines))
        pl.when(has_low)(functools.partial(await_lines, sent.at[S_DOWN], side_lines))
        await_tiles(sent.at[S_RET], 4 * (n_tm - 1))
        if direct:
            await_lines(sent.at[S_ANY], n_all - 1)
        else:
            slot = sum_tm.at[k, pl.ds(0, 1)]
            for o in range(1, n_tm):
                remote(slot, slot, far_send.at[0, o], far_recv.at[0, k], (at_tm(o), s)).wait_send()

    def back(semaphore, kinds):
        await_tiles(semaphore, kinds * (fields - 1), owner)
        await_tiles(semaphore, kinds * fields, ~owner)

    back(come.at[R_RET], 3)
    table = wait_sums()
    rz, dq = (jnp.sum(table[:, at : at + 1], axis=0, keepdims=True) for at in range(2))
    alpha = rz / dq
    shift = alpha - table[:, 2:3]
    lane = lax.broadcasted_iota(jnp.int32, table.shape, 1)
    scale = jnp.ones(table.shape, jnp.float32)
    for at, power in enumerate(POWER):
        if power:
            scale = jnp.where(lane == at + 3, shift if power == 1 else shift * shift, scale)
    table = jnp.sum(table * scale, axis=0, keepdims=True)
    lane = lax.broadcasted_iota(jnp.int32, (1, 128), 1)

    def group(least, most):
        inside = jnp.logical_and(lane >= 3 + least, lane < 3 + most)
        return jnp.sum(jnp.where(inside, table, 0.0), axis=1, keepdims=True)

    rz2, dd, cross = group(0, 3), group(3, 6), group(6, 8)
    beta = rz2 / rz
    alpha2 = rz2 / (dd + beta * cross + beta * beta * dq)
    first = alpha + alpha2 * (1.0 + beta)
    second = alpha2 * alpha
    back(come.at[R_LAST], 1)
    for f in range(fields):
        out[0, 0, f] = first * ret[Z, f] - second * ret[Y, f]
        out[1, 0, f] = r_own[f] - first * ret[Q, f] + second * ret[W, f]
    for has, kinds in ((has_next, 6), (~has_next, 3)):
        await_tiles(sent.at[S_TM], kinds * (fields - 1), has, owner)
        await_tiles(sent.at[S_TM], kinds * fields, has, ~owner)
    await_tiles(sent.at[S_BY], fields, off_chip)
    if not direct:
        slot = sums.at[pl.ds(s * 8, 8)]
        for o in range(1, n_sp):
            remote(slot, slot, far_send.at[1, o], far_recv.at[1, o], (k, at_sp(o))).wait_send()


def on_device(wind, decay, iev, obs, weight, innov):
    n_tm, n_sp = lax.axis_size("tm"), lax.axis_size("space")
    fields, rows, width = decay.shape[1:]
    n_own = fields * n_sp
    direct = n_tm * n_sp <= DIRECT
    f32 = jnp.float32
    tile = (rows, width)
    tall = (3 * rows, width)
    vmem = pl.BlockSpec(memory_space=pltpu.VMEM)
    both = pl.pallas_call(
        functools.partial(kernel, n_tm, n_sp),
        out_shape=pltpu.VMEM((2,) + decay.shape, f32),
        in_specs=[pl.BlockSpec(memory_space=pltpu.HBM)] * 6,
        out_specs=vmem,
        scratch_shapes=[
            pltpu.VMEM(obs.shape, jnp.int32),
            pltpu.VMEM(weight.shape, f32),
            pltpu.VMEM(innov.shape, f32),
            pltpu.SemaphoreType.DMA((2,)),
            pltpu.VMEM((fields,) + tile, f32),
            pltpu.VMEM((fields,) + tile, f32),
            pltpu.VMEM((n_tm,) + tall, f32),
            pltpu.VMEM((n_tm,) + tall, f32),
            pltpu.VMEM((n_tm,) + tile, f32),
            pltpu.VMEM((n_tm,) + tall, f32),
            pltpu.VMEM((n_tm, 2) + tall, f32),
            pltpu.VMEM((n_tm - 1, 4) + tall, f32),
            pltpu.VMEM((n_tm,) + tall, f32),
            pltpu.VMEM((n_tm,) + tall, f32),
            pltpu.VMEM((n_tm - 1,) + tile, f32),
            pltpu.VMEM((n_tm - 1, 4) + tile, f32),
            pltpu.VMEM((n_tm,) + tile, f32),
            pltpu.VMEM((n_tm,) + tile, f32),
            pltpu.VMEM((n_tm,) + tile, f32),
            pltpu.VMEM((4, fields) + tile, f32),
            pltpu.VMEM((n_own if direct else 8 * n_sp, 128), f32),
            pltpu.VMEM((n_tm, 8, 128), f32),
            pltpu.VMEM((rows * width // 128 * max(6 * fields, 5 * n_tm), 128), f32),
            pltpu.SemaphoreType.DMA((7,)),
            pltpu.SemaphoreType.DMA((4, n_tm)),
            pltpu.SemaphoreType.DMA((8 + 2 * 4,)),
            pltpu.SemaphoreType.DMA((1, 1) if direct else (2, max(n_tm, n_sp))),
            pltpu.SemaphoreType.DMA((1, 1) if direct else (2, max(n_tm, n_sp))),
            pltpu.SemaphoreType.REGULAR((3 if n_sp <= 8 else n_sp, 2)),
        ],
        compiler_params=pltpu.CompilerParams(
            collective_id=0, has_side_effects=True, vmem_limit_bytes=62 * 1024 * 1024
        ),
    )(wind, decay, iev, obs, weight, innov)
    return both[0], both[1]


def solution(mesh):
    placed = (
        P(None, "tm", "space", None),
        P("tm", None, "space", None),
        P("tm", None, "space", None),
        P("tm", "space"),
        P("tm", "space"),
        P("tm", "space"),
    )
    return jax.shard_map(
        on_device,
        mesh=mesh,
        in_specs=placed,
        out_specs=(P("tm", None, "space", None), P("tm", None, "space", None)),
        check_vma=False,
    )
```

```python
import functools

import jax
import jax.numpy as jnp
from jax import lax
from jax.experimental import pallas as pl
from jax.experimental.pallas import tpu as pltpu
from jax.sharding import PartitionSpec as P

STEPS = 4
DIFFUSION = 0.15
MESH = pl.DeviceIdType.MESH
CHUNK = 2048
DIRECT = 64
DEC, WIND, IEV, RES, DIAG = range(5)
NEXT = 3
S_TM, S_BY, S_MATE, S_UP, S_DOWN, S_RET, S_ANY = range(7)
R_DIAG, R_BY, R_MATE, R_RET, R_LAST, R_ANY, R_RIM, R_SIDE = 0, 1, 2, 3, 4, 5, 6, 8
Z, Q, Y, W = range(4)


def split(x):
    high = x.astype(jnp.bfloat16)
    return high, (x - high.astype(jnp.float32)).astype(jnp.bfloat16)


POWER = (0, 1, 2, 0, 1, 2, 0, 1)


def folded(x):
    total = x[:, :128]
    for at in range(128, x.shape[1], 128):
        total = total + x[:, at : at + 128]
    return total


def packed(*terms):
    lane = lax.broadcasted_iota(jnp.int32, (1, 128), 1)
    out = jnp.zeros((1, 128), jnp.float32)
    for at, term in enumerate(terms):
        total = term if term.shape == (1, 1) else jnp.sum(term, axis=(0, 1), keepdims=True)
        out = jnp.where(lane == at, total, out)
    return out


def kernel(
    n_tm, n_sp, wind_in, decay_in, iev_in, obs_in, weight_in, innov_in, out,
    obs, weight, innov, load_sem,
    r_own, g_own, dec_f, r_f, g_f, iev_f, wind_f, coef, z_f, y_f, y_rim, coef_rim, jump_f, q_f, w_f, ret,
    sums, sum_tm, size, sent, tm_recv, come, far_send, far_recv, met,
):
    k = lax.axis_index("tm")
    s = lax.axis_index("space")
    fields, rows, width = decay_in.shape[1:]
    n_own = fields * n_sp
    n_all = n_tm * n_sp
    owner = k < fields
    has_next, has_high, has_low = k < n_tm - 1, s < n_sp - 1, s > 0
    me = k * n_sp + s
    direct = n_all <= DIRECT
    mid = pl.ds(rows, rows)

    def at_tm(o):
        return lax.rem(k + o + n_tm, n_tm)

    def at_sp(o):
        return lax.rem(s + o + n_sp, n_sp)

    def place(at):
        return (at // n_sp, lax.rem(at, n_sp))

    def all_of(*conds):
        return functools.reduce(jnp.logical_and, conds)

    loads = [
        pltpu.make_async_copy(src, dst, load_sem.at[0])
        for src, dst in ((obs_in, obs), (innov_in, innov), (weight_in, weight))
    ]
    for load in loads:
        load.start()
    barrier = pltpu.get_barrier_semaphore()

    def hello(semaphore, device):
        pl.semaphore_signal(semaphore, inc=1, device_id=device, device_id_type=MESH)

    @pl.when(owner)
    def _():
        for o in range(1, n_tm):
            hello(barrier, (at_tm(o), s))
        for cond, side in ((has_low, at_sp(-1)), (has_high, at_sp(1))):
            @pl.when(cond)
            def _():
                for o in range(n_tm):
                    hello(barrier, (at_tm(o), side))

    def remote(src, dst, send, recv, device):
        return pltpu.make_async_remote_copy(
            src_ref=src, dst_ref=dst, send_sem=send, recv_sem=recv,
            device_id=device, device_id_type=MESH,
        )

    def start(copy, *conds):
        if conds:
            pl.when(all_of(*conds))(copy.start)
        else:
            copy.start()

    tile_lines = rows * width // 128

    def await_lines(semaphore, count):
        pltpu.make_async_copy(size.at[pl.ds(0, count)], size.at[pl.ds(0, count)], semaphore).wait()

    def await_tiles(semaphore, count, *conds):
        if conds:
            pl.when(all_of(*conds))(lambda: await_lines(semaphore, count * tile_lines))
        else:
            await_lines(semaphore, count * tile_lines)

    tiles_of = (
        lambda at, part: dec_f.at[at, part],
        lambda at, part: wind_f.at[at, :, part],
        lambda at, part: iev_f.at[at, part],
        lambda at, part: r_f.at[at, part],
        lambda at, part: g_f.at[at],
    )
    sources = (
        lambda j: decay_in.at[0, j], lambda j: wind_in.at[:, 0], lambda j: iev_in.at[0, j],
        lambda j: r_own.at[j], lambda j: g_own.at[j],
    )
    last_has = (False, False, True, True, True)

    def came(kind, at):
        return come.at[R_DIAG] if kind == DIAG else tm_recv.at[kind, at]

    def give(kind, *when):
        for j in range(fields):
            conds = (k != j,) + when if last_has[kind] else (k != j, has_next) + when
            start(remote(
                sources[kind](j), tiles_of[kind](k, mid), sent.at[S_TM], came(kind, k), (j, s),
            ), *conds)

    even = lax.rem(s, 2) == 0
    low, upper = pl.ds(0, rows), pl.ds(2 * rows, rows)

    off_chip = jnp.logical_or(all_of(even, has_low), all_of(~even, has_high))

    def give_beside():
        for cond, part, slab in ((all_of(even, has_low), upper, at_sp(-1)), (all_of(~even, has_high), low, at_sp(1))):
            for j in range(fields):
                copy = remote(r_own.at[j], r_f.at[k, part], sent.at[S_BY], come.at[R_BY], (j, slab))
                start(copy, cond)

    def to_mate(at):
        for cond, part, slab in ((even, low, at_sp(1)), (~even, upper, at_sp(-1))):
            start(remote(r_f.at[at, mid], r_f.at[at, part], sent.at[S_MATE], come.at[R_MATE], (k, slab)), cond)

    def take(kind, at):
        dst = tiles_of[kind](at, mid)
        pl.when(k != at)(remote(dst, dst, sent.at[S_TM], came(kind, at), (at, s)).wait_recv)

    needed = {DEC: rows, WIND: rows, IEV: STEPS, NEXT: rows}

    def to_sides(kind, source, target, *conds):
        rim, side = needed[kind], R_SIDE + 2 * kind
        start(remote(
            source(rows - rim, rim), target(pl.ds(rows - rim, rim)), sent.at[S_UP], come.at[side], (k, at_sp(1)),
        ), has_high, *conds)
        start(remote(
            source(0, rim), target(pl.ds(2 * rows, rim)), sent.at[S_DOWN], come.at[side + 1], (k, at_sp(-1)),
        ), has_low, *conds)

    def from_sides(kind, count):
        lines = count * needed[kind] * width // 128
        for side, cond in enumerate((has_low, has_high)):
            pl.when(cond)(functools.partial(await_lines, come.at[R_SIDE + 2 * kind + side], lines))

    def held(kind, at):
        return lambda first, rim: tiles_of[kind](at, pl.ds(rows + first, rim))

    own = {
        DEC: lambda first, rim: decay_in.at[0, k, pl.ds(first, rim)],
        WIND: lambda first, rim: wind_in.at[:, 0, pl.ds(first, rim)],
        IEV: lambda first, rim: iev_in.at[0, k, pl.ds(first, rim)],
    }

    def give_back(kind, source):
        for o in range(1, n_tm):
            start(remote(
                source(at_tm(o)), ret.at[kind, k], sent.at[S_RET], come.at[R_LAST if kind == W else R_RET], (at_tm(o), s),
            ))
        keep = source(k)
        ret[kind, k] = keep[...]

    keeps = [
        pltpu.make_async_copy(sources[kind](k), tiles_of[kind](k, mid), load_sem.at[1])
        for kind in (DEC, WIND, IEV)
    ]

    @pl.when(owner)
    def _():
        for copy in keeps:
            copy.start()

    slabs = 1 + has_low.astype(jnp.int32) + has_high.astype(jnp.int32)
    pl.semaphore_wait(barrier, fields * slabs - owner.astype(jnp.int32))

    reach = [1]
    while 2 * reach[-1] < n_sp - 1:
        reach.append(2 * reach[-1])

    def greet(at):
        if at < len(reach):
            far = reach[at]
            pl.when(s >= far)(lambda: hello(met.at[at, 0], (k, s - far)))
            pl.when(s < n_sp - far)(lambda: hello(met.at[at, 1], (k, s + far)))

    def greeted(at):
        if at < len(reach):
            far = reach[at]
            pl.when(s >= far)(lambda: pl.semaphore_wait(met.at[at, 1], 1))
            pl.when(s < n_sp - far)(lambda: pl.semaphore_wait(met.at[at, 0], 1))

    pl.when(owner)(lambda: greet(0))
    for kind in (DEC, WIND):
        give(kind)
    give(IEV, k > 0)

    @pl.when(owner)
    def _():
        for kind in (DEC, WIND):
            to_sides(kind, own[kind], functools.partial(tiles_of[kind], k))
        to_sides(IEV, own[IEV], functools.partial(tiles_of[IEV], k), k > 0)


    blocks = width // 128
    tiles = fields * blocks * rows
    n_obs = obs.shape[1]
    lefts, rights = [], []
    await_lines(load_sem.at[0], 3 * n_obs // 128)
    for at in range(0, n_obs, CHUNK):
        cell = obs[:, pl.ds(at, CHUNK)]
        field = cell // (rows * width)
        row = lax.rem(cell // width, rows)
        block = lax.rem(cell // 128, blocks)
        tile = (field * blocks + block) * rows + row
        lane = jnp.bitwise_and(cell, 127)
        left = (lax.broadcasted_iota(jnp.int32, (tiles, CHUNK), 0) == tile).astype(jnp.float32)
        lefts.append(left.astype(jnp.bfloat16).reshape(tiles // 16, 16, CHUNK))
        right = (lax.broadcasted_iota(jnp.int32, (128, CHUNK), 0) == lane).astype(jnp.float32)
        rights.append(right.astype(jnp.bfloat16))

    def scattered(values_of, target):
        acc = jnp.zeros((2 * tiles, 128), jnp.float32)
        for at in range(0, n_obs, CHUNK):
            left, right = lefts[at // CHUNK], rights[at // CHUNK]
            parts = [
                (left * piece[None]).reshape(tiles, CHUNK)
                for piece in split(jnp.broadcast_to(values_of(pl.ds(at, CHUNK)), (16, CHUNK)))
            ]
            acc = acc + lax.dot_general(
                jnp.concatenate(parts, axis=0), right, (((1,), (1,)), ((), ())),
                preferred_element_type=jnp.float32,
            )
        x = acc[:tiles] + acc[tiles:]
        for f in range(fields):
            target[f] = jnp.concatenate([x[(f * blocks + b) * rows :][:rows] for b in range(blocks)], axis=1)

    scattered(lambda part: weight[:, part] * innov[:, part], r_own)
    give(RES)
    give_beside()
    scattered(lambda part: weight[:, part], g_own)
    give(DIAG)
    give(IEV, k == 0)

    line = lax.broadcasted_iota(jnp.int32, (3 * rows, width), 0) + (s - 1) * rows
    column = lax.broadcasted_iota(jnp.int32, (3 * rows, width), 1)
    inside = jnp.logical_and(line >= 0, line < n_sp * rows)
    to_right = jnp.logical_and(inside, column < width - 1)
    to_left = jnp.logical_and(inside, column > 0)

    def ring(own_rows, rim):
        return jnp.concatenate([own_rows, rim], axis=0)

    def rim_of(x):
        return jnp.concatenate([x[2 * rows : 2 * rows + STEPS], x[rows - STEPS : rows]], axis=0)

    def tall_by(by, c):
        return coef[by, c]

    def ring_by(by, c):
        return ring(coef[by, c, mid], coef_rim[by, c])

    def model(us, factor):
        last = us[0].shape[0] - 1
        for _ in range(STEPS):
            us = [
                (1.0 - 4.0 * DIFFUSION) * u
                + factor(by, 0) * pltpu.roll(u, last, 0) + factor(by, 1) * pltpu.roll(u, 1, 0)
                + factor(by, 2) * pltpu.roll(u, width - 1, 1) + factor(by, 3) * pltpu.roll(u, 1, 1)
                for by, u in enumerate(us)
            ]
        return us

    def adjoint(vs, factor):
        last = vs[0].shape[0] - 1
        for _ in range(STEPS):
            vs = [
                (1.0 - 4.0 * DIFFUSION) * v
                + pltpu.roll(factor(by, 0) * v, 1, 0) + pltpu.roll(factor(by, 1) * v, last, 0)
                + pltpu.roll(factor(by, 2) * v, 1, 1) + pltpu.roll(factor(by, 3) * v, width - 1, 1)
                for by, v in enumerate(vs)
            ]
        return vs

    def precondition(source, target, part):
        v = [source[at] for at in range(n_tm)]
        for at in range(n_tm - 2, -1, -1):
            v[at] = v[at] + dec_f[at, part] * v[at + 1]
        for at in range(1, n_tm):
            v[at] = v[at] + dec_f[at - 1, part] * v[at - 1]
        for at in range(n_tm):
            target[at, part] = v[at]

    def forward(source, pause=None):
        jumps, outer = [source[0, mid]], []
        reached = model([source[at] for at in range(n_tm - 1)], tall_by)
        if pause is not None:
            pause()
        for at, ahead in enumerate(reached):
            jump = source[at + 1] - ahead
            jumps.append(jump[rows : 2 * rows])
            weighted = iev_f[at + 1] * jump
            outer.append(ring(weighted[rows : 2 * rows], rim_of(weighted)))
        return jumps, outer

    def closed(source, jumps, outer, target):
        back = adjoint(outer, ring_by)
        for at in range(n_tm):
            image = iev_f[at, mid] * jumps[at] + g_f[at] * source[at, mid]
            if at < n_tm - 1:
                image = image - back[at][:rows]
            target[at] = image

    def send_sums(row):
        if direct:
            slot = sums.at[pl.ds(me, 1)]
            slot[...] = row
            for to in range(n_all):
                start(remote(
                    slot, slot, sent.at[S_ANY], come.at[R_ANY], (to // n_sp, to % n_sp)), me != to)
        else:
            slot = sum_tm.at[k, pl.ds(0, 1)]
            slot[...] = row
            for o in range(1, n_tm):
                start(remote(slot, slot, far_send.at[0, o], far_recv.at[0, k], (at_tm(o), s)))

    def wait_sums():
        if direct:
            pl.when(owner)(lambda: await_lines(come.at[R_ANY], n_own - 1))
            pl.when(~owner)(lambda: await_lines(come.at[R_ANY], n_own))
        else:
            for src in range(fields):
                slot = sum_tm.at[src, pl.ds(0, 1)]
                pl.when(k != src)(remote(
                    slot, slot, far_send.at[0, 0], far_recv.at[0, src], (src, s)).wait_recv)
            slot = sums.at[pl.ds(s * 8, 8)]
            slot[...] = jnp.concatenate(
                [sum_tm[at, 0:1] for at in range(fields)] + [jnp.zeros((8 - fields, 128), jnp.float32)], axis=0)
            for o in range(1, n_sp):
                start(remote(slot, slot, far_send.at[1, o], far_recv.at[1, o], (k, at_sp(o))))
            for o in range(1, n_sp):
                slot = sums.at[pl.ds(at_sp(-o) * 8, 8)]
                remote(slot, slot, far_send.at[1, o], far_recv.at[1, o], (k, at_sp(-o))).wait_recv()
        return sums[...]

    reach_of = {DEC: range(n_tm - 1), WIND: range(n_tm - 1), IEV: range(1, n_tm)}

    @pl.when(owner)
    def work():
        for edge, cond in ((0, jnp.logical_not(has_low)), (2 * rows, jnp.logical_not(has_high))):
            @pl.when(cond)
            def _():
                for buffer in (r_f, y_f, iev_f, dec_f):
                    buffer[:, pl.ds(edge, rows)] = jnp.zeros((n_tm, rows, width), jnp.float32)
                y_rim[:, pl.ds(STEPS if edge == 0 else 0, STEPS)] = jnp.zeros((n_tm - 1, STEPS, width), jnp.float32)
                wind_f[:, :, pl.ds(edge, rows)] = jnp.zeros((n_tm, 2, rows, width), jnp.float32)
        for edge in (0, 3 * rows - (rows - STEPS)):
            iev_f[:, pl.ds(edge, rows - STEPS)] = jnp.zeros((n_tm, rows - STEPS, width), jnp.float32)
        r_f[k, mid] = r_own[k]
        g_f[k] = g_own[k]
        await_tiles(load_sem.at[1], 4)
        greeted(0)
        for at in (1, 0) + tuple(range(2, n_tm)):
            for kind in (DEC, WIND, IEV):
                if at in reach_of[kind]:
                    take(kind, at)
                    to_sides(kind, held(kind, at), functools.partial(tiles_of[kind], at), k != at)
        for at in range(n_tm):
            take(RES, at)
            to_mate(at)
        from_sides(WIND, 2 * (n_tm - 1))
        for at in range(n_tm - 1):
            x_flow, y_flow = wind_f[at, 0], wind_f[at, 1]
            coef[at, 0] = jnp.where(inside, DIFFUSION - 0.5 * x_flow, 0.0)
            coef[at, 1] = jnp.where(inside, DIFFUSION + 0.5 * x_flow, 0.0)
            coef[at, 2] = jnp.where(to_right, DIFFUSION - 0.5 * y_flow, 0.0)
            coef[at, 3] = jnp.where(to_left, DIFFUSION + 0.5 * y_flow, 0.0)
            for c in range(4):
                coef_rim[at, c] = rim_of(coef[at, c])
        from_sides(DEC, n_tm - 1)
        await_tiles(come.at[R_MATE], n_tm)
        await_tiles(come.at[R_BY], n_tm, off_chip)
        greet(1)
        precondition(r_f, z_f, slice(None))

        def weights():
            from_sides(IEV, n_tm - 1)
            take(IEV, 0)
            await_tiles(come.at[R_DIAG], n_tm - 1)

        jumps, outer = forward(z_f, weights)
        closed(z_f, jumps, outer, q_f)
        precondition(q_f, y_f, mid)
        whole_k = pl.ds(0, n_tm - 1)
        start(remote(
            y_f.at[whole_k, pl.ds(2 * rows - STEPS, STEPS)], y_rim.at[:, pl.ds(STEPS, STEPS)],
            sent.at[S_UP], come.at[R_RIM], (k, at_sp(1))), has_high)
        start(remote(
            y_f.at[whole_k, pl.ds(rows, STEPS)], y_rim.at[:, pl.ds(0, STEPS)],
            sent.at[S_DOWN], come.at[R_RIM + 1], (k, at_sp(-1))), has_low)
        rz_part = dq_part = 0.0
        for at in range(n_tm):
            z = z_f[at, mid]
            jump_f[at] = jumps[at]
            rz_part = rz_part + folded(r_f[at, mid] * z)
            dq_part = dq_part + folded(iev_f[at, mid] * jumps[at] * jumps[at] + g_f[at] * z * z)
        rz_part, dq_part = (jnp.sum(part, axis=(0, 1), keepdims=True) for part in (rz_part, dq_part))
        guess = jnp.where(dq_part > 0.0, rz_part / jnp.where(dq_part > 0.0, dq_part, 1.0), 0.0)
        give_back(Z, lambda at: z_f.at[at, mid])
        give_back(Q, lambda at: q_f.at[at])
        give_back(Y, lambda at: y_f.at[at, mid])
        greeted(1)
        greet(2)
        to_sides(NEXT, lambda first, rim: y_f.at[:, pl.ds(rows + first, rim)], lambda part: y_f.at[:, part])
        terms = [0.0] * len(POWER)
        for at in range(n_tm):
            z, y, q = z_f[at, mid], y_f[at, mid], q_f[at]
            r2, z2 = r_f[at, mid] - guess * q, z - guess * y
            seen2, seen_y = g_f[at] * z2, g_f[at] * y
            for i, term in enumerate((
                r2 * z2, -(r2 * y + z2 * q), q * y,
                seen2 * z2, -2.0 * (seen2 * y), seen_y * y, 2.0 * (seen2 * z), -2.0 * (seen_y * z),
            )):
                terms[i] = terms[i] + folded(term)
        terms[:3] = [jnp.sum(term, axis=(0, 1), keepdims=True) for term in terms[:3]]
        rim_lines = (n_tm - 1) * STEPS * width // 128
        for side, cond in enumerate((has_low, has_high)):
            pl.when(cond)(functools.partial(await_lines, come.at[R_RIM + side], rim_lines))
        ahead = model([ring(y_f[at, mid], y_rim[at]) for at in range(n_tm - 1)], ring_by)
        for at in range(n_tm):
            jump_z = jump_f[at]
            jump_y = y_f[at, mid] - ahead[at - 1][:rows] if at else y_f[at, mid]
            jump2 = jump_z - guess * jump_y
            scaled2, scaled_y = iev_f[at, mid] * jump2, iev_f[at, mid] * jump_y
            for i, term in enumerate((
                scaled2 * jump2, -2.0 * (scaled2 * jump_y), scaled_y * jump_y,
                2.0 * (scaled2 * jump_z), -2.0 * (scaled_y * jump_z),
            )):
                terms[3 + i] = terms[3 + i] + folded(term)
        for at in range(2, len(reach)):
            greeted(at)
            greet(at + 1)
        send_sums(packed(rz_part, dq_part, guess, *terms))
        from_sides(NEXT, n_tm)
        jumps, outer = forward(y_f)
        closed(y_f, jumps, outer, w_f)
        give_back(W, lambda at: w_f.at[at])
        side_lines = ((n_tm - 1) * (3 * rows + 2 * STEPS) + n_tm * rows) * width // 128
        await_tiles(sent.at[S_MATE], n_tm)
        pl.when(has_high)(functools.partial(await_lines, sent.at[S_UP], side_lines))
        pl.when(has_low)(functools.partial(await_lines, sent.at[S_DOWN], side_lines))
        await_tiles(sent.at[S_RET], 4 * (n_tm - 1))
        if direct:
            await_lines(sent.at[S_ANY], n_all - 1)
        else:
            slot = sum_tm.at[k, pl.ds(0, 1)]
            for o in range(1, n_tm):
                remote(slot, slot, far_send.at[0, o], far_recv.at[0, k], (at_tm(o), s)).wait_send()

    def back(semaphore, kinds):
        await_tiles(semaphore, kinds * (fields - 1), owner)
        await_tiles(semaphore, kinds * fields, ~owner)

    back(come.at[R_RET], 3)
    table = wait_sums()
    rz, dq = (jnp.sum(table[:, at : at + 1], axis=0, keepdims=True) for at in range(2))
    alpha = rz / dq
    shift = alpha - table[:, 2:3]
    lane = lax.broadcasted_iota(jnp.int32, table.shape, 1)
    scale = jnp.ones(table.shape, jnp.float32)
    for at, power in enumerate(POWER):
        if power:
            scale = jnp.where(lane == at + 3, shift if power == 1 else shift * shift, scale)
    table = jnp.sum(table * scale, axis=0, keepdims=True)
    lane = lax.broadcasted_iota(jnp.int32, (1, 128), 1)

    def group(least, most):
        inside = jnp.logical_and(lane >= 3 + least, lane < 3 + most)
        return jnp.sum(jnp.where(inside, table, 0.0), axis=1, keepdims=True)

    rz2, dd, cross = group(0, 3), group(3, 6), group(6, 8)
    beta = rz2 / rz
    alpha2 = rz2 / (dd + beta * cross + beta * beta * dq)
    first = alpha + alpha2 * (1.0 + beta)
    second = alpha2 * alpha
    back(come.at[R_LAST], 1)
    for f in range(fields):
        out[0, 0, f] = first * ret[Z, f] - second * ret[Y, f]
        out[1, 0, f] = r_own[f] - first * ret[Q, f] + second * ret[W, f]
    for has, kinds in ((has_next, 6), (~has_next, 3)):
        await_tiles(sent.at[S_TM], kinds * (fields - 1), has, owner)
        await_tiles(sent.at[S_TM], kinds * fields, has, ~owner)
    await_tiles(sent.at[S_BY], fields, off_chip)
    if not direct:
        slot = sums.at[pl.ds(s * 8, 8)]
        for o in range(1, n_sp):
            remote(slot, slot, far_send.at[1, o], far_recv.at[1, o], (k, at_sp(o))).wait_send()


def on_device(wind, decay, iev, obs, weight, innov):
    n_tm, n_sp = lax.axis_size("tm"), lax.axis_size("space")
    fields, rows, width = decay.shape[1:]
    n_own = fields * n_sp
    direct = n_tm * n_sp <= DIRECT
    f32 = jnp.float32
    tile = (rows, width)
    tall = (3 * rows, width)
    vmem = pl.BlockSpec(memory_space=pltpu.VMEM)
    both = pl.pallas_call(
        functools.partial(kernel, n_tm, n_sp),
        out_shape=pltpu.VMEM((2,) + decay.shape, f32),
        in_specs=[pl.BlockSpec(memory_space=pltpu.HBM)] * 6,
        out_specs=vmem,
        scratch_shapes=[
            pltpu.VMEM(obs.shape, jnp.int32),
            pltpu.VMEM(weight.shape, f32),
            pltpu.VMEM(innov.shape, f32),
            pltpu.SemaphoreType.DMA((2,)),
            pltpu.VMEM((fields,) + tile, f32),
            pltpu.VMEM((fields,) + tile, f32),
            pltpu.VMEM((n_tm,) + tall, f32),
            pltpu.VMEM((n_tm,) + tall, f32),
            pltpu.VMEM((n_tm,) + tile, f32),
            pltpu.VMEM((n_tm,) + tall, f32),
            pltpu.VMEM((n_tm, 2) + tall, f32),
            pltpu.VMEM((n_tm - 1, 4) + tall, f32),
            pltpu.VMEM((n_tm,) + tall, f32),
            pltpu.VMEM((n_tm,) + tall, f32),
            pltpu.VMEM((n_tm - 1,) + tile, f32),
            pltpu.VMEM((n_tm - 1, 4) + tile, f32),
            pltpu.VMEM((n_tm,) + tile, f32),
            pltpu.VMEM((n_tm,) + tile, f32),
            pltpu.VMEM((n_tm,) + tile, f32),
            pltpu.VMEM((4, fields) + tile, f32),
            pltpu.VMEM((n_own if direct else 8 * n_sp, 128), f32),
            pltpu.VMEM((n_tm, 8, 128), f32),
            pltpu.VMEM((rows * width // 128 * max(6 * fields, 5 * n_tm), 128), f32),
            pltpu.SemaphoreType.DMA((7,)),
            pltpu.SemaphoreType.DMA((4, n_tm)),
            pltpu.SemaphoreType.DMA((8 + 2 * 4,)),
            pltpu.SemaphoreType.DMA((1, 1) if direct else (2, max(n_tm, n_sp))),
            pltpu.SemaphoreType.DMA((1, 1) if direct else (2, max(n_tm, n_sp))),
            pltpu.SemaphoreType.REGULAR((3 if n_sp <= 8 else n_sp, 2)),
        ],
        compiler_params=pltpu.CompilerParams(
            collective_id=0, has_side_effects=True, vmem_limit_bytes=62 * 1024 * 1024
        ),
    )(wind, decay, iev, obs, weight, innov)
    return both[0], both[1]


def solution(mesh):
    placed = (
        P(None, "tm", "space", None),
        P("tm", None, "space", None),
        P("tm", None, "space", None),
        P("tm", "space"),
        P("tm", "space"),
        P("tm", "space"),
    )
    return jax.shard_map(
        on_device,
        mesh=mesh,
        in_specs=placed,
        out_specs=(P("tm", None, "space", None), P("tm", None, "space", None)),
        check_vma=False,
    )
```
